512 devices in a mesh: axial: 32 (over z, core), circ: 16 (over y, x).
Axes of the slice: x: 4, y: 4, z: 16, core: 2. Of those that a mesh axis runs over, the one named last changes fastest.
Arguments:
- load_terms: float32 [32, 16, 128, 512], P('axial', 'circ'), may hold values from -19 to 19
- diffusivity: float32 [32, 16, 512], P('axial', 'circ'), may hold values from 0.1 to 10
- interface_diag: float32 [32, 16, 512], P('axial', 'circ'), may hold values from 4 to 8
- coupling: float32 [32, 16, 512, 512], P('axial', 'circ'), may hold values from -0.125 to 0.125
- interior_inverse: float32 [32, 16, 4, 128, 128], P('axial', 'circ'), may hold values from -1 to 3, as said below
- neumann_solve: float32 [32, 16, 512, 512], P('axial', 'circ'), may hold values from -1 to 3, as said below
- row_coarse: float32 [32, 8, 8], P('axial'), may hold values from -1 to 3, as said below
- lower_coef: float32 [32, 8], P('axial'), may hold values from 0.1 to 1
- upper_coef: float32 [32, 8], P('axial'), may hold values from 0.1 to 1
- face_order: int32 [32, 16, 512], P('axial', 'circ'), may hold values from 0 to 511, as said below
- primal_lists: int32 [32, 16, 8, 64], P('axial', 'circ'), may hold values from 0 to 511, as said below
Outputs:
- solution_field: float32 [32, 16, 128, 512], P('axial', 'circ')
- residual: float32 [32, 16, 128, 512], P('axial', 'circ')
The draws below stay inside these ranges and needn't reach their ends.
Inputs may be any that keep to these rules, and one draw needn't show every extreme that they name: `face_order`: in each subdomain the values on face f (points f * 128 to f * 128 + 127) are those same numbers in some order; equal values on the two sides of a face name the same point. `primal_lists`: lists 2f and 2f + 1 together name every point of face f once. `interior_inverse`: symmetric in the last two dimensions. `neumann_solve`: symmetric in the last two dimensions. `row_coarse`: Symmetric, each diagonal entry larger than the sum of its row's other magnitudes.
All inputs are finite; a program needn't handle non-finite values.
Results may differ from the reference program's by a relative error of at most 0.0003.
Values sent between devices are 32-bit elements; how exact they have to be, the bound alone decides.
No kernel may reach another device: no remote copies, remote signals or barrier semaphores. Data moves between devices by JAX's collectives and lax.ppermute only.
A program may use at most 64 MiB of HBM per device.

```python
import math
import jax
import jax.numpy as jnp
from jax import lax

R = 128
F = 128
NB = 4
BLK = 128
NP = 8
ITERS = 3
SUBDOMAIN_AXIAL = 32
SUB_CI = 16
B = 512
NI = 512
LIST = 64


def symmetric_table(key, count, size, low, high, spread):
    diag_key, off_key = jax.random.split(key)
    diagonal = jax.random.uniform(diag_key, (count, size), jnp.float32, low, high)
    raw = jax.random.uniform(off_key, (count, size, size), jnp.float32, -spread, spread)
    mirrored = 0.5 * (raw + jnp.swapaxes(raw, 1, 2))
    identity = jnp.eye(size, dtype=jnp.float32)[None]
    return mirrored * (1.0 - identity) + identity * diagonal[:, :, None]


def draw_load_terms(key, part):
    base = jnp.clip(jax.random.normal(key, (SUBDOMAIN_AXIAL, SUB_CI, R, B), jnp.float32), -6.0, 6.0)
    rise = 1.0 + 2.0 * jnp.arange(SUBDOMAIN_AXIAL, dtype=jnp.float32) / (SUBDOMAIN_AXIAL - 1)
    return base * rise[:, None, None, None]


def draw_interior_inverse(key, part):
    table = symmetric_table(key, SUBDOMAIN_AXIAL * SUB_CI * NB, BLK, 1.0, 2.0, 0.6 / BLK ** 0.5)
    return table.reshape(SUBDOMAIN_AXIAL, SUB_CI, NB, BLK, BLK)


def draw_neumann_solve(key, part):
    table = symmetric_table(key, SUBDOMAIN_AXIAL * SUB_CI, B, 1.0, 2.0, 0.6 / B ** 0.5)
    return table.reshape(SUBDOMAIN_AXIAL, SUB_CI, B, B)


def draw_row_coarse(key, part):
    return symmetric_table(key, SUBDOMAIN_AXIAL, NP, 1.6, 2.8, 0.2)


def decay_table(key, slow_share):
    selection_key, baseline_key, noise_key, spike_key = jax.random.split(key, 4)
    slow = jax.random.uniform(selection_key, (NP,), jnp.float32) < slow_share
    slow_rate = jax.random.uniform(baseline_key, (NP,), jnp.float32, 0.01, 0.05)
    fast_rate = jax.random.uniform(jax.random.fold_in(baseline_key, 1), (NP,), jnp.float32, 0.35, 1.2)
    baseline_rate = jnp.where(slow, slow_rate, fast_rate)
    random_noise = jax.random.uniform(noise_key, (SUBDOMAIN_AXIAL, NP), jnp.float32, 0.7, 1.4)
    sudden_spike = jax.random.uniform(spike_key, (SUBDOMAIN_AXIAL, 1), jnp.float32) < 0.1
    return jnp.exp(-baseline_rate[None, :] * random_noise) * jnp.where(sudden_spike, 0.6, 1.0)


def draw_lower_coef(key, part):
    return decay_table(jax.random.fold_in(key, 5), 0.5)


def draw_upper_coef(key, part):
    return decay_table(jax.random.fold_in(key, 9), 0.5)


def face_permutations(key):
    keys = jax.random.split(key, SUBDOMAIN_AXIAL * SUB_CI * 4)
    perms = jax.vmap(lambda single: jax.random.permutation(single, F))(keys).astype(jnp.int32)
    offsets = jnp.arange(SUBDOMAIN_AXIAL * SUB_CI * 4, dtype=jnp.int32) % 4 * F
    return perms + offsets[:, None]


def draw_face_order(key, part):
    return face_permutations(jax.random.fold_in(key, 11)).reshape(SUBDOMAIN_AXIAL, SUB_CI, B).astype(jnp.int32)


def draw_primal_lists(key, part):
    perms = face_permutations(jax.random.fold_in(key, 13))
    return perms.reshape(SUBDOMAIN_AXIAL, SUB_CI, NP, LIST).astype(jnp.int32)


def shard_levels(rng, dims, pieces, least, high):
    def one(axis_at, shards_of):
        steps = jax.random.uniform(jax.random.fold_in(jax.random.fold_in(rng, 6), axis_at), (shards_of,), jnp.float32, least / len(pieces), high / len(pieces))
        return jnp.repeat(jnp.exp(steps), dims[axis_at] // shards_of).reshape((-1,) + (1,) * (len(dims) - axis_at - 1))

    loudness = one(*pieces[0])
    for cut in pieces[1:]:
        loudness = loudness * one(*cut)
    return loudness


def noise(own_key, dims, scale, most, shards=(), held_as=jnp.bfloat16):
    drawn = jax.random.normal(own_key, dims, jnp.float32) * scale
    if len(shards) > 0:
        drawn = shard_levels(own_key, dims, shards, -0.22, 0.18) * drawn
    return jnp.clip(drawn, min=-most, max=most).astype(held_as)


def setup_inputs(seed: int = 0) -> dict:
    seeds = jax.random.split(jax.random.key(seed), 12)
    return {
        "load_terms": draw_load_terms(jax.random.fold_in(seeds[11], 71), 0),
        "diffusivity": jnp.clip(jnp.exp(math.log(10.0) - 4.6051702 * jax.random.uniform(seeds[1], (SUBDOMAIN_AXIAL, SUB_CI, B), jnp.float32) ** shard_levels(seeds[1], (SUBDOMAIN_AXIAL, SUB_CI, B), ((0, 32), (1, 16)), -0.2, 0.2)), 0.1, 10.0),
        "interface_diag": jnp.clip(4.0 + 4.0 * jax.random.uniform(seeds[2], (SUBDOMAIN_AXIAL, SUB_CI, B), jnp.float32) ** shard_levels(seeds[2], (SUBDOMAIN_AXIAL, SUB_CI, B), ((0, 32), (1, 16)), -0.2, 0.2), 4.0, 8.0),
        "coupling": noise(seeds[3], (SUBDOMAIN_AXIAL, SUB_CI, B, NI), (4 * NI) ** -0.5, 0.125, ((0, 32), (1, 16)), jnp.float32),
        "interior_inverse": draw_interior_inverse(jax.random.fold_in(seeds[11], 71), 0),
        "neumann_solve": draw_neumann_solve(jax.random.fold_in(seeds[11], 71), 0),
        "row_coarse": draw_row_coarse(jax.random.fold_in(seeds[11], 71), 0),
        "lower_coef": draw_lower_coef(jax.random.fold_in(seeds[11], 71), 0),
        "upper_coef": draw_upper_coef(jax.random.fold_in(seeds[11], 71), 0),
        "face_order": draw_face_order(jax.random.fold_in(seeds[11], 71), 0),
        "primal_lists": draw_primal_lists(jax.random.fold_in(seeds[11], 71), 0),
    }


def invert_order(order):
    size = order.shape[0]
    return jnp.zeros((size,), jnp.int32).at[order].set(jnp.arange(size, dtype=jnp.int32))


def relabel(values, index):
    if values.ndim == 4:
        index = jnp.broadcast_to(index[:, :, None, :], values.shape)
    return jnp.take_along_axis(values, index, axis=-1)


def reference(load_terms, diffusivity, interface_diag, coupling, interior_inverse, neumann_solve, row_coarse, lower_coef, upper_coef, face_order, primal_lists):
    highest = lax.Precision.HIGHEST
    width = F
    flat_order = face_order.reshape(-1, B)
    inverse = jax.vmap(invert_order)(flat_order).reshape(face_order.shape)

    def assemble(values):
        shared = relabel(values, inverse)
        south = shared[..., :width]
        north = shared[..., width:2 * width]
        west = shared[..., 2 * width:3 * width]
        east = shared[..., 3 * width:]
        below = jnp.concatenate([jnp.zeros_like(north[:1]), north[:-1]], axis=0)
        above = jnp.concatenate([south[1:], jnp.zeros_like(south[:1])], axis=0)
        left_side = jnp.roll(east, 1, axis=1)
        right_side = jnp.roll(west, -1, axis=1)
        summed = jnp.concatenate([south + below, north + above, west + left_side, east + right_side], axis=-1)
        return relabel(summed, face_order)

    ends = jnp.ones((SUBDOMAIN_AXIAL, B), jnp.float32)
    ends = ends.at[0, :width].set(0.0).at[SUBDOMAIN_AXIAL - 1, width:2 * width].set(0.0)
    keep = ends[:, None, None, :]
    share = (diffusivity / assemble(diffusivity))[:, :, None, :]
    positions = jnp.arange(B, dtype=jnp.int32)
    averaging = jnp.sum((primal_lists[..., None] == positions).astype(jnp.float32), axis=3) / LIST

    def schur(direction):
        inner = jnp.einsum("acrb,acbi->acri", direction, coupling, precision=highest)
        blocked = inner.reshape(SUBDOMAIN_AXIAL, SUB_CI, R, NB, BLK)
        solved = jnp.einsum("acrnk,acnkl->acrnl", blocked, interior_inverse, precision=highest)
        solved = solved.reshape(SUBDOMAIN_AXIAL, SUB_CI, R, NI)
        back = jnp.einsum("acri,acbi->acrb", solved, coupling, precision=highest)
        return assemble(interface_diag[:, :, None, :] * direction - back) * keep

    def forward_step(carry, inputs):
        factor, value = inputs
        carry = factor * carry + (1.0 - factor) * value
        return carry, carry

    def precondition(residual):
        weighted = share * residual
        local_part = jnp.einsum("acrb,acbd->acrd", weighted, neumann_solve, precision=highest)
        primal = jnp.einsum("acrb,acpb->acrp", weighted, averaging, precision=highest)
        row_total = jnp.sum(primal, axis=1)
        row_part = jnp.einsum("arp,apq->arq", row_total, row_coarse, precision=highest)
        start = jnp.zeros((R, NP), jnp.float32)
        _, smoothed = lax.scan(forward_step, start, (lower_coef[:, None, :], row_total))
        _, top_part = lax.scan(forward_step, start, (upper_coef[:, None, :], smoothed), reverse=True)
        coarse = row_part + top_part
        coarse_part = jnp.einsum("arp,acpb->acrb", coarse, averaging, precision=highest)
        return assemble(share * (local_part + coarse_part)) * keep

    def inner_product(first, second):
        return 0.5 * jnp.sum(first * second, axis=(0, 1, 3))

    residual = assemble(load_terms) * keep
    solution_field = jnp.zeros_like(residual)
    precond = precondition(residual)
    direction = precond
    rz_value = inner_product(residual, precond)
    for iteration in range(ITERS):
        image = schur(direction)
        alpha = rz_value / inner_product(direction, image)
        solution_field = solution_field + alpha[None, None, :, None] * direction
        residual = residual - alpha[None, None, :, None] * image
        if iteration + 1 < ITERS:
            precond = precondition(residual)
            new_value = inner_product(residual, precond)
            direction = precond + (new_value / rz_value)[None, None, :, None] * direction
            rz_value = new_value
    return solution_field, residual
```

```python
import functools

import jax
import jax.numpy as jnp
from jax import lax
from jax.experimental import pallas as pl
from jax.experimental.pallas import tpu as pltpu
from jax.sharding import PartitionSpec as P

SHIFT = 12.0
HIGHEST = lax.Precision.HIGHEST
F32 = jnp.float32
LANES = 128


def mm(a, b):
    return lax.dot_general(
        a, b, (((1,), (0,)), ((), ())), precision=HIGHEST, preferred_element_type=F32
    )


def mm_t(a, b):
    return lax.dot_general(
        a, b, (((1,), (1,)), ((), ())), precision=HIGHEST, preferred_element_type=F32
    )


def faces_of(full):
    return [full[:, f * LANES : (f + 1) * LANES] for f in range(4)]


def one_hot_faces(order):
    rows = lax.broadcasted_iota(jnp.int32, (LANES, LANES), 0)
    return [
        jnp.where(order[:, f * LANES : (f + 1) * LANES] - f * LANES == rows, 1.0, 0.0).astype(F32)
        for f in range(4)
    ]


def to_shared(full, hots):
    return jnp.concatenate([mm_t(part, hot) for part, hot in zip(faces_of(full), hots)], axis=1)


def to_points(full, hots):
    return jnp.concatenate([mm(part, hot) for part, hot in zip(faces_of(full), hots)], axis=1)


class Place:
    def __init__(self, place):
        row, rows, column = place[0], place[1], place[2]
        self.row = row
        self.even_row = lax.rem(row, 2) == 0
        self.even_column = lax.rem(column, 2) == 0
        self.keep_south = jnp.where(row > 0, 1.0, 0.0).astype(F32)
        self.keep_north = jnp.where(row < rows - 1, 1.0, 0.0).astype(F32)


def put_sends(sends, full, at):
    south, north, west, east = faces_of(full)
    sends[0][...] = jnp.where(at.even_row, north, south)
    sends[1][...] = jnp.where(at.even_row, south, north)
    sends[2][...] = jnp.where(at.even_column, east, west)
    sends[3][...] = jnp.where(at.even_column, west, east)


def neighbours(got, at):
    core, link, near, far = [ref[...] for ref in got]
    above = jnp.where(at.even_row, core, link)
    below = jnp.where(at.even_row, link, core)
    right = jnp.where(at.even_column, near, far)
    left = jnp.where(at.even_column, far, near)
    return below, above, left, right


def assembled(full, got, at, rhs, keep=True):
    count = full.shape[0]
    extra = count - rhs
    own = faces_of(full)
    other = neighbours(got, at)
    scale = (at.keep_south, at.keep_north, None, None)
    shift = (0, 16, 8, 8)
    out = []
    for f in range(4):
        part = own[f][:rhs] + other[f][:rhs]
        if extra:
            zero = jnp.zeros((8, LANES), F32)
            mine = jnp.concatenate([zero, own[f][rhs:], zero], axis=0)
            pieces = [jnp.zeros((shift[f], LANES), F32)] if shift[f] else []
            pieces.append(other[f][rhs:])
            if shift[f] < 16:
                pieces.append(jnp.zeros((16 - shift[f], LANES), F32))
            part = jnp.concatenate([part, mine + jnp.concatenate(pieces, axis=0)], axis=0)
        if keep and scale[f] is not None:
            part = part * scale[f]
        out.append(part)
    return jnp.concatenate(out, axis=1)


def schur(z, diag, couple, blocks):
    inner = mm(z, couple)
    solved = jnp.concatenate([mm(part, blocks[n]) for n, part in enumerate(faces_of(inner))], axis=1)
    return diag * z - mm_t(solved, couple)


def k_prepare(place, load, rho, order, shared_o, *sends):
    at = Place(place)
    hots = one_hot_faces(order[...])
    pad = jnp.zeros((7, rho.shape[1]), F32)
    full = to_shared(jnp.concatenate([load[...], rho[...], pad], axis=0), hots)
    shared_o[...] = full
    put_sends(sends, full, at)


def k_matrices(order, diag, couple, neumann, lists, diag_o, couple_o, neumann_o, avg_o):
    hots = one_hot_faces(order[...])
    diag_o[...] = to_shared(jnp.broadcast_to(diag[...], (8, diag.shape[1])), hots)[:1]
    for f in range(4):
        rows = slice(f * LANES, (f + 1) * LANES)
        couple_o[rows, :] = mm(hots[f], couple[rows, :])
        neumann_o[rows, :] = to_shared(mm(hots[f], neumann[rows, :]), hots)
    points = order.shape[1]
    named = lists[...]
    position = lax.broadcasted_iota(jnp.int32, (8, points), 1)
    total = jnp.zeros((8, points), F32)
    length = named.shape[1]
    for item in range(length):
        total = total + jnp.where(named[:, item : item + 1] == position, 1.0, 0.0)
    avg_o[...] = to_shared(total * (1.0 / length), hots)


def k_first(place, shared, g0, g1, g2, g3, neumann, avg, r_o, share_o, prim_o, t_o, *sends):
    at = Place(place)
    rhs = r_o.shape[0]
    full = assembled(shared[...], (g0, g1, g2, g3), at, shared.shape[0], keep=False)
    share = shared[rhs : rhs + 1, :] / full[rhs : rhs + 1]
    south, north, west, east = faces_of(full[:rhs])
    r = jnp.concatenate([south * at.keep_south, north * at.keep_north, west, east], axis=1)
    r_o[...] = r
    share_o[...] = share
    weighted = share * r
    prim_o[...] = mm_t(avg[...], weighted)
    t = jnp.concatenate([share * mm(weighted, neumann[...]), share * avg[...]], axis=0)
    t_o[...] = t
    put_sends(sends, t, at)


def k_schur(place, t, g0, g1, g2, g3, diag, couple, blocks, z_o, q_o, *sends, rhs):
    at = Place(place)
    z = assembled(t[...], (g0, g1, g2, g3), at, rhs)
    z_o[...] = z
    q = schur(z, diag[...], couple[...], blocks)
    q_o[...] = q
    put_sends(sends, q, at)


def k_second(place, q, g0, g1, g2, g3, r, share, neumann, avg, v_o, t_o, pr_o, *sends):
    at = Place(place)
    rhs = r.shape[0]
    w = assembled(q[...], (g0, g1, g2, g3), at, rhs)
    v = jnp.concatenate([w[:rhs] - SHIFT * r[...], w[rhs:]], axis=0)
    v_o[...] = v
    weighted = share[...] * v
    pr_o[...] = jnp.concatenate(
        [mm_t(avg[...], weighted[:rhs]), mm_t(avg[...], weighted[rhs:])], axis=1
    )
    t = share[...] * mm(weighted, neumann[...])
    t_o[...] = t
    put_sends(sends, t, at)


def k_third(place, q, g0, g1, g2, g3, v, share, avg, prim0, prim1, v2_o, pay_o):
    at = Place(place)
    rhs = prim0.shape[1]
    w = assembled(q[...], (g0, g1, g2, g3), at, rhs)
    zero = jnp.zeros((16, w.shape[1]), F32)
    older = jnp.concatenate([v[...][:rhs], zero, v[...][rhs:], zero], axis=0)
    v2 = w - SHIFT * older
    v2_o[...] = v2
    weighted = share[...] * v2
    prim2 = mm_t(avg[...], weighted[:rhs])
    reach2 = mm_t(avg[...], weighted[rhs:])
    reach1 = prim1[...][:, rhs:]
    spare = jnp.zeros((8, LANES - reach1.shape[1] - reach2.shape[1]), F32)
    tail = jnp.concatenate([reach1, reach2, spare], axis=1)
    pay_o[...] = jnp.concatenate([prim0[...], prim1[...][:, :rhs], prim2, tail], axis=0)


def k_sum_spread(got, coefs, out):
    total = got[0]
    for item in range(1, got.shape[0]):
        total = total + got[item]
    total = total + coefs[...]
    for item in range(out.shape[0]):
        out[item] = total


def coarse_rows(totals, lowers, uppers):
    carry = jnp.zeros_like(totals[0])
    smooth = []
    for low, value in zip(lowers, totals):
        carry = low * carry + (1.0 - low) * value
        smooth.append(carry)
    carry = jnp.zeros_like(totals[0])
    tops = []
    for up, value in zip(uppers[::-1], smooth[::-1]):
        carry = up * carry + (1.0 - up) * value
        tops.append(carry)
    return tops[::-1]


def k_coarse(
    place, got, v2, v1, share, neumann,
    v_o, t_o, c0_o, c1_o, c2_o, s0, s1, s2, s3,
    band0, band1, band2, c0_s, c1_s, c2_s,
):
    at = Place(place)
    rhs = v_o.shape[0]
    rows = got.shape[0]
    width = band0.shape[1]
    lane = lax.broadcasted_iota(jnp.int32, (8, width), 1)
    lowers, uppers = [], []
    for ref in (band0, band1, band2):
        if ref.shape[0] > rows * 8:
            ref[rows * 8 :, :] = jnp.zeros((ref.shape[0] - rows * 8, width), F32)
    for k in range(rows):
        tail = got[k, 24:32, :]
        lowers.append(jnp.broadcast_to(tail[:, 120:121], (8, rhs)))
        uppers.append(jnp.broadcast_to(tail[:, 121:122], (8, rhs)))
        wide = tail
        if width > LANES:
            wide = jnp.concatenate([tail, jnp.zeros((8, width - LANES), F32)], axis=1)
        for ref, first, last, to in (
            (band1, 0, 40, 8 * (k - 2)),
            (band2, 40, 112, 8 * (k - 4)),
            (band0, 112, 120, 8 * k),
        ):
            picked = jnp.where((lane >= first) & (lane < last), wide, 0.0)
            ref[8 * k : 8 * k + 8, :] = pltpu.roll(picked, (to - first) % width, 1)

    def stacked(tiles):
        if width > rows * 8:
            tiles = tiles + [jnp.zeros((width - rows * 8, rhs), F32)]
        return jnp.concatenate(tiles, axis=0)

    def solve(total):
        tiles = [total[8 * k : 8 * k + 8] for k in range(rows)]
        return stacked(coarse_rows(tiles, lowers, uppers)) + mm(band0[...], total)

    edge = jnp.zeros((32, rhs), F32)
    c0 = solve(stacked([got[k, 0:8, :] for k in range(rows)]))
    c1 = solve(stacked([got[k, 8:16, :] for k in range(rows)]) + mm(band1[...], c0))
    c2 = solve(
        stacked([got[k, 16:24, :] for k in range(rows)]) + mm(band2[...], c0) + mm(band1[...], c1)
    )
    for ref, value in ((c0_s, c0), (c1_s, c1), (c2_s, c2)):
        ref[0:32, :] = edge
        ref[32 : 32 + width, :] = value
        ref[32 + width :, :] = edge
    start = at.row * 8
    c0w = c0_s[pl.ds(pl.multiple_of(start, 8), 72), :]
    c1w = c1_s[pl.ds(pl.multiple_of(start + 16, 8), 40), :]
    c2w = c2_s[pl.ds(pl.multiple_of(start + 24, 8), 24), :]
    c0_o[...] = c0w
    c1_o[...] = c1w
    c2_o[...] = c2w
    v = v2[:rhs, :] + mm_first(jnp.concatenate([c0w, c1w], axis=0),
                               jnp.concatenate([v2[rhs:, :], v1[rhs:, :]], axis=0))
    v_o[...] = v
    t = share[...] * mm(share[...] * v, neumann[...])
    t_o[...] = t
    put_sends((s0, s1, s2, s3), t, at)


def mm_first(a, b):
    return lax.dot_general(
        a, b, (((0,), (0,)), ((), ())), precision=HIGHEST, preferred_element_type=F32
    )


def dot_rows(pairs):
    rows = lax.broadcasted_iota(jnp.int32, (16, LANES), 0)
    total = jnp.zeros((16, LANES), F32)
    for index, (a, b) in pairs:
        part = sum(faces_of(a * b)[1:], faces_of(a * b)[0])
        total = total + mm_t(jnp.where(rows == index, 1.0, 0.0).astype(F32), part)
    return total


def k_known(r, z0, v1, z1, v2, vv2, c0, c1, z0_o, w0_o, z1_o, w1_o, dots_o):
    rhs = r.shape[0]
    c0, c1 = c0[...], c1[...]
    z0f = z0[:rhs, :] + mm_first(c0[24:48], z0[rhs:, :])
    v1f = v1[:rhs, :] + mm_first(c0[16:56], v1[rhs:, :])
    z1f = z1[:rhs, :] + mm_first(
        jnp.concatenate([c0[8:64], c1[8:32]], axis=0),
        jnp.concatenate([z1[rhs:, :], z0[rhs:, :]], axis=0),
    )
    v2f = vv2[...]
    z0_o[...] = z0f
    z1_o[...] = z1f
    w0_o[...] = v1f + SHIFT * r[...]
    w1_o[...] = v2f + SHIFT * v1f
    vs = (r[...], v1f, v2f)
    dots_o[...] = dot_rows([(3 * i + j, (vs[i], (z0f, z1f)[j])) for i in range(3) for j in range(2)])


def k_last_schur(place, t, g0, g1, g2, g3, pbasis, c2, diag, couple, blocks, z_o, q_o, *sends):
    at = Place(place)
    rhs = z_o.shape[0]
    z = assembled(t[...], (g0, g1, g2, g3), at, rhs) + mm_first(c2[...], pbasis[rhs:, :])
    z_o[...] = z
    q = schur(z, diag[...], couple[...], blocks)
    q_o[...] = q
    put_sends(sends, q, at)


def k_dots(place, q, g0, g1, g2, g3, r, w0, vv2, z0, z1, z2, dots, w2_o, pay_o):
    at = Place(place)
    w2 = assembled(q[...], (g0, g1, g2, g3), at, q.shape[0])
    w2_o[...] = w2
    v1 = w0[...] - SHIFT * r[...]
    vs = (r[...], v1, vv2[...])
    pairs = [(3 * i + 2, (vs[i], z2[...])) for i in range(3)]
    pairs += [(9 + i, (z, w2)) for i, z in enumerate((z0[...], z1[...], z2[...]))]
    pay_o[...] = dots[...] + dot_rows(pairs)


def k_final(got, order, r0, z0, z1, z2, w0, w1, w2, x_o, r_o):
    total = got[0]
    for item in range(1, got.shape[0]):
        total = total + got[item]
    vz = [[total[3 * i + j : 3 * i + j + 1] for j in range(3)] for i in range(3)]
    zw = [[None] * 3 for _ in range(3)]
    for i in range(3):
        for j in range(2):
            zw[i][j] = vz[j + 1][i] + SHIFT * vz[j][i]
        zw[i][2] = total[9 + i : 10 + i]

    def form(left, table, right):
        value = None
        for i, a in enumerate(left):
            for j, b in enumerate(right):
                if a is None or b is None:
                    continue
                term = a * table[i][j] * b
                value = term if value is None else value + term
        return value

    one = jnp.ones_like(vz[0][0])
    zero = jnp.zeros_like(one)
    toward = [one, None, None]
    steps = [zero, zero, zero]
    drops = [zero, zero, zero]
    rz = vz[0][0]
    for iteration in range(3):
        alpha = rz / form(toward, zw, toward)
        for j in range(3):
            if toward[j] is not None:
                steps[j] = steps[j] + alpha * toward[j]
                drops[j] = drops[j] - alpha * toward[j]
        if iteration < 2:
            mix = [one + SHIFT * drops[0], drops[0] + SHIFT * drops[1], None]
            if iteration == 1:
                mix[2] = drops[1]
            new = form(mix, vz, mix)
            beta = new / rz
            toward = [
                m if d is None else (beta * d if m is None else m + beta * d)
                for m, d in zip(mix, toward)
            ]
            rz = new
    table = jnp.concatenate(steps + drops + [zero, zero], axis=0)
    eye = jnp.where(
        lax.broadcasted_iota(jnp.int32, (LANES, LANES), 0)
        == lax.broadcasted_iota(jnp.int32, (LANES, LANES), 1),
        1.0,
        0.0,
    ).astype(F32)
    columns = mm_t(eye, table)
    col = [columns[:, i : i + 1] for i in range(6)]
    hots = one_hot_faces(order[...])
    x = col[0] * z0[...] + col[1] * z1[...] + col[2] * z2[...]
    r = r0[...] + col[3] * w0[...] + col[4] * w1[...] + col[5] * w2[...]
    x_o[...] = to_points(x, hots)
    r_o[...] = to_points(r, hots)


def call(body, outs, place, *args, scratch=(), flops=1_000_000):
    specs = [pl.BlockSpec(memory_space=pltpu.VMEM) for _ in args]
    if place is not None:
        specs = [pl.BlockSpec(memory_space=pltpu.SMEM)] + specs
        args = (place,) + args
    return pl.pallas_call(
        body,
        out_shape=[jax.ShapeDtypeStruct(shape, F32) for shape in outs],
        in_specs=specs,
        out_specs=[pl.BlockSpec(memory_space=pltpu.VMEM) for _ in outs],
        scratch_shapes=list(scratch),
        compiler_params=pltpu.CompilerParams(vmem_limit_bytes=32 * 1024 * 1024),
        cost_estimate=pl.CostEstimate(flops=flops, bytes_accessed=1_000_000, transcendentals=0),
    )(*args)


def exchange(sends, rows, columns):
    core = [(i, i ^ 1) for i in range(rows)]
    link = [(i, i + 1 if i % 2 else i - 1) for i in range(1, rows - 1)]
    near = [(i, i ^ 1) for i in range(columns)]
    far = [(i, (i + 1 if i % 2 else i - 1) % columns) for i in range(columns)]
    return [
        lax.ppermute(sends[0], "axial", core),
        lax.ppermute(sends[1], "axial", link),
        lax.ppermute(sends[2], "circ", near),
        lax.ppermute(sends[3], "circ", far),
    ]


def spread(value, axis):
    return lax.all_to_all(value, axis, split_axis=0, concat_axis=0, tiled=True)


def local(
    load_terms, diffusivity, interface_diag, coupling, interior_inverse, neumann_solve,
    row_coarse, lower_coef, upper_coef, face_order, primal_lists,
):
    rows, columns = lax.axis_size("axial"), lax.axis_size("circ")
    rhs, points = load_terms.shape[2], load_terms.shape[3]
    place = jnp.stack(
        [lax.axis_index("axial"), jnp.int32(rows), lax.axis_index("circ")]
    ).astype(jnp.int32)
    order = face_order[0]
    blocks = interior_inverse[0, 0]
    swap = functools.partial(exchange, rows=rows, columns=columns)

    def face(n):
        return [(n, LANES)] * 4

    shared, *sends = call(
        k_prepare, [(rhs + 8, points)] + face(rhs + 8), place, load_terms[0, 0], diffusivity[0], order
    )
    got = swap(sends)
    diag, couple, neumann, avg = call(
        k_matrices,
        [(1, points), (points, points), (points, points), (8, points)],
        None, order, interface_diag[0], coupling[0, 0], neumann_solve[0, 0], primal_lists[0, 0],
        flops=2_000_000_000,
    )
    r0, share, prim0, t0, *sends = call(
        k_first,
        [(rhs, points), (1, points), (8, rhs), (rhs + 8, points)] + face(rhs + 8),
        place, shared, *got, neumann, avg,
    )
    got = swap(sends)
    n = rhs + 24
    z0, q0, *sends = call(
        functools.partial(k_schur, rhs=rhs), [(n, points)] * 2 + face(n),
        place, t0, *got, diag, couple, blocks,
    )
    got = swap(sends)
    n = rhs + 40
    v1, t1, prim1, *sends = call(
        k_second, [(n, points)] * 2 + [(8, n)] + face(n), place, q0, *got, r0, share, neumann, avg
    )
    got = swap(sends)
    n = rhs + 56
    z1, q1, *sends = call(
        functools.partial(k_schur, rhs=rhs), [(n, points)] * 2 + face(n),
        place, t1, *got, diag, couple, blocks,
    )
    got = swap(sends)
    n = rhs + 72
    v2, pay = call(
        k_third, [(n, points), (32, LANES)], place, q1, *got, v1, share, avg, prim0, prim1
    )
    coefs = jnp.concatenate(
        [jnp.swapaxes(row_coarse[0], 0, 1), lower_coef[0][:, None], upper_coef[0][:, None]], axis=1
    )
    coefs = jnp.pad(coefs, ((24, 0), (112, LANES - 112 - coefs.shape[1])))
    got = spread(jnp.broadcast_to(pay[None], (columns, 32, LANES)), "circ")
    (pay,) = call(k_sum_spread, [(rows, 32, LANES)], None, got, coefs)
    got = spread(pay, "axial")
    width = max(LANES, 8 * rows)
    vv2, t2, c0, c1, c2, *sends = call(
        k_coarse,
        [(rhs, points)] * 2 + [(72, rhs), (40, rhs), (24, rhs)] + face(rhs),
        place, got, v2, v1, share, neumann,
        scratch=[pltpu.VMEM((width, width), F32)] * 3 + [pltpu.VMEM((width + 64, rhs), F32)] * 3,
    )
    got = swap(sends)
    z0f, w0f, z1f, w1f, dots = call(
        k_known, [(rhs, points)] * 4 + [(16, rhs)], None, r0, z0, v1, z1, v2, vv2, c0, c1
    )
    z2f, q2, *sends = call(
        k_last_schur, [(rhs, points)] * 2 + face(rhs),
        place, t2, *got, z0, c2, diag, couple, blocks,
    )
    got = swap(sends)
    w2f, pay = call(
        k_dots, [(rhs, points), (16, rhs)],
        place, q2, *got, r0, w0f, vv2, z0f, z1f, z2f, dots,
    )
    got = spread(jnp.broadcast_to(pay[None], (columns, 16, rhs)), "circ")
    (pay,) = call(k_sum_spread, [(rows, 16, rhs)], None, got, jnp.zeros((16, rhs), F32))
    got = spread(pay, "axial")
    x, r = call(
        k_final, [(rhs, points)] * 2, None, got, order, r0, z0f, z1f, z2f, w0f, w1f, w2f
    )
    return (x[None, None], r[None, None])


def solution(mesh):
    in_specs = (
        P("axial", "circ", None, None),
        P("axial", "circ", None),
        P("axial", "circ", None),
        P("axial", "circ", None, None),
        P("axial", "circ", None, None, None),
        P("axial", "circ", None, None),
        P("axial", None, None),
        P("axial", None),
        P("axial", None),
        P("axial", "circ", None),
        P("axial", "circ", None, None),
    )
    out_specs = (P("axial", "circ", None, None), P("axial", "circ", None, None))
    return jax.shard_map(local, mesh=mesh, in_specs=in_specs, out_specs=out_specs, check_vma=False)
```

```python
import functools

import jax
import jax.numpy as jnp
from jax import lax
from jax.experimental import pallas as pl
from jax.experimental.pallas import tpu as pltpu
from jax.sharding import PartitionSpec as P

SHIFT = 12.0
HIGHEST = lax.Precision.HIGHEST
F32 = jnp.float32
BF16 = jnp.bfloat16
LANES = 128
PIECES = 2


def mm(a, b):
    return lax.dot_general(
        a, b, (((1,), (0,)), ((), ())), precision=HIGHEST, preferred_element_type=F32
    )


def mm_t(a, b):
    return lax.dot_general(
        a, b, (((1,), (1,)), ((), ())), precision=HIGHEST, preferred_element_type=F32
    )


def cut(value, count):
    pieces = []
    for _ in range(count):
        piece = value.astype(BF16)
        pieces.append(piece)
        value = value - piece.astype(F32)
    return pieces


def narrow(a, b, transposed=False):
    return lax.dot_general(
        a, b, (((1,), (1 if transposed else 0,)), ((), ())), preferred_element_type=F32
    )


def product(a, pieces, transposed=False):
    count = a.shape[0]
    levels = len(pieces)
    if count % 16:
        a = jnp.concatenate([a, jnp.zeros((16 - count % 16, a.shape[1]), F32)], axis=0)
    tall = a.shape[0]
    left = cut(a, levels)
    by_level = [None] * levels
    for n, piece in enumerate(pieces):
        used = left[: levels - n]
        stack = used[0] if len(used) == 1 else jnp.concatenate(used, axis=0)
        out = narrow(stack, piece, transposed)
        for m in range(len(used)):
            part = out[m * tall : (m + 1) * tall]
            level = n + m
            by_level[level] = part if by_level[level] is None else by_level[level] + part
    total = by_level[-1]
    for part in by_level[-2::-1]:
        total = total + part
    return total[:count]


def select_columns(a, hot, transposed):
    count = a.shape[0]
    if count % 16:
        a = jnp.concatenate([a, jnp.zeros((16 - count % 16, a.shape[1]), F32)], axis=0)
    tall = a.shape[0]
    out = narrow(jnp.concatenate(cut(a, 3), axis=0), hot, transposed)
    return ((out[2 * tall :] + out[tall : 2 * tall]) + out[:tall])[:count]


def faces_of(full):
    return [full[:, f * LANES : (f + 1) * LANES] for f in range(4)]


def one_hot_faces(order):
    rows = lax.broadcasted_iota(jnp.int32, (LANES, LANES), 0)
    return [
        jnp.where(order[:, f * LANES : (f + 1) * LANES] - f * LANES == rows, 1.0, 0.0)
        .astype(F32)
        .astype(BF16)
        for f in range(4)
    ]


def to_shared(full, hots):
    return jnp.concatenate(
        [select_columns(part, hot, True) for part, hot in zip(faces_of(full), hots)], axis=1
    )


def to_points(full, hots):
    return jnp.concatenate(
        [select_columns(part, hot, False) for part, hot in zip(faces_of(full), hots)], axis=1
    )


class Place:
    def __init__(self, place):
        row, rows, column = place[0], place[1], place[2]
        self.row = row
        self.even_row = lax.rem(row, 2) == 0
        self.even_column = lax.rem(column, 2) == 0
        self.keep_south = jnp.where(row > 0, 1.0, 0.0).astype(F32)
        self.keep_north = jnp.where(row < rows - 1, 1.0, 0.0).astype(F32)


def put_sends(sends, full, at):
    south, north, west, east = faces_of(full)
    sends[0][...] = jnp.where(at.even_row, north, south)
    sends[1][...] = jnp.where(at.even_row, south, north)
    sends[2][...] = jnp.where(at.even_column, east, west)
    sends[3][...] = jnp.where(at.even_column, west, east)


def neighbours(got, at):
    core, link, near, far = [ref[...] for ref in got]
    above = jnp.where(at.even_row, core, link)
    below = jnp.where(at.even_row, link, core)
    right = jnp.where(at.even_column, near, far)
    left = jnp.where(at.even_column, far, near)
    return below, above, left, right


def assembled(full, got, at, rhs, keep=True):
    count = full.shape[0]
    extra = count - rhs
    own = faces_of(full)
    other = neighbours(got, at)
    scale = (at.keep_south, at.keep_north, None, None)
    shift = (0, 16, 8, 8)
    out = []
    for f in range(4):
        part = own[f][:rhs] + other[f][:rhs]
        if extra:
            zero = jnp.zeros((8, LANES), F32)
            mine = jnp.concatenate([zero, own[f][rhs:], zero], axis=0)
            pieces = [jnp.zeros((shift[f], LANES), F32)] if shift[f] else []
            pieces.append(other[f][rhs:])
            if shift[f] < 16:
                pieces.append(jnp.zeros((16 - shift[f], LANES), F32))
            part = jnp.concatenate([part, mine + jnp.concatenate(pieces, axis=0)], axis=0)
        if keep and scale[f] is not None:
            part = part * scale[f]
        out.append(part)
    return jnp.concatenate(out, axis=1)


def held(ref):
    return [ref[n] for n in range(ref.shape[0])]


def schur(z, diag, couple, blocks):
    inner = product(z, couple)
    solved = jnp.concatenate(
        [
            product(part, [piece[n] for piece in blocks])
            for n, part in enumerate(faces_of(inner))
        ],
        axis=1,
    )
    return diag * z - product(solved, couple, True)


def k_prepare(place, load, rho, order, shared_o, order_o, s0, s1, s2, s3, load_s, rho_s, sem):
    at = Place(place)
    copies = [
        pltpu.make_async_copy(source, target, sem.at[n])
        for n, (source, target) in enumerate(((order, order_o), (load, load_s), (rho, rho_s)))
    ]
    for copy in copies:
        copy.start()
    copies[0].wait()
    hots = one_hot_faces(order_o[...])
    copies[1].wait()
    copies[2].wait()
    pad = jnp.zeros((7, rho_s.shape[1]), F32)
    full = to_shared(jnp.concatenate([load_s[...], rho_s[...], pad], axis=0), hots)
    shared_o[...] = full
    put_sends((s0, s1, s2, s3), full, at)


def k_neumann(order, neumann, lists, neumann_o, avg_o, neumann_s, sem):
    copies = []
    for f in range(4):
        rows = pl.ds(f * LANES, LANES)
        copies.append(pltpu.make_async_copy(neumann.at[rows], neumann_s.at[rows], sem.at[f]))
        copies[f].start()
    hots = one_hot_faces(order[...])
    points = order.shape[1]
    named = lists[...]
    position = lax.broadcasted_iota(jnp.int32, (8, points), 1)
    total = jnp.zeros((8, points), F32)
    length = named.shape[1]
    for item in range(length):
        total = total + jnp.where(named[:, item : item + 1] == position, 1.0, 0.0)
    avg_o[...] = to_shared(total * (1.0 / length), hots)
    for f in range(4):
        rows = slice(f * LANES, (f + 1) * LANES)
        copies[f].wait()
        for n, piece in enumerate(cut(neumann_s[rows, :], PIECES)):
            half = narrow(hots[f], piece).astype(BF16)
            neumann_o[n, rows, :] = jnp.concatenate(
                [narrow(part, hot, True) for part, hot in zip(faces_of(half), hots)], axis=1
            ).astype(BF16)


def k_couple(order, diag, after, couple, blocks, diag_o, couple_o, blocks_o, couple_s, blocks_s, sem):
    copies = []
    for f in range(4):
        rows = pl.ds(f * LANES, LANES)
        copies.append(pltpu.make_async_copy(couple.at[rows], couple_s.at[rows], sem.at[f]))
    copies.append(pltpu.make_async_copy(blocks, blocks_s, sem.at[4]))
    for copy in copies:
        copy.start()
    hots = one_hot_faces(order[...])
    diag_o[...] = to_shared(jnp.broadcast_to(diag[...], (8, diag.shape[1])), hots)[:1]
    for f in range(4):
        rows = slice(f * LANES, (f + 1) * LANES)
        copies[f].wait()
        for n, piece in enumerate(cut(couple_s[rows, :], PIECES)):
            couple_o[n, rows, :] = narrow(hots[f], piece).astype(BF16)
    copies[4].wait()
    for f in range(4):
        for n, piece in enumerate(cut(blocks_s[f], PIECES)):
            blocks_o[n, f] = piece


def k_first(place, shared, g0, g1, g2, g3, neumann, avg, r_o, share_o, prim_o, t_o, *sends):
    at = Place(place)
    rhs = r_o.shape[0]
    full = assembled(shared[...], (g0, g1, g2, g3), at, shared.shape[0], keep=False)
    share = shared[rhs : rhs + 1, :] / full[rhs : rhs + 1]
    south, north, west, east = faces_of(full[:rhs])
    r = jnp.concatenate([south * at.keep_south, north * at.keep_north, west, east], axis=1)
    r_o[...] = r
    share_o[...] = share
    weighted = share * r
    prim_o[...] = mm_t(avg[...], weighted)
    t = jnp.concatenate([share * product(weighted, held(neumann)), share * avg[...]], axis=0)
    t_o[...] = t
    put_sends(sends, t, at)


def k_schur(place, t, g0, g1, g2, g3, diag, couple, blocks, z_o, q_o, *sends, rhs):
    at = Place(place)
    z = assembled(t[...], (g0, g1, g2, g3), at, rhs)
    z_o[...] = z
    q = schur(z, diag[...], held(couple), held(blocks))
    q_o[...] = q
    put_sends(sends, q, at)


def k_second(place, q, g0, g1, g2, g3, r, share, neumann, avg, v_o, t_o, pr_o, *sends):
    at = Place(place)
    rhs = r.shape[0]
    w = assembled(q[...], (g0, g1, g2, g3), at, rhs)
    v = jnp.concatenate([w[:rhs] - SHIFT * r[...], w[rhs:]], axis=0)
    v_o[...] = v
    weighted = share[...] * v
    pr_o[...] = jnp.concatenate(
        [mm_t(avg[...], weighted[:rhs]), mm_t(avg[...], weighted[rhs:])], axis=1
    )
    t = share[...] * product(weighted, held(neumann))
    t_o[...] = t
    put_sends(sends, t, at)


def k_third(place, q, g0, g1, g2, g3, v, share, avg, prim0, prim1, v2_o, pay_o):
    at = Place(place)
    rhs = prim0.shape[1]
    w = assembled(q[...], (g0, g1, g2, g3), at, rhs)
    zero = jnp.zeros((16, w.shape[1]), F32)
    older = jnp.concatenate([v[...][:rhs], zero, v[...][rhs:], zero], axis=0)
    v2 = w - SHIFT * older
    v2_o[...] = v2
    weighted = share[...] * v2
    prim2 = mm_t(avg[...], weighted[:rhs])
    reach2 = mm_t(avg[...], weighted[rhs:])
    reach1 = prim1[...][:, rhs:]
    spare = jnp.zeros((8, LANES - reach1.shape[1] - reach2.shape[1]), F32)
    tail = jnp.concatenate([reach1, reach2, spare], axis=1)
    pay_o[...] = jnp.concatenate([prim0[...], prim1[...][:, :rhs], prim2, tail], axis=0)


def summed(got):
    total = got[0]
    for item in range(1, got.shape[0]):
        total = total + got[item]
    return total


def k_sum_halves(got, coefs, out):
    total = summed(got) + coefs[...]
    half = total.shape[0] // 2
    for item in range(out.shape[0]):
        out[item] = total[half * (item % 2) : half * (item % 2) + half]


def k_sum_spread(got, out):
    total = summed(got)
    for item in range(out.shape[0]):
        out[item] = total


def coarse_rows(totals, lowers, uppers):
    carry = jnp.zeros_like(totals[0])
    smooth = []
    for low, value in zip(lowers, totals):
        carry = low * carry + (1.0 - low) * value
        smooth.append(carry)
    carry = jnp.zeros_like(totals[0])
    tops = []
    for up, value in zip(uppers[::-1], smooth[::-1]):
        carry = up * carry + (1.0 - up) * value
        tops.append(carry)
    return tops[::-1]


def k_coarse(
    place, mine, other, v2, v1, share, neumann,
    v_o, t_o, c0_o, c1_o, c2_o, s0, s1, s2, s3,
    band0, band1, band2, c0_s, c1_s, c2_s,
):
    at = Place(place)
    rhs = v_o.shape[0]
    rows = mine.shape[0]
    width = band0.shape[1]
    lane = lax.broadcasted_iota(jnp.int32, (8, width), 1)
    lowers, uppers = [], []
    for ref in (band0, band1, band2):
        if ref.shape[0] > rows * 8:
            ref[rows * 8 :, :] = jnp.zeros((ref.shape[0] - rows * 8, width), F32)
    upper = [jnp.where(at.even_row, mine[k], other[k]) for k in range(rows)]
    lower = [jnp.where(at.even_row, other[k], mine[k]) for k in range(rows)]
    for k in range(rows):
        tail = lower[k][8:16]
        lowers.append(jnp.broadcast_to(tail[:, 120:121], (8, rhs)))
        uppers.append(jnp.broadcast_to(tail[:, 121:122], (8, rhs)))
        wide = tail
        if width > LANES:
            wide = jnp.concatenate([tail, jnp.zeros((8, width - LANES), F32)], axis=1)
        for ref, first, last, to in (
            (band1, 0, 40, 8 * (k - 2)),
            (band2, 40, 112, 8 * (k - 4)),
            (band0, 112, 120, 8 * k),
        ):
            picked = jnp.where((lane >= first) & (lane < last), wide, 0.0)
            ref[8 * k : 8 * k + 8, :] = pltpu.roll(picked, (to - first) % width, 1)

    def stacked(tiles):
        if width > rows * 8:
            tiles = tiles + [jnp.zeros((width - rows * 8, rhs), F32)]
        return jnp.concatenate(tiles, axis=0)

    def solve(total):
        tiles = [total[8 * k : 8 * k + 8] for k in range(rows)]
        return stacked(coarse_rows(tiles, lowers, uppers)) + mm(band0[...], total)

    edge = jnp.zeros((32, rhs), F32)
    c0 = solve(stacked([part[0:8] for part in upper]))
    c1 = solve(stacked([part[8:16] for part in upper]) + mm(band1[...], c0))
    c2 = solve(
        stacked([part[0:8] for part in lower]) + mm(band2[...], c0) + mm(band1[...], c1)
    )
    for ref, value in ((c0_s, c0), (c1_s, c1), (c2_s, c2)):
        ref[0:32, :] = edge
        ref[32 : 32 + width, :] = value
        ref[32 + width :, :] = edge
    start = at.row * 8
    c0w = c0_s[pl.ds(pl.multiple_of(start, 8), 72), :]
    c1w = c1_s[pl.ds(pl.multiple_of(start + 16, 8), 40), :]
    c2w = c2_s[pl.ds(pl.multiple_of(start + 24, 8), 24), :]
    c0_o[...] = c0w
    c1_o[...] = c1w
    c2_o[...] = c2w
    v = v2[:rhs, :] + mm_first(jnp.concatenate([c0w, c1w], axis=0),
                               jnp.concatenate([v2[rhs:, :], v1[rhs:, :]], axis=0))
    v_o[...] = v
    t = share[...] * product(share[...] * v, held(neumann))
    t_o[...] = t
    put_sends((s0, s1, s2, s3), t, at)


def mm_first(a, b):
    return lax.dot_general(
        a, b, (((0,), (0,)), ((), ())), precision=HIGHEST, preferred_element_type=F32
    )


def dot_rows(pairs):
    rows = lax.broadcasted_iota(jnp.int32, (16, LANES), 0)
    total = jnp.zeros((16, LANES), F32)
    for index, (a, b) in pairs:
        part = sum(faces_of(a * b)[1:], faces_of(a * b)[0])
        total = total + mm_t(jnp.where(rows == index, 1.0, 0.0).astype(F32), part)
    return total


def k_known(r, z0, v1, z1, v2, vv2, c0, c1, z0_o, w0_o, z1_o, w1_o, dots_o):
    rhs = r.shape[0]
    c0, c1 = c0[...], c1[...]
    z0f = z0[:rhs, :] + mm_first(c0[24:48], z0[rhs:, :])
    v1f = v1[:rhs, :] + mm_first(c0[16:56], v1[rhs:, :])
    z1f = z1[:rhs, :] + mm_first(
        jnp.concatenate([c0[8:64], c1[8:32]], axis=0),
        jnp.concatenate([z1[rhs:, :], z0[rhs:, :]], axis=0),
    )
    v2f = vv2[...]
    z0_o[...] = z0f
    z1_o[...] = z1f
    w0_o[...] = v1f + SHIFT * r[...]
    w1_o[...] = v2f + SHIFT * v1f
    vs = (r[...], v1f, v2f)
    dots_o[...] = dot_rows(
        [(0, (vs[0], z0f)), (1, (vs[0], z1f)), (2, (vs[1], z0f)), (3, (vs[1], z1f)), (4, (v2f, z1f))]
    )


def k_last_schur(place, t, g0, g1, g2, g3, pbasis, c2, diag, couple, blocks, z_o, q_o, *sends):
    at = Place(place)
    rhs = z_o.shape[0]
    z = assembled(t[...], (g0, g1, g2, g3), at, rhs) + mm_first(c2[...], pbasis[rhs:, :])
    z_o[...] = z
    q = schur(z, diag[...], held(couple), held(blocks))
    q_o[...] = q
    put_sends(sends, q, at)


def k_dots(place, q, g0, g1, g2, g3, r, w0, vv2, z2, dots, w2_o, pay_o):
    at = Place(place)
    w2 = assembled(q[...], (g0, g1, g2, g3), at, q.shape[0])
    w2_o[...] = w2
    v1 = w0[...] - SHIFT * r[...]
    vs = (r[...], v1, vv2[...])
    pairs = [(5 + i, (vs[i], z2[...])) for i in range(3)] + [(8, (z2[...], w2))]
    table = dots[...] + dot_rows(pairs)
    pay_o[...] = jnp.concatenate([table[i : i + 1] for i in range(9)], axis=1)


def k_final(got, order, r0, z0, z1, z2, w0, w1, w2, x_o, r_o):
    total = summed(got)
    v0z0, v0z1, v1z0, v1z1, v2z1, v0z2, v1z2, v2z2, z2w2 = [
        total[:, i * LANES : (i + 1) * LANES] for i in range(9)
    ]
    z1w0 = v1z1 + SHIFT * v0z1
    z2w0 = v1z2 + SHIFT * v0z2
    z2w1 = v2z2 + SHIFT * v1z2
    zw = [
        [v1z0 + SHIFT * v0z0, z1w0, z2w0],
        [z1w0, v2z1 + SHIFT * v1z1, z2w1],
        [z2w0, z2w1, z2w2],
    ]
    vz = [[v0z0, v0z1, v0z2], [v1z0, v1z1, v1z2], [z1w0 - SHIFT * v1z0, v2z1, v2z2]]

    def form(left, table, right):
        value = None
        for i, a in enumerate(left):
            for j, b in enumerate(right):
                if a is None or b is None:
                    continue
                term = a * table[i][j] * b
                value = term if value is None else value + term
        return value

    one = jnp.ones_like(vz[0][0])
    zero = jnp.zeros_like(one)
    toward = [one, None, None]
    steps = [zero, zero, zero]
    drops = [zero, zero, zero]
    rz = vz[0][0]
    for iteration in range(3):
        alpha = rz / form(toward, zw, toward)
        for j in range(3):
            if toward[j] is not None:
                steps[j] = steps[j] + alpha * toward[j]
                drops[j] = drops[j] - alpha * toward[j]
        if iteration < 2:
            mix = [one + SHIFT * drops[0], drops[0] + SHIFT * drops[1], None]
            if iteration == 1:
                mix[2] = drops[1]
            new = form(mix, vz, mix)
            beta = new / rz
            toward = [
                m if d is None else (beta * d if m is None else m + beta * d)
                for m, d in zip(mix, toward)
            ]
            rz = new
    table = jnp.concatenate(steps + drops + [zero, zero], axis=0)
    eye = jnp.where(
        lax.broadcasted_iota(jnp.int32, (LANES, LANES), 0)
        == lax.broadcasted_iota(jnp.int32, (LANES, LANES), 1),
        1.0,
        0.0,
    ).astype(F32)
    columns = mm_t(eye, table)
    col = [columns[:, i : i + 1] for i in range(6)]
    hots = one_hot_faces(order[...])
    x = col[0] * z0[...] + col[1] * z1[...] + col[2] * z2[...]
    r = r0[...] + col[3] * w0[...] + col[4] * w1[...] + col[5] * w2[...]
    both = to_points(jnp.concatenate([x, r], axis=0), hots)
    rhs = x.shape[0]
    x_o[...] = both[:rhs]
    r_o[...] = both[rhs:]


def call(body, outs, place, *args, scratch=(), raw=(), flops=1_000_000):
    space = [pl.ANY if n in raw else pltpu.VMEM for n in range(len(args))]
    specs = [pl.BlockSpec(memory_space=kind) for kind in space]
    if place is not None:
        specs = [pl.BlockSpec(memory_space=pltpu.SMEM)] + specs
        args = (place,) + args
    return pl.pallas_call(
        body,
        out_shape=[
            out if isinstance(out, jax.ShapeDtypeStruct) else jax.ShapeDtypeStruct(out, F32)
            for out in outs
        ],
        in_specs=specs,
        out_specs=[pl.BlockSpec(memory_space=pltpu.VMEM) for _ in outs],
        scratch_shapes=list(scratch),
        compiler_params=pltpu.CompilerParams(vmem_limit_bytes=32 * 1024 * 1024),
        cost_estimate=pl.CostEstimate(flops=flops, bytes_accessed=1_000_000, transcendentals=0),
    )(*args)


def exchange(sends, rows, columns):
    core = [(i, i ^ 1) for i in range(rows)]
    link = [(i, i + 1 if i % 2 else i - 1) for i in range(1, rows - 1)]
    near = [(i, i ^ 1) for i in range(columns)]
    far = [(i, (i + 1 if i % 2 else i - 1) % columns) for i in range(columns)]
    got3 = lax.ppermute(sends[3], "circ", far)
    got2 = lax.ppermute(sends[2], "circ", near)
    got1 = lax.ppermute(sends[1], "axial", link)
    got0 = lax.ppermute(sends[0], "axial", core)
    return [got0, got1, got2, got3]


def spread(value, axis):
    return lax.all_to_all(value, axis, split_axis=0, concat_axis=0, tiled=True)


def local(
    load_terms, diffusivity, interface_diag, coupling, interior_inverse, neumann_solve,
    row_coarse, lower_coef, upper_coef, face_order, primal_lists,
):
    rows, columns = lax.axis_size("axial"), lax.axis_size("circ")
    rhs, points = load_terms.shape[2], load_terms.shape[3]
    place = jnp.stack(
        [lax.axis_index("axial"), jnp.int32(rows), lax.axis_index("circ")]
    ).astype(jnp.int32)
    swap = functools.partial(exchange, rows=rows, columns=columns)
    dma = pltpu.SemaphoreType.DMA

    def face(n):
        return [(n, LANES)] * 4

    def bf16(*shape):
        return jax.ShapeDtypeStruct((PIECES,) + shape, BF16)

    shared, order, *sends = call(
        k_prepare,
        [(rhs + 8, points), jax.ShapeDtypeStruct((1, points), jnp.int32)] + face(rhs + 8),
        place, load_terms[0, 0], diffusivity[0], face_order[0],
        raw=(0, 1, 2),
        scratch=[pltpu.VMEM((rhs, points), F32), pltpu.VMEM((1, points), F32), dma((3,))],
    )
    got = swap(sends)
    neumann, avg = call(
        k_neumann,
        [bf16(points, points), (8, points)],
        None, order, neumann_solve[0, 0], primal_lists[0, 0],
        raw=(1,),
        scratch=[pltpu.VMEM((points, points), F32), dma((4,))],
        flops=2_000_000_000,
    )
    r0, share, prim0, t0, *sends = call(
        k_first,
        [(rhs, points), (1, points), (8, rhs), (rhs + 8, points)] + face(rhs + 8),
        place, shared, *got, neumann, avg,
    )
    got = swap(sends)
    inner = interior_inverse.shape[2:]
    diag, couple, blocks = call(
        k_couple,
        [(1, points), bf16(points, points), bf16(*inner)],
        None, order, interface_diag[0], share, coupling[0, 0], interior_inverse[0, 0],
        raw=(3, 4),
        scratch=[pltpu.VMEM((points, points), F32), pltpu.VMEM(inner, F32), dma((5,))],
        flops=2_000_000_000,
    )
    n = rhs + 24
    z0, q0, *sends = call(
        functools.partial(k_schur, rhs=rhs), [(n, points)] * 2 + face(n),
        place, t0, *got, diag, couple, blocks,
    )
    got = swap(sends)
    n = rhs + 40
    v1, t1, prim1, *sends = call(
        k_second, [(n, points)] * 2 + [(8, n)] + face(n), place, q0, *got, r0, share, neumann, avg
    )
    got = swap(sends)
    n = rhs + 56
    z1, q1, *sends = call(
        functools.partial(k_schur, rhs=rhs), [(n, points)] * 2 + face(n),
        place, t1, *got, diag, couple, blocks,
    )
    got = swap(sends)
    n = rhs + 72
    v2, pay = call(
        k_third, [(n, points), (32, LANES)], place, q1, *got, v1, share, avg, prim0, prim1
    )
    coefs = jnp.concatenate(
        [jnp.swapaxes(row_coarse[0], 0, 1), lower_coef[0][:, None], upper_coef[0][:, None]], axis=1
    )
    coefs = jnp.pad(coefs, ((24, 0), (112, LANES - 112 - coefs.shape[1])))
    got = spread(jnp.broadcast_to(pay[None], (columns, 32, LANES)), "circ")
    (pay,) = call(k_sum_halves, [(rows, 16, LANES)], None, got, coefs)
    mine = spread(pay, "axial")
    other = lax.ppermute(mine, "axial", [(i, i ^ 1) for i in range(rows)])
    width = max(LANES, 8 * rows)
    vv2, t2, c0, c1, c2, *sends = call(
        k_coarse,
        [(rhs, points)] * 2 + [(72, rhs), (40, rhs), (24, rhs)] + face(rhs),
        place, mine, other, v2, v1, share, neumann,
        scratch=[pltpu.VMEM((width, width), F32)] * 3 + [pltpu.VMEM((width + 64, rhs), F32)] * 3,
    )
    got = swap(sends)
    z0f, w0f, z1f, w1f, dots = call(
        k_known, [(rhs, points)] * 4 + [(16, rhs)], None, r0, z0, v1, z1, v2, vv2, c0, c1
    )
    z2f, q2, *sends = call(
        k_last_schur, [(rhs, points)] * 2 + face(rhs),
        place, t2, *got, z0, c2, diag, couple, blocks,
    )
    got = swap(sends)
    w2f, pay = call(
        k_dots, [(rhs, points), (1, 9 * LANES)], place, q2, *got, r0, w0f, vv2, z2f, dots
    )
    got = spread(jnp.broadcast_to(pay[None], (columns,) + pay.shape), "circ")
    (pay,) = call(k_sum_spread, [(rows,) + pay.shape], None, got)
    got = spread(pay, "axial")
    x, r = call(
        k_final, [(rhs, points)] * 2, None, got, order, r0, z0f, z1f, z2f, w0f, w1f, w2f
    )
    return (x[None, None], r[None, None])


def solution(mesh):
    in_specs = (
        P("axial", "circ", None, None),
        P("axial", "circ", None),
        P("axial", "circ", None),
        P("axial", "circ", None, None),
        P("axial", "circ", None, None, None),
        P("axial", "circ", None, None),
        P("axial", None, None),
        P("axial", None),
        P("axial", None),
        P("axial", "circ", None),
        P("axial", "circ", None, None),
    )
    out_specs = (P("axial", "circ", None, None), P("axial", "circ", None, None))
    return jax.shard_map(local, mesh=mesh, in_specs=in_specs, out_specs=out_specs, check_vma=False)
```

```python
import functools

import jax
import jax.numpy as jnp
from jax import lax
from jax.experimental import pallas as pl
from jax.experimental.pallas import tpu as pltpu
from jax.sharding import PartitionSpec as P

SHIFT = 12.0
HIGHEST = lax.Precision.HIGHEST
F32 = jnp.float32
BF16 = jnp.bfloat16
LANES = 128
PIECES = 2


def mm(a, b):
    return lax.dot_general(
        a, b, (((1,), (0,)), ((), ())), precision=HIGHEST, preferred_element_type=F32
    )


def mm_t(a, b):
    return lax.dot_general(
        a, b, (((1,), (1,)), ((), ())), precision=HIGHEST, preferred_element_type=F32
    )


def cut(value, count):
    pieces = []
    for _ in range(count):
        piece = value.astype(BF16)
        pieces.append(piece)
        value = value - piece.astype(F32)
    return pieces


def narrow(a, b, transposed=False):
    return lax.dot_general(
        a, b, (((1,), (1 if transposed else 0,)), ((), ())), preferred_element_type=F32
    )


def product(a, pieces, transposed=False):
    count = a.shape[0]
    levels = len(pieces)
    if count % 16:
        a = jnp.concatenate([a, jnp.zeros((16 - count % 16, a.shape[1]), F32)], axis=0)
    tall = a.shape[0]
    left = cut(a, levels)
    by_level = [None] * levels
    for n, piece in enumerate(pieces):
        used = left[: levels - n]
        stack = used[0] if len(used) == 1 else jnp.concatenate(used, axis=0)
        out = narrow(stack, piece, transposed)
        for m in range(len(used)):
            part = out[m * tall : (m + 1) * tall]
            level = n + m
            by_level[level] = part if by_level[level] is None else by_level[level] + part
    total = by_level[-1]
    for part in by_level[-2::-1]:
        total = total + part
    return total[:count]


def select_columns(a, hot, transposed):
    count = a.shape[0]
    if count % 16:
        a = jnp.concatenate([a, jnp.zeros((16 - count % 16, a.shape[1]), F32)], axis=0)
    tall = a.shape[0]
    out = narrow(jnp.concatenate(cut(a, 3), axis=0), hot, transposed)
    return ((out[2 * tall :] + out[tall : 2 * tall]) + out[:tall])[:count]


def faces_of(full):
    return [full[:, f * LANES : (f + 1) * LANES] for f in range(4)]


def one_hot_faces(order):
    rows = lax.broadcasted_iota(jnp.int32, (LANES, LANES), 0)
    return [
        jnp.where(order[:, f * LANES : (f + 1) * LANES] - f * LANES == rows, 1.0, 0.0)
        .astype(F32)
        .astype(BF16)
        for f in range(4)
    ]


def to_shared(full, hots):
    return jnp.concatenate(
        [select_columns(part, hot, True) for part, hot in zip(faces_of(full), hots)], axis=1
    )


def to_points(full, hots):
    return jnp.concatenate(
        [select_columns(part, hot, False) for part, hot in zip(faces_of(full), hots)], axis=1
    )


class Place:
    def __init__(self, place):
        row, rows, column = place[0], place[1], place[2]
        self.row = row
        self.even_row = lax.rem(row, 2) == 0
        self.even_column = lax.rem(column, 2) == 0
        self.keep_south = jnp.where(row > 0, 1.0, 0.0).astype(F32)
        self.keep_north = jnp.where(row < rows - 1, 1.0, 0.0).astype(F32)


def put_sends(sends, full, at):
    south, north, west, east = faces_of(full)
    sends[0][...] = jnp.where(at.even_column, west, east)
    sends[1][...] = jnp.where(at.even_column, east, west)
    sends[2][...] = jnp.where(at.even_row, south, north)
    sends[3][...] = jnp.where(at.even_row, north, south)


def neighbours(got, at):
    far, near, link, core = [ref[...] for ref in got]
    above = jnp.where(at.even_row, core, link)
    below = jnp.where(at.even_row, link, core)
    right = jnp.where(at.even_column, near, far)
    left = jnp.where(at.even_column, far, near)
    return below, above, left, right


def assembled(full, got, at, rhs, keep=True):
    count = full.shape[0]
    extra = count - rhs
    own = faces_of(full)
    other = neighbours(got, at)
    scale = (at.keep_south, at.keep_north, None, None)
    shift = (0, 16, 8, 8)
    out = []
    for f in range(4):
        part = own[f][:rhs] + other[f][:rhs]
        if extra:
            zero = jnp.zeros((8, LANES), F32)
            mine = jnp.concatenate([zero, own[f][rhs:], zero], axis=0)
            pieces = [jnp.zeros((shift[f], LANES), F32)] if shift[f] else []
            pieces.append(other[f][rhs:])
            if shift[f] < 16:
                pieces.append(jnp.zeros((16 - shift[f], LANES), F32))
            part = jnp.concatenate([part, mine + jnp.concatenate(pieces, axis=0)], axis=0)
        if keep and scale[f] is not None:
            part = part * scale[f]
        out.append(part)
    return jnp.concatenate(out, axis=1)


def held(ref):
    return [ref[n] for n in range(ref.shape[0])]


def schur(z, diag, couple, blocks):
    inner = product(z, couple)
    solved = jnp.concatenate(
        [
            product(part, [piece[n] for piece in blocks])
            for n, part in enumerate(faces_of(inner))
        ],
        axis=1,
    )
    return diag * z - product(solved, couple, True)


def k_prepare(place, load, rho, order, shared_o, order_o, s0, s1, s2, s3, load_s, rho_s, sem):
    at = Place(place)
    copies = [
        pltpu.make_async_copy(source, target, sem.at[n])
        for n, (source, target) in enumerate(((order, order_o), (load, load_s), (rho, rho_s)))
    ]
    for copy in copies:
        copy.start()
    copies[0].wait()
    hots = one_hot_faces(order_o[...])
    copies[1].wait()
    copies[2].wait()
    pad = jnp.zeros((7, rho_s.shape[1]), F32)
    full = to_shared(jnp.concatenate([load_s[...], rho_s[...], pad], axis=0), hots)
    shared_o[...] = full
    put_sends((s0, s1, s2, s3), full, at)


def k_neumann(order, neumann, lists, neumann_o, avg_o, neumann_s, lists_s, sem):
    listed = pltpu.make_async_copy(lists, lists_s, sem.at[4])
    listed.start()
    copies = []
    for f in range(4):
        rows = pl.ds(f * LANES, LANES)
        copies.append(pltpu.make_async_copy(neumann.at[rows], neumann_s.at[rows], sem.at[f]))
        copies[f].start()
    hots = one_hot_faces(order[...])
    points = order.shape[1]
    listed.wait()
    named = lists_s[...]
    position = lax.broadcasted_iota(jnp.int32, (8, points), 1)
    total = jnp.zeros((8, points), F32)
    length = named.shape[1]
    for item in range(length):
        total = total + jnp.where(named[:, item : item + 1] == position, 1.0, 0.0)
    avg_o[...] = to_shared(total * (1.0 / length), hots)
    for f in range(4):
        rows = slice(f * LANES, (f + 1) * LANES)
        copies[f].wait()
        for n, piece in enumerate(cut(neumann_s[rows, :], PIECES)):
            half = narrow(hots[f], piece).astype(BF16)
            neumann_o[n, rows, :] = jnp.concatenate(
                [narrow(part, hot, True) for part, hot in zip(faces_of(half), hots)], axis=1
            ).astype(BF16)


def k_couple(
    order, after, diag, couple, blocks, diag_o, couple_o, blocks_o, diag_s, couple_s, blocks_s, sem
):
    copies = []
    for f in range(4):
        rows = pl.ds(f * LANES, LANES)
        copies.append(pltpu.make_async_copy(couple.at[rows], couple_s.at[rows], sem.at[f]))
    copies.append(pltpu.make_async_copy(blocks, blocks_s, sem.at[4]))
    copies.append(pltpu.make_async_copy(diag, diag_s, sem.at[5]))
    for copy in copies:
        copy.start()
    hots = one_hot_faces(order[...])
    copies[5].wait()
    diag_o[...] = to_shared(jnp.broadcast_to(diag_s[...], (8, diag_s.shape[1])), hots)[:1]
    for f in range(4):
        rows = slice(f * LANES, (f + 1) * LANES)
        copies[f].wait()
        for n, piece in enumerate(cut(couple_s[rows, :], PIECES)):
            couple_o[n, rows, :] = narrow(hots[f], piece).astype(BF16)
    copies[4].wait()
    for f in range(4):
        for n, piece in enumerate(cut(blocks_s[f], PIECES)):
            blocks_o[n, f] = piece


def k_first(place, shared, g0, g1, g2, g3, neumann, avg, r_o, share_o, prim_o, t_o, *sends):
    at = Place(place)
    rhs = r_o.shape[0]
    full = assembled(shared[...], (g0, g1, g2, g3), at, shared.shape[0], keep=False)
    share = shared[rhs : rhs + 1, :] / full[rhs : rhs + 1]
    south, north, west, east = faces_of(full[:rhs])
    r = jnp.concatenate([south * at.keep_south, north * at.keep_north, west, east], axis=1)
    r_o[...] = r
    share_o[...] = share
    weighted = share * r
    prim_o[...] = mm_t(avg[...], weighted)
    t = jnp.concatenate([share * product(weighted, held(neumann)), share * avg[...]], axis=0)
    t_o[...] = t
    put_sends(sends, t, at)


def k_schur(
    place, t, g0, g1, g2, g3, diag, couple, blocks, z_o, q_o, s0, s1, s2, s3, z_s, sem, *, rhs
):
    at = Place(place)
    z = assembled(t[...], (g0, g1, g2, g3), at, rhs)
    z_s[...] = z
    copy = pltpu.make_async_copy(z_s, z_o, sem.at[0])
    copy.start()
    q = schur(z, diag[...], held(couple), held(blocks))
    q_o[...] = q
    put_sends((s0, s1, s2, s3), q, at)
    copy.wait()


def k_second(place, q, g0, g1, g2, g3, r, share, neumann, avg, v_o, t_o, pr_o, *sends):
    at = Place(place)
    rhs = r.shape[0]
    w = assembled(q[...], (g0, g1, g2, g3), at, rhs)
    v = jnp.concatenate([w[:rhs] - SHIFT * r[...], w[rhs:]], axis=0)
    v_o[...] = v
    weighted = share[...] * v
    pr_o[...] = jnp.concatenate(
        [mm_t(avg[...], weighted[:rhs]), mm_t(avg[...], weighted[rhs:])], axis=1
    )
    t = share[...] * product(weighted, held(neumann))
    t_o[...] = t
    put_sends(sends, t, at)


def k_third(place, q, g0, g1, g2, g3, v, share, avg, prim0, prim1, v2_o, pay_o):
    at = Place(place)
    rhs = prim0.shape[1]
    w = assembled(q[...], (g0, g1, g2, g3), at, rhs)
    zero = jnp.zeros((16, w.shape[1]), F32)
    older = jnp.concatenate([v[...][:rhs], zero, v[...][rhs:], zero], axis=0)
    v2 = w - SHIFT * older
    v2_o[...] = v2
    weighted = share[...] * v2
    prim2 = mm_t(avg[...], weighted[:rhs])
    reach2 = mm_t(avg[...], weighted[rhs:])
    reach1 = prim1[...][:, rhs:]
    spare = jnp.zeros((8, LANES - reach1.shape[1] - reach2.shape[1]), F32)
    tail = jnp.concatenate([reach1, reach2, spare], axis=1)
    pay = jnp.concatenate([prim0[...], prim1[...][:, :rhs], prim2, tail], axis=0)
    for item in range(pay_o.shape[0]):
        pay_o[item] = pay


def summed(got):
    total = got[0]
    for item in range(1, got.shape[0]):
        total = total + got[item]
    return total


def k_sum_halves(got, coefs, out):
    total = summed(got) + coefs[...]
    half = total.shape[0] // 2
    for item in range(out.shape[0]):
        out[item] = total[half * (item % 2) : half * (item % 2) + half]


def k_sum_spread(got, out):
    total = summed(got)
    for item in range(out.shape[0]):
        out[item] = total


def banded_product(pieces, value):
    first, second = cut(value, 2)
    return (narrow(pieces[1], first) + narrow(pieces[0], second)) + narrow(pieces[0], first)


def coarse_rows(totals, lowers, uppers):
    carry = jnp.zeros_like(totals[0])
    smooth = []
    for low, value in zip(lowers, [(1.0 - low) * value for low, value in zip(lowers, totals)]):
        carry = low * carry + value
        smooth.append(carry)
    carry = jnp.zeros_like(totals[0])
    tops = []
    smooth = [(1.0 - up) * value for up, value in zip(uppers, smooth)]
    for up, value in zip(uppers[::-1], smooth[::-1]):
        carry = up * carry + value
        tops.append(carry)
    return tops[::-1]


def k_coarse(
    place, mine, other, v2, v1, share, neumann,
    v_o, t_o, c0_o, c1_o, c2_o, s0, s1, s2, s3,
    band0, band1, band2, c0_s, c1_s, c2_s,
):
    at = Place(place)
    rhs = v_o.shape[0]
    rows = mine.shape[0]
    width = band0.shape[1]
    lane = lax.broadcasted_iota(jnp.int32, (8, width), 1)
    lowers, uppers = [], []
    for ref in (band0, band1, band2):
        if ref.shape[0] > rows * 8:
            ref[rows * 8 :, :] = jnp.zeros((ref.shape[0] - rows * 8, width), F32)
    upper = [jnp.where(at.even_row, mine[k], other[k]) for k in range(rows)]
    lower = [jnp.where(at.even_row, other[k], mine[k]) for k in range(rows)]
    for k in range(rows):
        tail = lower[k][8:16]
        lowers.append(jnp.broadcast_to(tail[:, 120:121], (8, rhs)))
        uppers.append(jnp.broadcast_to(tail[:, 121:122], (8, rhs)))
        wide = tail
        if width > LANES:
            wide = jnp.concatenate([tail, jnp.zeros((8, width - LANES), F32)], axis=1)
        for ref, first, last, to in (
            (band1, 0, 40, 8 * (k - 2)),
            (band2, 40, 112, 8 * (k - 4)),
            (band0, 112, 120, 8 * k),
        ):
            picked = jnp.where((lane >= first) & (lane < last), wide, 0.0)
            ref[8 * k : 8 * k + 8, :] = pltpu.roll(picked, (to - first) % width, 1)

    def stacked(tiles):
        if width > rows * 8:
            tiles = tiles + [jnp.zeros((width - rows * 8, rhs), F32)]
        return jnp.concatenate(tiles, axis=0)

    own, near, wide = [cut(ref[...], 2) for ref in (band0, band1, band2)]

    def solve(total):
        tiles = [total[8 * k : 8 * k + 8] for k in range(rows)]
        return stacked(coarse_rows(tiles, lowers, uppers)) + banded_product(own, total)

    edge = jnp.zeros((32, rhs), F32)
    c0 = solve(stacked([part[0:8] for part in upper]))
    c1 = solve(stacked([part[8:16] for part in upper]) + banded_product(near, c0))
    c2 = solve(
        stacked([part[0:8] for part in lower])
        + banded_product(wide, c0)
        + banded_product(near, c1)
    )
    for ref, value in ((c0_s, c0), (c1_s, c1), (c2_s, c2)):
        ref[0:32, :] = edge
        ref[32 : 32 + width, :] = value
        ref[32 + width :, :] = edge
    start = at.row * 8
    c0w = c0_s[pl.ds(pl.multiple_of(start, 8), 72), :]
    c1w = c1_s[pl.ds(pl.multiple_of(start + 16, 8), 40), :]
    c2w = c2_s[pl.ds(pl.multiple_of(start + 24, 8), 24), :]
    c0_o[...] = c0w
    c1_o[...] = c1w
    c2_o[...] = c2w
    v = v2[:rhs, :] + mm_first(jnp.concatenate([c0w, c1w], axis=0),
                               jnp.concatenate([v2[rhs:, :], v1[rhs:, :]], axis=0))
    v_o[...] = v
    t = share[...] * product(share[...] * v, held(neumann))
    t_o[...] = t
    put_sends((s0, s1, s2, s3), t, at)


def mm_first(a, b):
    return lax.dot_general(
        a, b, (((0,), (0,)), ((), ())), precision=HIGHEST, preferred_element_type=F32
    )


def dot_rows(pairs):
    rows = lax.broadcasted_iota(jnp.int32, (16, LANES), 0)
    total = jnp.zeros((16, LANES), F32)
    for index, (a, b) in pairs:
        part = sum(faces_of(a * b)[1:], faces_of(a * b)[0])
        total = total + mm_t(jnp.where(rows == index, 1.0, 0.0).astype(F32), part)
    return total


def k_known(r, z0, v1, z1, v2, vv2, c0, c1, z0_o, w0_o, z1_o, w1_o, dots_o):
    rhs = r.shape[0]
    c0, c1 = c0[...], c1[...]
    z0f = z0[:rhs, :] + mm_first(c0[24:48], z0[rhs:, :])
    v1f = v1[:rhs, :] + mm_first(c0[16:56], v1[rhs:, :])
    z1f = z1[:rhs, :] + mm_first(
        jnp.concatenate([c0[8:64], c1[8:32]], axis=0),
        jnp.concatenate([z1[rhs:, :], z0[rhs:, :]], axis=0),
    )
    v2f = vv2[...]
    z0_o[...] = z0f
    z1_o[...] = z1f
    w0_o[...] = v1f + SHIFT * r[...]
    w1_o[...] = v2f + SHIFT * v1f
    vs = (r[...], v1f, v2f)
    dots_o[...] = dot_rows(
        [(0, (vs[0], z0f)), (1, (vs[0], z1f)), (2, (vs[1], z0f)), (3, (vs[1], z1f)), (4, (v2f, z1f))]
    )


def k_last_schur(
    place, t, g0, g1, g2, g3, pbasis, c2, diag, couple, blocks, r, w0, vv2, dots,
    z_o, q_o, pay_o, s0, s1, s2, s3,
):
    at = Place(place)
    rhs = z_o.shape[0]
    z = assembled(t[...], (g0, g1, g2, g3), at, rhs) + mm_first(c2[...], pbasis[rhs:, :])
    z_o[...] = z
    q = schur(z, diag[...], held(couple), held(blocks))
    q_o[...] = q
    put_sends((s0, s1, s2, s3), q, at)
    v1 = w0[...] - SHIFT * r[...]
    pairs = [(5 + i, (v, z)) for i, v in enumerate((r[...], v1, vv2[...]))]
    table = dots[...] + dot_rows(pairs + [(8, (z, q + q))])
    line = jnp.concatenate([table[i : i + 1] for i in range(9)], axis=1)
    for item in range(pay_o.shape[0]):
        pay_o[item] = line


def k_final(place, got, q, g0, g1, g2, g3, order, r0, z0, z1, z2, w0, w1, x_o, r_o):
    w2 = assembled(q[...], (g0, g1, g2, g3), Place(place), q.shape[0])
    total = summed(got)
    v0z0, v0z1, v1z0, v1z1, v2z1, v0z2, v1z2, v2z2, z2w2 = [
        total[:, i * LANES : (i + 1) * LANES] for i in range(9)
    ]
    z1w0 = v1z1 + SHIFT * v0z1
    z2w0 = v1z2 + SHIFT * v0z2
    z2w1 = v2z2 + SHIFT * v1z2
    zw = [
        [v1z0 + SHIFT * v0z0, z1w0, z2w0],
        [z1w0, v2z1 + SHIFT * v1z1, z2w1],
        [z2w0, z2w1, z2w2],
    ]
    vz = [[v0z0, v0z1, v0z2], [v1z0, v1z1, v1z2], [z1w0 - SHIFT * v1z0, v2z1, v2z2]]

    def form(left, table, right):
        value = None
        for i, a in enumerate(left):
            for j, b in enumerate(right):
                if a is None or b is None:
                    continue
                term = a * table[i][j] * b
                value = term if value is None else value + term
        return value

    one = jnp.ones_like(vz[0][0])
    zero = jnp.zeros_like(one)
    toward = [one, None, None]
    steps = [zero, zero, zero]
    drops = [zero, zero, zero]
    rz = vz[0][0]
    for iteration in range(3):
        alpha = rz / form(toward, zw, toward)
        for j in range(3):
            if toward[j] is not None:
                steps[j] = steps[j] + alpha * toward[j]
                drops[j] = drops[j] - alpha * toward[j]
        if iteration < 2:
            mix = [one + SHIFT * drops[0], drops[0] + SHIFT * drops[1], None]
            if iteration == 1:
                mix[2] = drops[1]
            new = form(mix, vz, mix)
            beta = new / rz
            toward = [
                m if d is None else (beta * d if m is None else m + beta * d)
                for m, d in zip(mix, toward)
            ]
            rz = new
    table = jnp.concatenate(steps + drops + [zero, zero], axis=0)
    eye = jnp.where(
        lax.broadcasted_iota(jnp.int32, (LANES, LANES), 0)
        == lax.broadcasted_iota(jnp.int32, (LANES, LANES), 1),
        1.0,
        0.0,
    ).astype(F32)
    columns = mm_t(eye, table)
    col = [columns[:, i : i + 1] for i in range(6)]
    hots = one_hot_faces(order[...])
    x = col[0] * z0[...] + col[1] * z1[...] + col[2] * z2[...]
    r = r0[...] + col[3] * w0[...] + col[4] * w1[...] + col[5] * w2
    both = to_points(jnp.concatenate([x, r], axis=0), hots)
    rhs = x.shape[0]
    x_o[...] = both[:rhs]
    r_o[...] = both[rhs:]


def call(body, outs, place, *args, scratch=(), raw=(), raw_outs=(), flops=1_000_000):
    args = tuple(
        pltpu.with_memory_space_constraint(arg, pltpu.HBM) if n in raw else arg
        for n, arg in enumerate(args)
    )
    space = [pltpu.HBM if n in raw else pltpu.VMEM for n in range(len(args))]
    specs = [pl.BlockSpec(memory_space=kind) for kind in space]
    if place is not None:
        specs = [pl.BlockSpec(memory_space=pltpu.SMEM)] + specs
        args = (place,) + args
    return pl.pallas_call(
        body,
        out_shape=[
            out
            if isinstance(out, jax.ShapeDtypeStruct)
            else (pltpu.HBM(out, F32) if n in raw_outs else jax.ShapeDtypeStruct(out, F32))
            for n, out in enumerate(outs)
        ],
        in_specs=specs,
        out_specs=[
            pl.BlockSpec(memory_space=pltpu.HBM if n in raw_outs else pltpu.VMEM)
            for n in range(len(outs))
        ],
        scratch_shapes=list(scratch),
        compiler_params=pltpu.CompilerParams(vmem_limit_bytes=16 * 1024 * 1024),
        cost_estimate=pl.CostEstimate(flops=flops, bytes_accessed=1_000_000, transcendentals=0),
    )(*args)


def exchange(sends, rows, columns):
    core = [(i, i ^ 1) for i in range(rows)]
    link = [(i, i + 1 if i % 2 else i - 1) for i in range(1, rows - 1)]
    near = [(i, i ^ 1) for i in range(columns)]
    far = [(i, (i + 1 if i % 2 else i - 1) % columns) for i in range(columns)]
    return [
        lax.ppermute(sends[0], "circ", far),
        lax.ppermute(sends[1], "circ", near),
        lax.ppermute(sends[2], "axial", link),
        lax.ppermute(sends[3], "axial", core),
    ]


def spread(value, axis):
    return lax.all_to_all(value, axis, split_axis=0, concat_axis=0, tiled=True)


def local(
    load_terms, diffusivity, interface_diag, coupling, interior_inverse, neumann_solve,
    row_coarse, lower_coef, upper_coef, face_order, primal_lists,
):
    rows, columns = lax.axis_size("axial"), lax.axis_size("circ")
    rhs, points = load_terms.shape[2], load_terms.shape[3]
    place = jnp.stack(
        [lax.axis_index("axial"), jnp.int32(rows), lax.axis_index("circ")]
    ).astype(jnp.int32)
    swap = functools.partial(exchange, rows=rows, columns=columns)
    dma = pltpu.SemaphoreType.DMA

    def face(n):
        return [(n, LANES)] * 4

    def bf16(*shape):
        return jax.ShapeDtypeStruct((PIECES,) + shape, BF16)

    shared, order, *sends = call(
        k_prepare,
        [(rhs + 8, points), jax.ShapeDtypeStruct((1, points), jnp.int32)] + face(rhs + 8),
        place, load_terms[0, 0], diffusivity[0], face_order[0],
        raw=(0, 1, 2),
        scratch=[pltpu.VMEM((rhs, points), F32), pltpu.VMEM((1, points), F32), dma((3,))],
    )
    got = swap(sends)
    neumann, avg = call(
        k_neumann,
        [bf16(points, points), (8, points)],
        None, order, neumann_solve[0, 0], primal_lists[0, 0],
        raw=(1, 2),
        scratch=[
            pltpu.VMEM((points, points), F32),
            pltpu.VMEM(primal_lists.shape[2:], jnp.int32),
            dma((5,)),
        ],
        flops=2_000_000_000,
    )
    r0, share, prim0, t0, *sends = call(
        k_first,
        [(rhs, points), (1, points), (8, rhs), (rhs + 8, points)] + face(rhs + 8),
        place, shared, *got, neumann, avg,
    )
    got = swap(sends)
    inner = interior_inverse.shape[2:]
    diag, couple, blocks = call(
        k_couple,
        [(1, points), bf16(points, points), bf16(*inner)],
        None, order, share, interface_diag[0], coupling[0, 0], interior_inverse[0, 0],
        raw=(2, 3, 4),
        scratch=[
            pltpu.VMEM((1, points), F32),
            pltpu.VMEM((points, points), F32),
            pltpu.VMEM(inner, F32),
            dma((6,)),
        ],
        flops=2_000_000_000,
    )
    n = rhs + 24
    z0, q0, *sends = call(
        functools.partial(k_schur, rhs=rhs), [(n, points)] * 2 + face(n),
        place, t0, *got, diag, couple, blocks,
        raw_outs=(0,), scratch=[pltpu.VMEM((n, points), F32), dma((1,))],
    )
    got = swap(sends)
    n = rhs + 40
    v1, t1, prim1, *sends = call(
        k_second, [(n, points)] * 2 + [(8, n)] + face(n), place, q0, *got, r0, share, neumann, avg
    )
    got = swap(sends)
    n = rhs + 56
    z1, q1, *sends = call(
        functools.partial(k_schur, rhs=rhs), [(n, points)] * 2 + face(n),
        place, t1, *got, diag, couple, blocks,
        raw_outs=(0,), scratch=[pltpu.VMEM((n, points), F32), dma((1,))],
    )
    got = swap(sends)
    n = rhs + 72
    v2, pay = call(
        k_third, [(n, points), (columns, 32, LANES)], place, q1, *got, v1, share, avg, prim0, prim1
    )
    coefs = jnp.concatenate(
        [jnp.swapaxes(row_coarse[0], 0, 1), lower_coef[0][:, None], upper_coef[0][:, None]], axis=1
    )
    coefs = jnp.pad(coefs, ((24, 0), (112, LANES - 112 - coefs.shape[1])))
    got = spread(pay, "circ")
    (pay,) = call(k_sum_halves, [(rows, 16, LANES)], None, got, coefs)
    mine = spread(pay, "axial")
    other = lax.ppermute(mine, "axial", [(i, i ^ 1) for i in range(rows)])
    width = max(LANES, 8 * rows)
    vv2, t2, c0, c1, c2, *sends = call(
        k_coarse,
        [(rhs, points)] * 2 + [(72, rhs), (40, rhs), (24, rhs)] + face(rhs),
        place, mine, other, v2, v1, share, neumann,
        scratch=[pltpu.VMEM((width, width), F32)] * 3 + [pltpu.VMEM((width + 64, rhs), F32)] * 3,
    )
    got = swap(sends)
    z0f, w0f, z1f, w1f, dots = call(
        k_known, [(rhs, points)] * 4 + [(16, rhs)], None, r0, z0, v1, z1, v2, vv2, c0, c1
    )
    z2f, q2, pay, *sends = call(
        k_last_schur, [(rhs, points)] * 2 + [(columns, 1, 9 * LANES)] + face(rhs),
        place, t2, *got, z0, c2, diag, couple, blocks, r0, w0f, vv2, dots,
    )
    dots = spread(pay, "circ")
    got = swap(sends)
    (pay,) = call(k_sum_spread, [(rows, 1, 9 * LANES)], None, dots)
    dots = spread(pay, "axial")
    x, r = call(
        k_final, [(rhs, points)] * 2,
        place, dots, q2, *got, order, r0, z0f, z1f, z2f, w0f, w1f,
    )
    return (x[None, None], r[None, None])


def solution(mesh):
    in_specs = (
        P("axial", "circ", None, None),
        P("axial", "circ", None),
        P("axial", "circ", None),
        P("axial", "circ", None, None),
        P("axial", "circ", None, None, None),
        P("axial", "circ", None, None),
        P("axial", None, None),
        P("axial", None),
        P("axial", None),
        P("axial", "circ", None),
        P("axial", "circ", None, None),
    )
    out_specs = (P("axial", "circ", None, None), P("axial", "circ", None, None))
    return jax.shard_map(local, mesh=mesh, in_specs=in_specs, out_specs=out_specs, check_vma=False)
```

```python
import functools

import jax
import jax.numpy as jnp
from jax import lax
from jax.experimental import pallas as pl
from jax.experimental.pallas import tpu as pltpu
from jax.sharding import PartitionSpec as P

SHIFT = 12.0
HIGHEST = lax.Precision.HIGHEST
F32 = jnp.float32
BF16 = jnp.bfloat16
LANES = 128
PIECES = 2


def mm_t(a, b):
    return lax.dot_general(
        a, b, (((1,), (1,)), ((), ())), precision=HIGHEST, preferred_element_type=F32
    )


def cut(value, count):
    pieces = []
    for _ in range(count):
        piece = value.astype(BF16)
        pieces.append(piece)
        value = value - piece.astype(F32)
    return pieces


def narrow(a, b, transposed=False):
    return lax.dot_general(
        a, b, (((1,), (1 if transposed else 0,)), ((), ())), preferred_element_type=F32
    )


def product(a, pieces, transposed=False):
    count = a.shape[0]
    levels = len(pieces)
    if count % 16:
        a = jnp.concatenate([a, jnp.zeros((16 - count % 16, a.shape[1]), F32)], axis=0)
    tall = a.shape[0]
    left = cut(a, levels)
    by_level = [None] * levels
    for n, piece in enumerate(pieces):
        used = left[: levels - n]
        stack = used[0] if len(used) == 1 else jnp.concatenate(used, axis=0)
        out = narrow(stack, piece, transposed)
        for m in range(len(used)):
            part = out[m * tall : (m + 1) * tall]
            level = n + m
            by_level[level] = part if by_level[level] is None else by_level[level] + part
    total = by_level[-1]
    for part in by_level[-2::-1]:
        total = total + part
    return total[:count]


def select_columns(a, hot, transposed):
    count = a.shape[0]
    if count % 16:
        a = jnp.concatenate([a, jnp.zeros((16 - count % 16, a.shape[1]), F32)], axis=0)
    tall = a.shape[0]
    out = narrow(jnp.concatenate(cut(a, 3), axis=0), hot, transposed)
    return ((out[2 * tall :] + out[tall : 2 * tall]) + out[:tall])[:count]


def faces_of(full):
    return [full[:, f * LANES : (f + 1) * LANES] for f in range(4)]


def one_hot_faces(order):
    rows = lax.broadcasted_iota(jnp.int32, (LANES, LANES), 0)
    return [
        jnp.where(order[:, f * LANES : (f + 1) * LANES] - f * LANES == rows, 1.0, 0.0)
        .astype(F32)
        .astype(BF16)
        for f in range(4)
    ]


def to_shared(full, hots):
    return jnp.concatenate(
        [select_columns(part, hot, True) for part, hot in zip(faces_of(full), hots)], axis=1
    )


def to_points(full, hots):
    return jnp.concatenate(
        [select_columns(part, hot, False) for part, hot in zip(faces_of(full), hots)], axis=1
    )


class Place:
    def __init__(self, place):
        row, rows, column = place[0], place[1], place[2]
        self.row = row
        self.even_row = lax.rem(row, 2) == 0
        self.even_column = lax.rem(column, 2) == 0
        self.keep_south = jnp.where(row > 0, 1.0, 0.0).astype(F32)
        self.keep_north = jnp.where(row < rows - 1, 1.0, 0.0).astype(F32)


def put_sends(sends, full, at):
    south, north, west, east = faces_of(full)
    sends[0][...] = jnp.where(at.even_column, west, east)
    sends[1][...] = jnp.where(at.even_column, east, west)
    sends[2][...] = jnp.where(at.even_row, south, north)
    sends[3][...] = jnp.where(at.even_row, north, south)


def neighbours(got, at):
    far, near, link, core = [ref[...] for ref in got]
    above = jnp.where(at.even_row, core, link)
    below = jnp.where(at.even_row, link, core)
    right = jnp.where(at.even_column, near, far)
    left = jnp.where(at.even_column, far, near)
    return below, above, left, right


def assembled(full, got, at, rhs, keep=True):
    count = full.shape[0]
    extra = count - rhs
    own = faces_of(full)
    other = neighbours(got, at)
    scale = (at.keep_south, at.keep_north, None, None)
    shift = (0, 16, 8, 8)
    out = []
    for f in range(4):
        part = own[f][:rhs] + other[f][:rhs]
        if extra:
            zero = jnp.zeros((8, LANES), F32)
            mine = jnp.concatenate([zero, own[f][rhs:], zero], axis=0)
            pieces = [jnp.zeros((shift[f], LANES), F32)] if shift[f] else []
            pieces.append(other[f][rhs:])
            if shift[f] < 16:
                pieces.append(jnp.zeros((16 - shift[f], LANES), F32))
            part = jnp.concatenate([part, mine + jnp.concatenate(pieces, axis=0)], axis=0)
        if keep and scale[f] is not None:
            part = part * scale[f]
        out.append(part)
    return jnp.concatenate(out, axis=1)


def held(ref):
    return [ref[n] for n in range(ref.shape[0])]


def schur(z, diag, couple, blocks):
    inner = product(z, couple)
    solved = jnp.concatenate(
        [
            product(part, [piece[n] for piece in blocks])
            for n, part in enumerate(faces_of(inner))
        ],
        axis=1,
    )
    return diag * z - product(solved, couple, True)


def k_prepare(place, load, rho, order, shared_o, order_o, s0, s1, s2, s3, load_s, rho_s, sem):
    at = Place(place)
    copies = [
        pltpu.make_async_copy(source, target, sem.at[n])
        for n, (source, target) in enumerate(((order, order_o), (load, load_s), (rho, rho_s)))
    ]
    for copy in copies:
        copy.start()
    copies[0].wait()
    hots = one_hot_faces(order_o[...])
    copies[1].wait()
    copies[2].wait()
    pad = jnp.zeros((7, rho_s.shape[1]), F32)
    full = to_shared(jnp.concatenate([load_s[...], rho_s[...], pad], axis=0), hots)
    shared_o[...] = full
    put_sends((s0, s1, s2, s3), full, at)


def k_neumann(order, neumann, lists, neumann_o, avg_o, neumann_s, lists_s, sem):
    listed = pltpu.make_async_copy(lists, lists_s, sem.at[4])
    listed.start()
    copies = []
    for f in range(4):
        rows = pl.ds(f * LANES, LANES)
        copies.append(pltpu.make_async_copy(neumann.at[rows], neumann_s.at[rows], sem.at[f]))
        copies[f].start()
    hots = one_hot_faces(order[...])
    points = order.shape[1]
    listed.wait()
    named = lists_s[...]
    position = lax.broadcasted_iota(jnp.int32, (8, points), 1)
    total = jnp.zeros((8, points), F32)
    length = named.shape[1]
    for item in range(length):
        total = total + jnp.where(named[:, item : item + 1] == position, 1.0, 0.0)
    avg_o[...] = to_shared(total * (1.0 / length), hots)
    for f in range(4):
        rows = slice(f * LANES, (f + 1) * LANES)
        copies[f].wait()
        for n, piece in enumerate(cut(neumann_s[rows, :], PIECES)):
            half = narrow(hots[f], piece).astype(BF16)
            neumann_o[n, rows, :] = jnp.concatenate(
                [narrow(part, hot, True) for part, hot in zip(faces_of(half), hots)], axis=1
            ).astype(BF16)


def k_couple(
    order, after, diag, couple, blocks, row_coarse, lower, upper,
    diag_o, couple_o, blocks_o, coefs_o,
    diag_s, couple_s, blocks_s, rows_s, lower_s, upper_s, sem,
):
    copies = []
    for f in range(4):
        rows = pl.ds(f * LANES, LANES)
        copies.append(pltpu.make_async_copy(couple.at[rows], couple_s.at[rows], sem.at[f]))
    copies.append(pltpu.make_async_copy(blocks, blocks_s, sem.at[4]))
    copies.append(pltpu.make_async_copy(diag, diag_s, sem.at[5]))
    copies.append(pltpu.make_async_copy(row_coarse, rows_s, sem.at[6]))
    copies.append(pltpu.make_async_copy(lower, lower_s, sem.at[7]))
    copies.append(pltpu.make_async_copy(upper, upper_s, sem.at[8]))
    for copy in copies:
        copy.start()
    hots = one_hot_faces(order[...])
    copies[5].wait()
    diag_o[...] = to_shared(jnp.broadcast_to(diag_s[...], (8, diag_s.shape[1])), hots)[:1]
    for f in range(4):
        rows = slice(f * LANES, (f + 1) * LANES)
        copies[f].wait()
        for n, piece in enumerate(cut(couple_s[rows, :], PIECES)):
            couple_o[n, rows, :] = narrow(hots[f], piece).astype(BF16)
    copies[4].wait()
    for f in range(4):
        for n, piece in enumerate(cut(blocks_s[f], PIECES)):
            blocks_o[n, f] = piece
    for n in (6, 7, 8):
        copies[n].wait()
    count = lower_s.shape[1]
    lane = lax.broadcasted_iota(jnp.int32, (count, LANES), 1)
    eye = lax.broadcasted_iota(jnp.int32, (count, count), 0) == lax.broadcasted_iota(
        jnp.int32, (count, count), 1
    )
    tile = jnp.zeros((count, LANES), F32)
    for n in range(count):
        tile = tile + jnp.where(lane == 112 + n, rows_s[:, n : n + 1], 0.0)
    for n, ref in ((120, lower_s), (121, upper_s)):
        column = jnp.sum(
            jnp.where(eye, jnp.broadcast_to(ref[...], (count, count)), 0.0), axis=1, keepdims=True
        )
        tile = tile + jnp.where(lane == n, column, 0.0)
    coefs_o[0:24, :] = jnp.zeros((24, LANES), F32)
    coefs_o[24:32, :] = tile


def k_first(place, shared, g0, g1, g2, g3, neumann, avg, r_o, share_o, prim_o, t_o, *sends):
    at = Place(place)
    rhs = r_o.shape[0]
    full = assembled(shared[...], (g0, g1, g2, g3), at, shared.shape[0], keep=False)
    share = shared[rhs : rhs + 1, :] / full[rhs : rhs + 1]
    south, north, west, east = faces_of(full[:rhs])
    r = jnp.concatenate([south * at.keep_south, north * at.keep_north, west, east], axis=1)
    r_o[...] = r
    share_o[...] = share
    weighted = share * r
    prim_o[...] = mm_t(avg[...], weighted)
    t = jnp.concatenate([share * product(weighted, held(neumann)), share * avg[...]], axis=0)
    t_o[...] = t
    put_sends(sends, t, at)


def k_schur(
    place, t, g0, g1, g2, g3, diag, couple, blocks, z_o, q_o, s0, s1, s2, s3, z_s, sem, *, rhs
):
    at = Place(place)
    z = assembled(t[...], (g0, g1, g2, g3), at, rhs)
    z_s[...] = z
    copy = pltpu.make_async_copy(z_s, z_o, sem.at[0])
    copy.start()
    q = schur(z, diag[...], held(couple), held(blocks))
    q_o[...] = q
    put_sends((s0, s1, s2, s3), q, at)
    copy.wait()


def k_second(place, q, g0, g1, g2, g3, r, share, neumann, avg, v_o, t_o, pr_o, *sends):
    at = Place(place)
    rhs = r.shape[0]
    w = assembled(q[...], (g0, g1, g2, g3), at, rhs)
    v = jnp.concatenate([w[:rhs] - SHIFT * r[...], w[rhs:]], axis=0)
    v_o[...] = v
    weighted = share[...] * v
    pr_o[...] = jnp.concatenate(
        [mm_t(avg[...], weighted[:rhs]), mm_t(avg[...], weighted[rhs:])], axis=1
    )
    t = share[...] * product(weighted, held(neumann))
    t_o[...] = t
    put_sends(sends, t, at)


def k_third(place, q, g0, g1, g2, g3, v, share, avg, prim0, prim1, v2_o, pay_o, v2_s, sem):
    at = Place(place)
    rhs = prim0.shape[1]
    w = assembled(q[...], (g0, g1, g2, g3), at, rhs)
    zero = jnp.zeros((16, w.shape[1]), F32)
    older = jnp.concatenate([v[...][:rhs], zero, v[...][rhs:], zero], axis=0)
    v2 = w - SHIFT * older
    v2_s[...] = v2
    copy = pltpu.make_async_copy(v2_s, v2_o, sem.at[0])
    copy.start()
    weighted = share[...] * v2
    prim2 = mm_t(avg[...], weighted[:rhs])
    reach2 = mm_t(avg[...], weighted[rhs:])
    reach1 = prim1[...][:, rhs:]
    spare = jnp.zeros((8, LANES - reach1.shape[1] - reach2.shape[1]), F32)
    tail = jnp.concatenate([reach1, reach2, spare], axis=1)
    pay = jnp.concatenate([prim0[...], prim1[...][:, :rhs], prim2, tail], axis=0)
    for item in range(pay_o.shape[0]):
        pay_o[item] = pay
    copy.wait()


def summed(got):
    total = got[0]
    for item in range(1, got.shape[0]):
        total = total + got[item]
    return total


def k_sum_halves(got, coefs, out):
    total = summed(got) + coefs[...]
    half = total.shape[0] // 2
    for item in range(out.shape[0]):
        out[item] = total[half * (item % 2) : half * (item % 2) + half]


def k_sum_spread(got, out):
    total = summed(got)
    for item in range(out.shape[0]):
        out[item] = total


def banded_product(pieces, value):
    first, second = cut(value, 2)
    return (narrow(pieces[1], first) + narrow(pieces[0], second)) + narrow(pieces[0], first)


def coarse_rows(totals, lowers, uppers):
    carry = jnp.zeros_like(totals[0])
    smooth = []
    for low, value in zip(lowers, [(1.0 - low) * value for low, value in zip(lowers, totals)]):
        carry = low * carry + value
        smooth.append(carry)
    carry = jnp.zeros_like(totals[0])
    tops = []
    smooth = [(1.0 - up) * value for up, value in zip(uppers, smooth)]
    for up, value in zip(uppers[::-1], smooth[::-1]):
        carry = up * carry + value
        tops.append(carry)
    return tops[::-1]


def k_fourth(place, v2, share, neumann, after, t_o, *sends):
    at = Place(place)
    t = share[...] * product(share[...] * v2[...], held(neumann))
    t_o[...] = t
    put_sends(sends, t, at)


def lift(coefs, basis):
    spare = -coefs.shape[0] % 16
    if spare:
        coefs = jnp.concatenate([coefs, jnp.zeros((spare, coefs.shape[1]), F32)], axis=0)
        basis = jnp.concatenate([basis, jnp.zeros((spare, basis.shape[1]), F32)], axis=0)
    c, b = cut(coefs, 2), cut(basis, 2)

    def times(x, y):
        return lax.dot_general(x, y, (((0,), (0,)), ((), ())), preferred_element_type=F32)

    return (times(c[1], b[0]) + times(c[0], b[1])) + times(c[0], b[0])


def k_core(
    place, mine, other, t, g0, g1, g2, g3, z0, v1, z1, v2, r, diag, couple, blocks,
    z0_o, z1_o, z2_o, w0_o, w1_o, q_o, pay_o, s0, s1, s2, s3,
    band0, band1, band2, c0_s, c1_s, c2_s, full_s, sem,
):
    at = Place(place)
    rhs = r.shape[0]
    rows = mine.shape[0]
    width = band0.shape[1]
    lane = lax.broadcasted_iota(jnp.int32, (8, width), 1)
    lowers, uppers = [], []
    for ref in (band0, band1, band2):
        if ref.shape[0] > rows * 8:
            ref[rows * 8 :, :] = jnp.zeros((ref.shape[0] - rows * 8, width), F32)
    upper = [jnp.where(at.even_row, mine[k], other[k]) for k in range(rows)]
    lower = [jnp.where(at.even_row, other[k], mine[k]) for k in range(rows)]
    for k in range(rows):
        tail = lower[k][8:16]
        lowers.append(jnp.broadcast_to(tail[:, 120:121], (8, rhs)))
        uppers.append(jnp.broadcast_to(tail[:, 121:122], (8, rhs)))
        wide = tail
        if width > LANES:
            wide = jnp.concatenate([tail, jnp.zeros((8, width - LANES), F32)], axis=1)
        for ref, first, last, to in (
            (band1, 0, 40, 8 * (k - 2)),
            (band2, 40, 112, 8 * (k - 4)),
            (band0, 112, 120, 8 * k),
        ):
            picked = jnp.where((lane >= first) & (lane < last), wide, 0.0)
            ref[8 * k : 8 * k + 8, :] = pltpu.roll(picked, (to - first) % width, 1)

    def stacked(tiles):
        if width > rows * 8:
            tiles = tiles + [jnp.zeros((width - rows * 8, rhs), F32)]
        return jnp.concatenate(tiles, axis=0)

    own, near, wide = [cut(ref[...], 2) for ref in (band0, band1, band2)]

    def solve(total):
        tiles = [total[8 * k : 8 * k + 8] for k in range(rows)]
        return stacked(coarse_rows(tiles, lowers, uppers)) + banded_product(own, total)

    edge = jnp.zeros((40, rhs), F32)
    c0 = solve(stacked([part[0:8] for part in upper]))
    c1 = solve(stacked([part[8:16] for part in upper]) + banded_product(near, c0))
    c2 = solve(
        stacked([part[0:8] for part in lower])
        + banded_product(wide, c0)
        + banded_product(near, c1)
    )
    for ref, value in ((c0_s, c0), (c1_s, c1), (c2_s, c2)):
        ref[0:40, :] = edge
        ref[40 : 40 + width, :] = value
        ref[40 + width :, :] = edge
    start = at.row * 8
    c0 = c0_s[pl.ds(pl.multiple_of(start, 8), 88), :]
    c1 = c1_s[pl.ds(pl.multiple_of(start + 16, 8), 56), :]
    c2 = c2_s[pl.ds(pl.multiple_of(start + 32, 8), 24), :]
    r0 = r[...]
    z2 = assembled(t[...], (g0, g1, g2, g3), at, rhs)
    z2f = z2[:rhs] + lift(
        jnp.concatenate([c0, c1, c2], axis=0),
        jnp.concatenate([z2[rhs:], z1[rhs:, :], z0[rhs:, :]], axis=0),
    )
    q = schur(z2f, diag[...], held(couple), held(blocks))
    q_o[...] = q
    put_sends((s0, s1, s2, s3), q, at)
    z0f = z0[:rhs, :] + lift(c0[32:56], z0[rhs:, :])
    v1f = v1[:rhs, :] + lift(c0[24:64], v1[rhs:, :])
    z1f = z1[:rhs, :] + lift(
        jnp.concatenate([c0[16:72], c1[16:40]], axis=0),
        jnp.concatenate([z1[rhs:, :], z0[rhs:, :]], axis=0),
    )
    v2f = v2[:rhs, :] + lift(
        jnp.concatenate([c0[8:80], c1[8:48]], axis=0),
        jnp.concatenate([v2[rhs:, :], v1[rhs:, :]], axis=0),
    )
    kept = ((z0f, z0_o), (z1f, z1_o), (z2f, z2_o), (v1f + SHIFT * r0, w0_o), (v2f + SHIFT * v1f, w1_o))
    copies = []
    for n, (value, out) in enumerate(kept):
        full_s[n] = value
        copies.append(pltpu.make_async_copy(full_s.at[n], out, sem.at[n]))
        copies[n].start()
    table = dot_rows(
        [(r0, z0f), (r0, z1f), (v1f, z0f), (v1f, z1f), (v2f, z1f)]
        + [(r0, z2f), (v1f, z2f), (v2f, z2f), (z2f, q + q)]
    )
    line = jnp.concatenate([table[i : i + 1] for i in range(9)], axis=1)
    for item in range(pay_o.shape[0]):
        pay_o[item] = line
    for copy in copies:
        copy.wait()


def dot_rows(pairs):
    parts = []
    for a, b in pairs:
        faces = faces_of(a * b)
        parts.append((faces[0] + faces[1]) + (faces[2] + faces[3]))
    wide = jnp.concatenate(parts, axis=1)
    shape = (16, wide.shape[1])
    pick = jnp.where(
        lax.broadcasted_iota(jnp.int32, shape, 0) == lax.broadcasted_iota(jnp.int32, shape, 1) // LANES,
        1.0,
        0.0,
    ).astype(BF16)
    high, middle, low = [narrow(pick, piece, True) for piece in cut(wide, 3)]
    return (low + middle) + high


def k_final(place, got, q, g0, g1, g2, g3, order, r0, z0, z1, z2, w0, w1, x_o, r_o):
    w2 = assembled(q[...], (g0, g1, g2, g3), Place(place), q.shape[0])
    total = summed(got)
    v0z0, v0z1, v1z0, v1z1, v2z1, v0z2, v1z2, v2z2, z2w2 = [
        total[:, i * LANES : (i + 1) * LANES] for i in range(9)
    ]
    z1w0 = v1z1 + SHIFT * v0z1
    z2w0 = v1z2 + SHIFT * v0z2
    z2w1 = v2z2 + SHIFT * v1z2
    zw = [
        [v1z0 + SHIFT * v0z0, z1w0, z2w0],
        [z1w0, v2z1 + SHIFT * v1z1, z2w1],
        [z2w0, z2w1, z2w2],
    ]
    vz = [[v0z0, v0z1, v0z2], [v1z0, v1z1, v1z2], [z1w0 - SHIFT * v1z0, v2z1, v2z2]]

    def form(left, table, right):
        value = None
        for i, a in enumerate(left):
            for j, b in enumerate(right):
                if a is None or b is None:
                    continue
                term = a * table[i][j] * b
                value = term if value is None else value + term
        return value

    one = jnp.ones_like(vz[0][0])
    zero = jnp.zeros_like(one)
    toward = [one, None, None]
    steps = [zero, zero, zero]
    drops = [zero, zero, zero]
    rz = vz[0][0]
    for iteration in range(3):
        alpha = rz / form(toward, zw, toward)
        for j in range(3):
            if toward[j] is not None:
                steps[j] = steps[j] + alpha * toward[j]
                drops[j] = drops[j] - alpha * toward[j]
        if iteration < 2:
            mix = [one + SHIFT * drops[0], drops[0] + SHIFT * drops[1], None]
            if iteration == 1:
                mix[2] = drops[1]
            new = form(mix, vz, mix)
            beta = new / rz
            toward = [
                m if d is None else (beta * d if m is None else m + beta * d)
                for m, d in zip(mix, toward)
            ]
            rz = new
    table = jnp.concatenate(steps + drops + [zero, zero], axis=0)
    eye = jnp.where(
        lax.broadcasted_iota(jnp.int32, (LANES, LANES), 0)
        == lax.broadcasted_iota(jnp.int32, (LANES, LANES), 1),
        1.0,
        0.0,
    ).astype(F32)
    columns = mm_t(eye, table)
    col = [columns[:, i : i + 1] for i in range(6)]
    hots = one_hot_faces(order[...])
    x = col[0] * z0[...] + col[1] * z1[...] + col[2] * z2[...]
    r = r0[...] + col[3] * w0[...] + col[4] * w1[...] + col[5] * w2
    both = to_points(jnp.concatenate([x, r], axis=0), hots)
    rhs = x.shape[0]
    x_o[...] = both[:rhs]
    r_o[...] = both[rhs:]


def call(body, outs, place, *args, scratch=(), raw=(), raw_outs=(), flops=1_000_000):
    args = tuple(
        pltpu.with_memory_space_constraint(arg, pltpu.HBM) if n in raw else arg
        for n, arg in enumerate(args)
    )
    space = [pltpu.HBM if n in raw else pltpu.VMEM for n in range(len(args))]
    specs = [pl.BlockSpec(memory_space=kind) for kind in space]
    if place is not None:
        specs = [pl.BlockSpec(memory_space=pltpu.SMEM)] + specs
        args = (place,) + args
    return pl.pallas_call(
        body,
        out_shape=[
            out
            if isinstance(out, jax.ShapeDtypeStruct)
            else (pltpu.HBM(out, F32) if n in raw_outs else jax.ShapeDtypeStruct(out, F32))
            for n, out in enumerate(outs)
        ],
        in_specs=specs,
        out_specs=[
            pl.BlockSpec(memory_space=pltpu.HBM if n in raw_outs else pltpu.VMEM)
            for n in range(len(outs))
        ],
        scratch_shapes=list(scratch),
        compiler_params=pltpu.CompilerParams(vmem_limit_bytes=16 * 1024 * 1024),
        cost_estimate=pl.CostEstimate(flops=flops, bytes_accessed=1_000_000, transcendentals=0),
    )(*args)


def exchange(sends, rows, columns):
    core = [(i, i ^ 1) for i in range(rows)]
    link = [(i, i + 1 if i % 2 else i - 1) for i in range(1, rows - 1)]
    near = [(i, i ^ 1) for i in range(columns)]
    far = [(i, (i + 1 if i % 2 else i - 1) % columns) for i in range(columns)]
    return [
        lax.ppermute(sends[0], "circ", far),
        lax.ppermute(sends[1], "circ", near),
        lax.ppermute(sends[2], "axial", link),
        lax.ppermute(sends[3], "axial", core),
    ]


def spread(value, axis):
    return lax.all_to_all(value, axis, split_axis=0, concat_axis=0, tiled=True)


def local(
    load_terms, diffusivity, interface_diag, coupling, interior_inverse, neumann_solve,
    row_coarse, lower_coef, upper_coef, face_order, primal_lists,
):
    rows, columns = lax.axis_size("axial"), lax.axis_size("circ")
    rhs, points = load_terms.shape[2], load_terms.shape[3]
    place = jnp.stack(
        [lax.axis_index("axial"), jnp.int32(rows), lax.axis_index("circ")]
    ).astype(jnp.int32)
    swap = functools.partial(exchange, rows=rows, columns=columns)
    dma = pltpu.SemaphoreType.DMA

    def face(n):
        return [(n, LANES)] * 4

    def bf16(*shape):
        return jax.ShapeDtypeStruct((PIECES,) + shape, BF16)

    shared, order, *sends = call(
        k_prepare,
        [(rhs + 8, points), jax.ShapeDtypeStruct((1, points), jnp.int32)] + face(rhs + 8),
        place, load_terms[0, 0], diffusivity[0], face_order[0],
        raw=(0, 1, 2),
        scratch=[pltpu.VMEM((rhs, points), F32), pltpu.VMEM((1, points), F32), dma((3,))],
    )
    got = swap(sends)
    neumann, avg = call(
        k_neumann,
        [bf16(points, points), (8, points)],
        None, order, neumann_solve[0, 0], primal_lists[0, 0],
        raw=(1, 2),
        scratch=[
            pltpu.VMEM((points, points), F32),
            pltpu.VMEM(primal_lists.shape[2:], jnp.int32),
            dma((5,)),
        ],
        flops=2_000_000_000,
    )
    r0, share, prim0, t0, *sends = call(
        k_first,
        [(rhs, points), (1, points), (8, rhs), (rhs + 8, points)] + face(rhs + 8),
        place, shared, *got, neumann, avg,
    )
    got = swap(sends)
    inner = interior_inverse.shape[2:]
    diag, couple, blocks, coefs = call(
        k_couple,
        [(1, points), bf16(points, points), bf16(*inner), (32, LANES)],
        None, order, share, interface_diag[0], coupling[0, 0], interior_inverse[0, 0],
        row_coarse[0], lower_coef, upper_coef,
        raw=(2, 3, 4, 5, 6, 7),
        scratch=[
            pltpu.VMEM((1, points), F32),
            pltpu.VMEM((points, points), F32),
            pltpu.VMEM(inner, F32),
            pltpu.VMEM(row_coarse.shape[1:], F32),
            pltpu.VMEM(lower_coef.shape, F32),
            pltpu.VMEM(upper_coef.shape, F32),
            dma((9,)),
        ],
        flops=2_000_000_000,
    )
    n = rhs + 24
    z0, q0, *sends = call(
        functools.partial(k_schur, rhs=rhs), [(n, points)] * 2 + face(n),
        place, t0, *got, diag, couple, blocks,
        raw_outs=(0,), scratch=[pltpu.VMEM((n, points), F32), dma((1,))],
    )
    got = swap(sends)
    n = rhs + 40
    v1, t1, prim1, *sends = call(
        k_second, [(n, points)] * 2 + [(8, n)] + face(n), place, q0, *got, r0, share, neumann, avg
    )
    got = swap(sends)
    n = rhs + 56
    z1, q1, *sends = call(
        functools.partial(k_schur, rhs=rhs), [(n, points)] * 2 + face(n),
        place, t1, *got, diag, couple, blocks,
        raw_outs=(0,), scratch=[pltpu.VMEM((n, points), F32), dma((1,))],
    )
    got = swap(sends)
    n = rhs + 72
    v2, pay = call(
        k_third, [(n, points), (columns, 32, LANES)], place, q1, *got, v1, share, avg, prim0, prim1,
        raw_outs=(0,), scratch=[pltpu.VMEM((n, points), F32), dma((1,))],
    )
    got = spread(pay, "circ")
    (pay,) = call(k_sum_halves, [(rows, 16, LANES)], None, got, coefs)
    mine = spread(pay, "axial")
    t2, *sends = call(
        k_fourth, [(n, points)] + face(n), place, v2, share, neumann, pay, flops=500_000_000
    )
    mine, *got = lax.optimization_barrier((mine, *swap(sends)))
    other = lax.ppermute(mine, "axial", [(i, i ^ 1) for i in range(rows)])
    width = max(LANES, 8 * rows)
    z0f, z1f, z2f, w0f, w1f, q2, pay, *sends = call(
        k_core,
        [(rhs, points)] * 6 + [(columns, 1, 9 * LANES)] + face(rhs),
        place, mine, other, t2, *got, z0, v1, z1, v2, r0, diag, couple, blocks,
        raw_outs=(0, 1, 2, 3, 4),
        scratch=[pltpu.VMEM((width, width), F32)] * 3
        + [pltpu.VMEM((width + 80, rhs), F32)] * 3
        + [pltpu.VMEM((5, rhs, points), F32), dma((5,))],
    )
    dots = spread(pay, "circ")
    got = swap(sends)
    (pay,) = call(k_sum_spread, [(rows, 1, 9 * LANES)], None, dots)
    dots = spread(pay, "axial")
    x, r = call(
        k_final, [(rhs, points)] * 2,
        place, dots, q2, *got, order, r0, z0f, z1f, z2f, w0f, w1f,
    )
    return (x[None, None], r[None, None])


def solution(mesh):
    in_specs = (
        P("axial", "circ", None, None),
        P("axial", "circ", None),
        P("axial", "circ", None),
        P("axial", "circ", None, None),
        P("axial", "circ", None, None, None),
        P("axial", "circ", None, None),
        P("axial", None, None),
        P("axial", None),
        P("axial", None),
        P("axial", "circ", None),
        P("axial", "circ", None, None),
    )
    out_specs = (P("axial", "circ", None, None), P("axial", "circ", None, None))
    return jax.shard_map(local, mesh=mesh, in_specs=in_specs, out_specs=out_specs, check_vma=False)
```

```python
import functools

import jax
import jax.numpy as jnp
from jax import lax
from jax.experimental import pallas as pl
from jax.experimental.pallas import tpu as pltpu
from jax.sharding import PartitionSpec as P

SHIFT = 12.0
HIGHEST = lax.Precision.HIGHEST
F32 = jnp.float32
BF16 = jnp.bfloat16
LANES = 128
PIECES = 2


def mm_t(a, b):
    return lax.dot_general(
        a, b, (((1,), (1,)), ((), ())), precision=HIGHEST, preferred_element_type=F32
    )


def cut(value, count):
    pieces = []
    for _ in range(count):
        piece = value.astype(BF16)
        pieces.append(piece)
        value = value - piece.astype(F32)
    return pieces


def narrow(a, b, transposed=False):
    return lax.dot_general(
        a, b, (((1,), (1 if transposed else 0,)), ((), ())), preferred_element_type=F32
    )


def product(a, pieces, transposed=False):
    count = a.shape[0]
    levels = len(pieces)
    if count % 16:
        a = jnp.concatenate([a, jnp.zeros((16 - count % 16, a.shape[1]), F32)], axis=0)
    tall = a.shape[0]
    left = cut(a, levels)
    by_level = [None] * levels
    for n, piece in enumerate(pieces):
        used = left[: levels - n]
        stack = used[0] if len(used) == 1 else jnp.concatenate(used, axis=0)
        out = narrow(stack, piece, transposed)
        for m in range(len(used)):
            part = out[m * tall : (m + 1) * tall]
            level = n + m
            by_level[level] = part if by_level[level] is None else by_level[level] + part
    total = by_level[-1]
    for part in by_level[-2::-1]:
        total = total + part
    return total[:count]


def select_columns(a, hot, transposed):
    count = a.shape[0]
    if count % 16:
        a = jnp.concatenate([a, jnp.zeros((16 - count % 16, a.shape[1]), F32)], axis=0)
    tall = a.shape[0]
    out = narrow(jnp.concatenate(cut(a, 3), axis=0), hot, transposed)
    return ((out[2 * tall :] + out[tall : 2 * tall]) + out[:tall])[:count]


def faces_of(full):
    return [full[:, f * LANES : (f + 1) * LANES] for f in range(4)]


def one_hot_faces(order):
    rows = lax.broadcasted_iota(jnp.int32, (LANES, LANES), 0)
    return [
        jnp.where(order[:, f * LANES : (f + 1) * LANES] - f * LANES == rows, 1.0, 0.0)
        .astype(F32)
        .astype(BF16)
        for f in range(4)
    ]


def to_shared(full, hots):
    return jnp.concatenate(
        [select_columns(part, hot, True) for part, hot in zip(faces_of(full), hots)], axis=1
    )


def to_points(full, hots):
    return jnp.concatenate(
        [select_columns(part, hot, False) for part, hot in zip(faces_of(full), hots)], axis=1
    )


class Place:
    def __init__(self, place):
        row, rows, column = place[0], place[1], place[2]
        self.row = row
        self.even_row = lax.rem(row, 2) == 0
        self.even_column = lax.rem(column, 2) == 0
        self.keep_south = jnp.where(row > 0, 1.0, 0.0).astype(F32)
        self.keep_north = jnp.where(row < rows - 1, 1.0, 0.0).astype(F32)


def put_sends(sends, full, at):
    south, north, west, east = faces_of(full)
    sends[0][...] = jnp.where(at.even_column, west, east)
    sends[1][...] = jnp.where(at.even_column, east, west)
    sends[2][...] = jnp.where(at.even_row, south, north)
    sends[3][...] = jnp.where(at.even_row, north, south)


def neighbours(got, at):
    far, near, link, core = [ref[...] for ref in got]
    above = jnp.where(at.even_row, core, link)
    below = jnp.where(at.even_row, link, core)
    right = jnp.where(at.even_column, near, far)
    left = jnp.where(at.even_column, far, near)
    return below, above, left, right


def assembled(full, got, at, rhs, keep=True):
    count = full.shape[0]
    extra = count - rhs
    own = faces_of(full)
    other = neighbours(got, at)
    scale = (at.keep_south, at.keep_north, None, None)
    shift = (0, 16, 8, 8)
    out = []
    for f in range(4):
        part = own[f][:rhs] + other[f][:rhs]
        if extra:
            zero = jnp.zeros((8, LANES), F32)
            mine = jnp.concatenate([zero, own[f][rhs:], zero], axis=0)
            pieces = [jnp.zeros((shift[f], LANES), F32)] if shift[f] else []
            pieces.append(other[f][rhs:])
            if shift[f] < 16:
                pieces.append(jnp.zeros((16 - shift[f], LANES), F32))
            part = jnp.concatenate([part, mine + jnp.concatenate(pieces, axis=0)], axis=0)
        if keep and scale[f] is not None:
            part = part * scale[f]
        out.append(part)
    return jnp.concatenate(out, axis=1)


def held(ref):
    return [ref[n] for n in range(ref.shape[0])]


def schur(z, diag, couple, blocks):
    inner = product(z, couple)
    solved = jnp.concatenate(
        [
            product(part, [piece[n] for piece in blocks])
            for n, part in enumerate(faces_of(inner))
        ],
        axis=1,
    )
    return diag * z - product(solved, couple, True)


def k_prepare(place, load, rho, order, shared_o, order_o, s0, s1, s2, s3, load_s, rho_s, sem):
    at = Place(place)
    copies = [
        pltpu.make_async_copy(source, target, sem.at[n])
        for n, (source, target) in enumerate(((order, order_o), (load, load_s), (rho, rho_s)))
    ]
    for copy in copies:
        copy.start()
    copies[0].wait()
    hots = one_hot_faces(order_o[...])
    copies[1].wait()
    copies[2].wait()
    pad = jnp.zeros((7, rho_s.shape[1]), F32)
    full = to_shared(jnp.concatenate([load_s[...], rho_s[...], pad], axis=0), hots)
    shared_o[...] = full
    put_sends((s0, s1, s2, s3), full, at)


def k_neumann(order, neumann, lists, neumann_o, avg_o, neumann_s, lists_s, sem):
    listed = pltpu.make_async_copy(lists, lists_s, sem.at[4])
    listed.start()
    copies = []
    for f in range(4):
        rows = pl.ds(f * LANES, LANES)
        copies.append(pltpu.make_async_copy(neumann.at[rows], neumann_s.at[rows], sem.at[f]))
        copies[f].start()
    hots = one_hot_faces(order[...])
    points = order.shape[1]
    listed.wait()
    named = lists_s[...]
    position = lax.broadcasted_iota(jnp.int32, (8, points), 1)
    total = jnp.zeros((8, points), F32)
    length = named.shape[1]
    for item in range(length):
        total = total + jnp.where(named[:, item : item + 1] == position, 1.0, 0.0)
    avg_o[...] = to_shared(total * (1.0 / length), hots)
    for f in range(4):
        rows = slice(f * LANES, (f + 1) * LANES)
        copies[f].wait()
        for n, piece in enumerate(cut(neumann_s[rows, :], PIECES)):
            half = narrow(hots[f], piece).astype(BF16)
            neumann_o[n, rows, :] = jnp.concatenate(
                [narrow(part, hot, True) for part, hot in zip(faces_of(half), hots)], axis=1
            ).astype(BF16)


def k_couple(
    order, after, diag, couple, blocks, row_coarse, lower, upper,
    diag_o, couple_o, blocks_o, coefs_o,
    diag_s, couple_s, blocks_s, rows_s, lower_s, upper_s, sem,
):
    copies = []
    for f in range(4):
        rows = pl.ds(f * LANES, LANES)
        copies.append(pltpu.make_async_copy(couple.at[rows], couple_s.at[rows], sem.at[f]))
    copies.append(pltpu.make_async_copy(blocks, blocks_s, sem.at[4]))
    copies.append(pltpu.make_async_copy(diag, diag_s, sem.at[5]))
    copies.append(pltpu.make_async_copy(row_coarse, rows_s, sem.at[6]))
    copies.append(pltpu.make_async_copy(lower, lower_s, sem.at[7]))
    copies.append(pltpu.make_async_copy(upper, upper_s, sem.at[8]))
    for copy in copies:
        copy.start()
    hots = one_hot_faces(order[...])
    copies[5].wait()
    diag_o[...] = to_shared(jnp.broadcast_to(diag_s[...], (8, diag_s.shape[1])), hots)[:1]
    for f in range(4):
        rows = slice(f * LANES, (f + 1) * LANES)
        copies[f].wait()
        for n, piece in enumerate(cut(couple_s[rows, :], PIECES)):
            couple_o[n, rows, :] = narrow(hots[f], piece).astype(BF16)
    copies[4].wait()
    for f in range(4):
        for n, piece in enumerate(cut(blocks_s[f], PIECES)):
            blocks_o[n, f] = piece
    for n in (6, 7, 8):
        copies[n].wait()
    count = lower_s.shape[1]
    lane = lax.broadcasted_iota(jnp.int32, (count, LANES), 1)
    eye = lax.broadcasted_iota(jnp.int32, (count, count), 0) == lax.broadcasted_iota(
        jnp.int32, (count, count), 1
    )
    tile = jnp.zeros((count, LANES), F32)
    for n in range(count):
        tile = tile + jnp.where(lane == 112 + n, rows_s[:, n : n + 1], 0.0)
    for n, ref in ((120, lower_s), (121, upper_s)):
        column = jnp.sum(
            jnp.where(eye, jnp.broadcast_to(ref[...], (count, count)), 0.0), axis=1, keepdims=True
        )
        tile = tile + jnp.where(lane == n, column, 0.0)
    coefs_o[0:24, :] = jnp.zeros((24, LANES), F32)
    coefs_o[24:32, :] = tile


def k_first(place, shared, g0, g1, g2, g3, neumann, avg, r_o, share_o, prim_o, t_o, *sends):
    at = Place(place)
    rhs = r_o.shape[0]
    full = assembled(shared[...], (g0, g1, g2, g3), at, shared.shape[0], keep=False)
    share = shared[rhs : rhs + 1, :] / full[rhs : rhs + 1]
    south, north, west, east = faces_of(full[:rhs])
    r = jnp.concatenate([south * at.keep_south, north * at.keep_north, west, east], axis=1)
    r_o[...] = r
    share_o[...] = share
    weighted = share * r
    prim_o[...] = mm_t(avg[...], weighted)
    t = jnp.concatenate([share * product(weighted, held(neumann)), share * avg[...]], axis=0)
    t_o[...] = t
    put_sends(sends, t, at)


def k_schur(
    place, t, g0, g1, g2, g3, diag, couple, blocks, z_o, q_o, s0, s1, s2, s3, z_s, sem, *, rhs
):
    at = Place(place)
    z = assembled(t[...], (g0, g1, g2, g3), at, rhs)
    z_s[...] = z
    copy = pltpu.make_async_copy(z_s, z_o, sem.at[0])
    copy.start()
    q = schur(z, diag[...], held(couple), held(blocks))
    q_o[...] = q
    put_sends((s0, s1, s2, s3), q, at)
    copy.wait()


def k_second(place, q, g0, g1, g2, g3, r, share, neumann, avg, v_o, t_o, pr_o, *sends):
    at = Place(place)
    rhs = r.shape[0]
    w = assembled(q[...], (g0, g1, g2, g3), at, rhs)
    v = jnp.concatenate([w[:rhs] - SHIFT * r[...], w[rhs:]], axis=0)
    v_o[...] = v
    weighted = share[...] * v
    pr_o[...] = jnp.concatenate(
        [mm_t(avg[...], weighted[:rhs]), mm_t(avg[...], weighted[rhs:])], axis=1
    )
    t = share[...] * product(weighted, held(neumann))
    t_o[...] = t
    put_sends(sends, t, at)


def k_third(place, q, g0, g1, g2, g3, v, share, avg, prim0, prim1, v2_o, pay_o, v2_s, sem):
    at = Place(place)
    rhs = prim0.shape[1]
    w = assembled(q[...], (g0, g1, g2, g3), at, rhs)
    zero = jnp.zeros((16, w.shape[1]), F32)
    older = jnp.concatenate([v[...][:rhs], zero, v[...][rhs:], zero], axis=0)
    v2 = w - SHIFT * older
    v2_s[...] = v2
    copy = pltpu.make_async_copy(v2_s, v2_o, sem.at[0])
    copy.start()
    weighted = share[...] * v2
    prim2 = mm_t(avg[...], weighted[:rhs])
    reach2 = mm_t(avg[...], weighted[rhs:])
    reach1 = prim1[...][:, rhs:]
    spare = jnp.zeros((8, LANES - reach1.shape[1] - reach2.shape[1]), F32)
    tail = jnp.concatenate([reach1, reach2, spare], axis=1)
    pay = jnp.concatenate([prim0[...], prim1[...][:, :rhs], prim2, tail], axis=0)
    for item in range(pay_o.shape[0]):
        pay_o[item] = pay
    copy.wait()


def summed(got):
    total = got[0]
    for item in range(1, got.shape[0]):
        total = total + got[item]
    return total


def k_sum_halves(got, coefs, out):
    total = summed(got) + coefs[...]
    half = total.shape[0] // 2
    for item in range(out.shape[0]):
        out[item] = total[half * (item % 2) : half * (item % 2) + half]


def k_sum_spread(got, out):
    total = summed(got)
    for item in range(out.shape[0]):
        out[item] = total


def banded_product(pieces, value):
    first, second = cut(value, 2)
    return (narrow(pieces[1], first) + narrow(pieces[0], second)) + narrow(pieces[0], first)


def coarse_rows(totals, lowers, uppers):
    carry = jnp.zeros_like(totals[0])
    smooth = []
    for low, value in zip(lowers, [(1.0 - low) * value for low, value in zip(lowers, totals)]):
        carry = low * carry + value
        smooth.append(carry)
    carry = jnp.zeros_like(totals[0])
    tops = []
    smooth = [(1.0 - up) * value for up, value in zip(uppers, smooth)]
    for up, value in zip(uppers[::-1], smooth[::-1]):
        carry = up * carry + value
        tops.append(carry)
    return tops[::-1]


def k_fourth(place, v2, share, neumann, t_o, s0, s1, s2, s3, v2_s, t_s, sem):
    at = Place(place)
    copy = pltpu.make_async_copy(v2, v2_s, sem.at[0])
    copy.start()
    copy.wait()
    t = share[...] * product(share[...] * v2_s[...], held(neumann))
    t_s[...] = t
    copy = pltpu.make_async_copy(t_s, t_o, sem.at[1])
    copy.start()
    put_sends((s0, s1, s2, s3), t, at)
    copy.wait()


def lift(coefs, basis):
    spare = -coefs.shape[0] % 16
    if spare:
        coefs = jnp.concatenate([coefs, jnp.zeros((spare, coefs.shape[1]), F32)], axis=0)
        basis = jnp.concatenate([basis, jnp.zeros((spare, basis.shape[1]), F32)], axis=0)
    c, b = cut(coefs, 2), cut(basis, 2)

    def times(x, y):
        return lax.dot_general(x, y, (((0,), (0,)), ((), ())), preferred_element_type=F32)

    return (times(c[1], b[0]) + times(c[0], b[1])) + times(c[0], b[0])


def k_core(
    place, mine, other, t, g0, g1, g2, g3, z0, v1, z1, v2, r, diag, couple, blocks,
    z0_o, z1_o, z2_o, w0_o, w1_o, q_o, pay_o, s0, s1, s2, s3,
    band0, band1, band2, c0_s, c1_s, c2_s, full_s, t_s, z0_s, z1_s, v2_s, sem, in_sem,
):
    at = Place(place)
    loads = [
        pltpu.make_async_copy(source, target, in_sem.at[n])
        for n, (source, target) in enumerate(((t, t_s), (z1, z1_s), (z0, z0_s), (v2, v2_s)))
    ]
    for load in loads:
        load.start()
    t, z0, z1, v2 = t_s, z0_s, z1_s, v2_s
    rhs = r.shape[0]
    rows = mine.shape[0]
    width = band0.shape[1]
    lane = lax.broadcasted_iota(jnp.int32, (8, width), 1)
    lowers, uppers = [], []
    for ref in (band0, band1, band2):
        if ref.shape[0] > rows * 8:
            ref[rows * 8 :, :] = jnp.zeros((ref.shape[0] - rows * 8, width), F32)
    upper = [jnp.where(at.even_row, mine[k], other[k]) for k in range(rows)]
    lower = [jnp.where(at.even_row, other[k], mine[k]) for k in range(rows)]
    for k in range(rows):
        tail = lower[k][8:16]
        lowers.append(jnp.broadcast_to(tail[:, 120:121], (8, rhs)))
        uppers.append(jnp.broadcast_to(tail[:, 121:122], (8, rhs)))
        wide = tail
        if width > LANES:
            wide = jnp.concatenate([tail, jnp.zeros((8, width - LANES), F32)], axis=1)
        for ref, first, last, to in (
            (band1, 0, 40, 8 * (k - 2)),
            (band2, 40, 112, 8 * (k - 4)),
            (band0, 112, 120, 8 * k),
        ):
            picked = jnp.where((lane >= first) & (lane < last), wide, 0.0)
            ref[8 * k : 8 * k + 8, :] = pltpu.roll(picked, (to - first) % width, 1)

    def stacked(tiles):
        if width > rows * 8:
            tiles = tiles + [jnp.zeros((width - rows * 8, rhs), F32)]
        return jnp.concatenate(tiles, axis=0)

    own, near, wide = [cut(ref[...], 2) for ref in (band0, band1, band2)]

    def solve(total):
        tiles = [total[8 * k : 8 * k + 8] for k in range(rows)]
        return stacked(coarse_rows(tiles, lowers, uppers)) + banded_product(own, total)

    edge = jnp.zeros((40, rhs), F32)
    c0 = solve(stacked([part[0:8] for part in upper]))
    c1 = solve(stacked([part[8:16] for part in upper]) + banded_product(near, c0))
    c2 = solve(
        stacked([part[0:8] for part in lower])
        + banded_product(wide, c0)
        + banded_product(near, c1)
    )
    for ref, value in ((c0_s, c0), (c1_s, c1), (c2_s, c2)):
        ref[0:40, :] = edge
        ref[40 : 40 + width, :] = value
        ref[40 + width :, :] = edge
    start = at.row * 8
    c0 = c0_s[pl.ds(pl.multiple_of(start, 8), 88), :]
    c1 = c1_s[pl.ds(pl.multiple_of(start + 16, 8), 56), :]
    c2 = c2_s[pl.ds(pl.multiple_of(start + 32, 8), 24), :]
    r0 = r[...]
    for load in loads:
        load.wait()
    z2 = assembled(t[...], (g0, g1, g2, g3), at, rhs)
    z2f = z2[:rhs] + lift(
        jnp.concatenate([c0, c1, c2], axis=0),
        jnp.concatenate([z2[rhs:], z1[rhs:, :], z0[rhs:, :]], axis=0),
    )
    q = schur(z2f, diag[...], held(couple), held(blocks))
    q_o[...] = q
    put_sends((s0, s1, s2, s3), q, at)
    z0f = z0[:rhs, :] + lift(c0[32:56], z0[rhs:, :])
    v1f = v1[:rhs, :] + lift(c0[24:64], v1[rhs:, :])
    z1f = z1[:rhs, :] + lift(
        jnp.concatenate([c0[16:72], c1[16:40]], axis=0),
        jnp.concatenate([z1[rhs:, :], z0[rhs:, :]], axis=0),
    )
    v2f = v2[:rhs, :] + lift(
        jnp.concatenate([c0[8:80], c1[8:48]], axis=0),
        jnp.concatenate([v2[rhs:, :], v1[rhs:, :]], axis=0),
    )
    kept = ((z0f, z0_o), (z1f, z1_o), (z2f, z2_o), (v1f + SHIFT * r0, w0_o), (v2f + SHIFT * v1f, w1_o))
    copies = []
    for n, (value, out) in enumerate(kept):
        full_s[n] = value
        copies.append(pltpu.make_async_copy(full_s.at[n], out, sem.at[n]))
        copies[n].start()
    table = dot_rows(
        [(r0, z0f), (r0, z1f), (v1f, z0f), (v1f, z1f), (v2f, z1f)]
        + [(r0, z2f), (v1f, z2f), (v2f, z2f), (z2f, q + q)]
    )
    line = jnp.concatenate([table[i : i + 1] for i in range(9)], axis=1)
    for item in range(pay_o.shape[0]):
        pay_o[item] = line
    for copy in copies:
        copy.wait()


def dot_rows(pairs):
    parts = []
    for a, b in pairs:
        faces = faces_of(a * b)
        parts.append((faces[0] + faces[1]) + (faces[2] + faces[3]))
    wide = jnp.concatenate(parts, axis=1)
    shape = (16, wide.shape[1])
    pick = jnp.where(
        lax.broadcasted_iota(jnp.int32, shape, 0) == lax.broadcasted_iota(jnp.int32, shape, 1) // LANES,
        1.0,
        0.0,
    ).astype(BF16)
    high, middle, low = [narrow(pick, piece, True) for piece in cut(wide, 3)]
    return (low + middle) + high


def k_final(
    place, got, q, g0, g1, g2, g3, order, r0, z0, z1, z2, w0, w1, x_o, r_o, full_s, sem
):
    loads = []
    for n, source in enumerate((z0, z1, z2, w0, w1)):
        loads.append(pltpu.make_async_copy(source, full_s.at[n], sem.at[n]))
        loads[n].start()
    w2 = assembled(q[...], (g0, g1, g2, g3), Place(place), q.shape[0])
    total = summed(got)
    v0z0, v0z1, v1z0, v1z1, v2z1, v0z2, v1z2, v2z2, z2w2 = [
        total[:, i * LANES : (i + 1) * LANES] for i in range(9)
    ]
    z1w0 = v1z1 + SHIFT * v0z1
    z2w0 = v1z2 + SHIFT * v0z2
    z2w1 = v2z2 + SHIFT * v1z2
    zw = [
        [v1z0 + SHIFT * v0z0, z1w0, z2w0],
        [z1w0, v2z1 + SHIFT * v1z1, z2w1],
        [z2w0, z2w1, z2w2],
    ]
    vz = [[v0z0, v0z1, v0z2], [v1z0, v1z1, v1z2], [z1w0 - SHIFT * v1z0, v2z1, v2z2]]

    def form(left, table, right):
        value = None
        for i, a in enumerate(left):
            for j, b in enumerate(right):
                if a is None or b is None:
                    continue
                term = a * table[i][j] * b
                value = term if value is None else value + term
        return value

    one = jnp.ones_like(vz[0][0])
    zero = jnp.zeros_like(one)
    toward = [one, None, None]
    steps = [zero, zero, zero]
    drops = [zero, zero, zero]
    rz = vz[0][0]
    for iteration in range(3):
        alpha = rz / form(toward, zw, toward)
        for j in range(3):
            if toward[j] is not None:
                steps[j] = steps[j] + alpha * toward[j]
                drops[j] = drops[j] - alpha * toward[j]
        if iteration < 2:
            mix = [one + SHIFT * drops[0], drops[0] + SHIFT * drops[1], None]
            if iteration == 1:
                mix[2] = drops[1]
            new = form(mix, vz, mix)
            beta = new / rz
            toward = [
                m if d is None else (beta * d if m is None else m + beta * d)
                for m, d in zip(mix, toward)
            ]
            rz = new
    table = jnp.concatenate(steps + drops + [zero, zero], axis=0)
    eye = jnp.where(
        lax.broadcasted_iota(jnp.int32, (LANES, LANES), 0)
        == lax.broadcasted_iota(jnp.int32, (LANES, LANES), 1),
        1.0,
        0.0,
    ).astype(F32)
    columns = mm_t(eye, table)
    col = [columns[:, i : i + 1] for i in range(6)]
    hots = one_hot_faces(order[...])
    for load in loads:
        load.wait()
    x = col[0] * full_s[0] + col[1] * full_s[1] + col[2] * full_s[2]
    r = r0[...] + col[3] * full_s[3] + col[4] * full_s[4] + col[5] * w2
    both = to_points(jnp.concatenate([x, r], axis=0), hots)
    rhs = x.shape[0]
    x_o[...] = both[:rhs]
    r_o[...] = both[rhs:]


def call(body, outs, place, *args, scratch=(), raw=(), raw_outs=(), flops=1_000_000):
    args = tuple(
        pltpu.with_memory_space_constraint(arg, pltpu.HBM) if n in raw else arg
        for n, arg in enumerate(args)
    )
    space = [pltpu.HBM if n in raw else pltpu.VMEM for n in range(len(args))]
    specs = [pl.BlockSpec(memory_space=kind) for kind in space]
    if place is not None:
        specs = [pl.BlockSpec(memory_space=pltpu.SMEM)] + specs
        args = (place,) + args
    return pl.pallas_call(
        body,
        out_shape=[
            out
            if isinstance(out, jax.ShapeDtypeStruct)
            else (pltpu.HBM(out, F32) if n in raw_outs else jax.ShapeDtypeStruct(out, F32))
            for n, out in enumerate(outs)
        ],
        in_specs=specs,
        out_specs=[
            pl.BlockSpec(memory_space=pltpu.HBM if n in raw_outs else pltpu.VMEM)
            for n in range(len(outs))
        ],
        scratch_shapes=list(scratch),
        compiler_params=pltpu.CompilerParams(vmem_limit_bytes=16 * 1024 * 1024),
        cost_estimate=pl.CostEstimate(flops=flops, bytes_accessed=1_000_000, transcendentals=0),
    )(*args)


def exchange_columns(sends, columns):
    near = [(i, i ^ 1) for i in range(columns)]
    far = [(i, (i + 1 if i % 2 else i - 1) % columns) for i in range(columns)]
    return [lax.ppermute(sends[0], "circ", far), lax.ppermute(sends[1], "circ", near)]


def exchange_rows(sends, rows):
    core = [(i, i ^ 1) for i in range(rows)]
    link = [(i, i + 1 if i % 2 else i - 1) for i in range(1, rows - 1)]
    return [lax.ppermute(sends[2], "axial", link), lax.ppermute(sends[3], "axial", core)]


def exchange(sends, rows, columns):
    return exchange_columns(sends, columns) + exchange_rows(sends, rows)


def spread(value, axis):
    return lax.all_to_all(value, axis, split_axis=0, concat_axis=0, tiled=True)


def local(
    load_terms, diffusivity, interface_diag, coupling, interior_inverse, neumann_solve,
    row_coarse, lower_coef, upper_coef, face_order, primal_lists,
):
    rows, columns = lax.axis_size("axial"), lax.axis_size("circ")
    rhs, points = load_terms.shape[2], load_terms.shape[3]
    place = jnp.stack(
        [lax.axis_index("axial"), jnp.int32(rows), lax.axis_index("circ")]
    ).astype(jnp.int32)
    swap = functools.partial(exchange, rows=rows, columns=columns)
    dma = pltpu.SemaphoreType.DMA

    def face(n):
        return [(n, LANES)] * 4

    def bf16(*shape):
        return jax.ShapeDtypeStruct((PIECES,) + shape, BF16)

    shared, order, *sends = call(
        k_prepare,
        [(rhs + 8, points), jax.ShapeDtypeStruct((1, points), jnp.int32)] + face(rhs + 8),
        place, load_terms[0, 0], diffusivity[0], face_order[0],
        raw=(0, 1, 2),
        scratch=[pltpu.VMEM((rhs, points), F32), pltpu.VMEM((1, points), F32), dma((3,))],
    )
    got = swap(sends)
    neumann, avg = call(
        k_neumann,
        [bf16(points, points), (8, points)],
        None, order, neumann_solve[0, 0], primal_lists[0, 0],
        raw=(1, 2),
        scratch=[
            pltpu.VMEM((points, points), F32),
            pltpu.VMEM(primal_lists.shape[2:], jnp.int32),
            dma((5,)),
        ],
        flops=2_000_000_000,
    )
    r0, share, prim0, t0, *sends = call(
        k_first,
        [(rhs, points), (1, points), (8, rhs), (rhs + 8, points)] + face(rhs + 8),
        place, shared, *got, neumann, avg,
    )
    got = swap(sends)
    inner = interior_inverse.shape[2:]
    diag, couple, blocks, coefs = call(
        k_couple,
        [(1, points), bf16(points, points), bf16(*inner), (32, LANES)],
        None, order, share, interface_diag[0], coupling[0, 0], interior_inverse[0, 0],
        row_coarse[0], lower_coef, upper_coef,
        raw=(2, 3, 4, 5, 6, 7),
        scratch=[
            pltpu.VMEM((1, points), F32),
            pltpu.VMEM((points, points), F32),
            pltpu.VMEM(inner, F32),
            pltpu.VMEM(row_coarse.shape[1:], F32),
            pltpu.VMEM(lower_coef.shape, F32),
            pltpu.VMEM(upper_coef.shape, F32),
            dma((9,)),
        ],
        flops=2_000_000_000,
    )
    n = rhs + 24
    z0, q0, *sends = call(
        functools.partial(k_schur, rhs=rhs), [(n, points)] * 2 + face(n),
        place, t0, *got, diag, couple, blocks,
        raw_outs=(0,), scratch=[pltpu.VMEM((n, points), F32), dma((1,))],
    )
    got = swap(sends)
    n = rhs + 40
    v1, t1, prim1, *sends = call(
        k_second, [(n, points)] * 2 + [(8, n)] + face(n), place, q0, *got, r0, share, neumann, avg
    )
    got = swap(sends)
    n = rhs + 56
    z1, q1, *sends = call(
        functools.partial(k_schur, rhs=rhs), [(n, points)] * 2 + face(n),
        place, t1, *got, diag, couple, blocks,
        raw_outs=(0,), scratch=[pltpu.VMEM((n, points), F32), dma((1,))],
    )
    got = swap(sends)
    n = rhs + 72
    v2, pay = call(
        k_third, [(n, points), (columns, 32, LANES)], place, q1, *got, v1, share, avg, prim0, prim1,
        raw_outs=(0,), scratch=[pltpu.VMEM((n, points), F32), dma((1,))],
    )
    got = spread(pay, "circ")
    t2, *sends = call(
        k_fourth, [(n, points)] + face(n), place, v2, share, neumann,
        raw=(0,), raw_outs=(0,),
        scratch=[pltpu.VMEM((n, points), F32)] * 2 + [dma((2,))],
        flops=500_000_000,
    )
    got, t2 = lax.optimization_barrier((got, t2))
    (pay,) = call(k_sum_halves, [(rows, 16, LANES)], None, got, coefs)
    pay, *sends = lax.optimization_barrier((pay, *sends))
    mine = spread(pay, "axial")
    mine, *got = lax.optimization_barrier((mine, *swap(sends)))
    other = lax.ppermute(mine, "axial", [(i, i ^ 1) for i in range(rows)])
    width = max(LANES, 8 * rows)
    z0f, z1f, z2f, w0f, w1f, q2, pay, *sends = call(
        k_core,
        [(rhs, points)] * 6 + [(columns, 1, 9 * LANES)] + face(rhs),
        place, mine, other, t2, *got, z0, v1, z1, v2, r0, diag, couple, blocks,
        raw=(2, 7, 9, 10),
        raw_outs=(0, 1, 2, 3, 4),
        scratch=[pltpu.VMEM((width, width), F32)] * 3
        + [pltpu.VMEM((width + 80, rhs), F32)] * 3
        + [pltpu.VMEM((5, rhs, points), F32)]
        + [pltpu.VMEM((rhs + m, points), F32) for m in (72, 24, 56, 72)]
        + [dma((5,)), dma((4,))],
    )
    dots = spread(pay, "circ")
    got = exchange_columns(sends, columns)
    dots, *got = lax.optimization_barrier((dots, *got))
    (pay,) = call(k_sum_spread, [(rows, 1, 9 * LANES)], None, dots)
    pay, *sends = lax.optimization_barrier((pay, *sends))
    dots = spread(pay, "axial")
    got = got + exchange_rows(sends, rows)
    x, r = call(
        k_final, [(rhs, points)] * 2,
        place, dots, q2, *got, order, r0, z0f, z1f, z2f, w0f, w1f,
        raw=(8, 9, 10, 11, 12),
        scratch=[pltpu.VMEM((5, rhs, points), F32), dma((5,))],
    )
    return (x[None, None], r[None, None])


def solution(mesh):
    in_specs = (
        P("axial", "circ", None, None),
        P("axial", "circ", None),
        P("axial", "circ", None),
        P("axial", "circ", None, None),
        P("axial", "circ", None, None, None),
        P("axial", "circ", None, None),
        P("axial", None, None),
        P("axial", None),
        P("axial", None),
        P("axial", "circ", None),
        P("axial", "circ", None, None),
    )
    out_specs = (P("axial", "circ", None, None), P("axial", "circ", None, None))
    return jax.shard_map(local, mesh=mesh, in_specs=in_specs, out_specs=out_specs, check_vma=False)
```

```python
import functools

import jax
import jax.numpy as jnp
from jax import lax
from jax.experimental import pallas as pl
from jax.experimental.pallas import tpu as pltpu
from jax.sharding import PartitionSpec as P

SHIFT = 12.0
HIGHEST = lax.Precision.HIGHEST
F32 = jnp.float32
BF16 = jnp.bfloat16
LANES = 128
PIECES = 2


def mm_t(a, b):
    return lax.dot_general(
        a, b, (((1,), (1,)), ((), ())), precision=HIGHEST, preferred_element_type=F32
    )


def cut(value, count):
    pieces = []
    for _ in range(count):
        piece = value.astype(BF16)
        pieces.append(piece)
        value = value - piece.astype(F32)
    return pieces


def narrow(a, b, transposed=False):
    return lax.dot_general(
        a, b, (((1,), (1 if transposed else 0,)), ((), ())), preferred_element_type=F32
    )


def product(a, pieces, transposed=False):
    count = a.shape[0]
    levels = len(pieces)
    if count % 16:
        a = jnp.concatenate([a, jnp.zeros((16 - count % 16, a.shape[1]), F32)], axis=0)
    tall = a.shape[0]
    left = cut(a, levels)
    by_level = [None] * levels
    for n, piece in enumerate(pieces):
        used = left[: levels - n]
        stack = used[0] if len(used) == 1 else jnp.concatenate(used, axis=0)
        out = narrow(stack, piece, transposed)
        for m in range(len(used)):
            part = out[m * tall : (m + 1) * tall]
            level = n + m
            by_level[level] = part if by_level[level] is None else by_level[level] + part
    total = by_level[-1]
    for part in by_level[-2::-1]:
        total = total + part
    return total[:count]


def select_columns(a, hot, transposed):
    count = a.shape[0]
    if count % 16:
        a = jnp.concatenate([a, jnp.zeros((16 - count % 16, a.shape[1]), F32)], axis=0)
    tall = a.shape[0]
    out = narrow(jnp.concatenate(cut(a, 3), axis=0), hot, transposed)
    return ((out[2 * tall :] + out[tall : 2 * tall]) + out[:tall])[:count]


def faces_of(full):
    return [full[:, f * LANES : (f + 1) * LANES] for f in range(4)]


def one_hot_faces(order):
    rows = lax.broadcasted_iota(jnp.int32, (LANES, LANES), 0)
    return [
        jnp.where(order[:, f * LANES : (f + 1) * LANES] - f * LANES == rows, 1.0, 0.0)
        .astype(F32)
        .astype(BF16)
        for f in range(4)
    ]


def to_shared(full, hots):
    return jnp.concatenate(
        [select_columns(part, hot, True) for part, hot in zip(faces_of(full), hots)], axis=1
    )


def to_points(full, hots):
    return jnp.concatenate(
        [select_columns(part, hot, False) for part, hot in zip(faces_of(full), hots)], axis=1
    )


class Place:
    def __init__(self, place):
        row, rows, column = place[0], place[1], place[2]
        self.row = row
        self.even_row = lax.rem(row, 2) == 0
        self.even_column = lax.rem(column, 2) == 0
        self.keep_south = jnp.where(row > 0, 1.0, 0.0).astype(F32)
        self.keep_north = jnp.where(row < rows - 1, 1.0, 0.0).astype(F32)


def put_sends(sends, full, at):
    south, north, west, east = faces_of(full)
    sends[0][...] = jnp.where(at.even_column, west, east)
    sends[1][...] = jnp.where(at.even_column, east, west)
    sends[2][...] = jnp.where(at.even_row, south, north)
    sends[3][...] = jnp.where(at.even_row, north, south)


def neighbours(got, at):
    far, near, link, core = [ref[...] for ref in got]
    above = jnp.where(at.even_row, core, link)
    below = jnp.where(at.even_row, link, core)
    right = jnp.where(at.even_column, near, far)
    left = jnp.where(at.even_column, far, near)
    return below, above, left, right


def assembled(full, got, at, rhs, keep=True):
    count = full.shape[0]
    extra = count - rhs
    own = faces_of(full)
    other = neighbours(got, at)
    scale = (at.keep_south, at.keep_north, None, None)
    shift = (0, 16, 8, 8)
    out = []
    for f in range(4):
        part = own[f][:rhs] + other[f][:rhs]
        if extra:
            zero = jnp.zeros((8, LANES), F32)
            mine = jnp.concatenate([zero, own[f][rhs:], zero], axis=0)
            pieces = [jnp.zeros((shift[f], LANES), F32)] if shift[f] else []
            pieces.append(other[f][rhs:])
            if shift[f] < 16:
                pieces.append(jnp.zeros((16 - shift[f], LANES), F32))
            part = jnp.concatenate([part, mine + jnp.concatenate(pieces, axis=0)], axis=0)
        if keep and scale[f] is not None:
            part = part * scale[f]
        out.append(part)
    return jnp.concatenate(out, axis=1)


def held(ref):
    return [ref[n] for n in range(ref.shape[0])]


def schur(z, diag, couple, blocks):
    inner = product(z, couple)
    solved = jnp.concatenate(
        [
            product(part, [piece[n] for piece in blocks])
            for n, part in enumerate(faces_of(inner))
        ],
        axis=1,
    )
    return diag * z - product(solved, couple, True)


def begin(source, target, sems, parts):
    rows = source.shape[0] // 8
    edges = [8 * (rows * n // parts) for n in range(parts)] + [source.shape[0]]
    copies = []
    for n in range(parts):
        band = pl.ds(edges[n], edges[n + 1] - edges[n])
        copies.append(pltpu.make_async_copy(source.at[band], target.at[band], sems.at[n]))
        copies[n].start()
    return copies


def finish(copies):
    for copy in copies:
        copy.wait()


def k_prepare(place, load, rho, order, shared_o, order_o, s0, s1, s2, s3, load_s, rho_s, sem):
    at = Place(place)
    copies = [
        pltpu.make_async_copy(source, target, sem.at[n])
        for n, (source, target) in enumerate(((order, order_o), (load, load_s), (rho, rho_s)))
    ]
    for copy in copies:
        copy.start()
    copies[0].wait()
    hots = one_hot_faces(order_o[...])
    copies[1].wait()
    copies[2].wait()
    pad = jnp.zeros((7, rho_s.shape[1]), F32)
    full = to_shared(jnp.concatenate([load_s[...], rho_s[...], pad], axis=0), hots)
    shared_o[...] = full
    put_sends((s0, s1, s2, s3), full, at)


def k_neumann(order, neumann, lists, neumann_o, avg_o, neumann_s, lists_s, sem):
    listed = pltpu.make_async_copy(lists, lists_s, sem.at[4])
    listed.start()
    copies = []
    for f in range(4):
        rows = pl.ds(f * LANES, LANES)
        copies.append(pltpu.make_async_copy(neumann.at[rows], neumann_s.at[rows], sem.at[f]))
        copies[f].start()
    hots = one_hot_faces(order[...])
    points = order.shape[1]
    listed.wait()
    named = lists_s[...]
    position = lax.broadcasted_iota(jnp.int32, (8, points), 1)
    total = jnp.zeros((8, points), F32)
    length = named.shape[1]
    for item in range(length):
        total = total + jnp.where(named[:, item : item + 1] == position, 1.0, 0.0)
    avg_o[...] = to_shared(total * (1.0 / length), hots)
    for f in range(4):
        rows = slice(f * LANES, (f + 1) * LANES)
        copies[f].wait()
        for n, piece in enumerate(cut(neumann_s[rows, :], PIECES)):
            half = narrow(hots[f], piece).astype(BF16)
            neumann_o[n, rows, :] = jnp.concatenate(
                [narrow(part, hot, True) for part, hot in zip(faces_of(half), hots)], axis=1
            ).astype(BF16)


def k_couple(
    order, after, diag, couple, blocks, row_coarse, lower, upper,
    diag_o, couple_o, blocks_o, coefs_o,
    diag_s, couple_s, blocks_s, rows_s, lower_s, upper_s, sem,
):
    copies = []
    for f in range(4):
        rows = pl.ds(f * LANES, LANES)
        copies.append(pltpu.make_async_copy(couple.at[rows], couple_s.at[rows], sem.at[f]))
    copies.append(pltpu.make_async_copy(blocks, blocks_s, sem.at[4]))
    copies.append(pltpu.make_async_copy(diag, diag_s, sem.at[5]))
    copies.append(pltpu.make_async_copy(row_coarse, rows_s, sem.at[6]))
    copies.append(pltpu.make_async_copy(lower, lower_s, sem.at[7]))
    copies.append(pltpu.make_async_copy(upper, upper_s, sem.at[8]))
    for copy in copies:
        copy.start()
    hots = one_hot_faces(order[...])
    copies[5].wait()
    diag_o[...] = to_shared(jnp.broadcast_to(diag_s[...], (8, diag_s.shape[1])), hots)[:1]
    for f in range(4):
        rows = slice(f * LANES, (f + 1) * LANES)
        copies[f].wait()
        for n, piece in enumerate(cut(couple_s[rows, :], PIECES)):
            couple_o[n, rows, :] = narrow(hots[f], piece).astype(BF16)
    copies[4].wait()
    for f in range(4):
        for n, piece in enumerate(cut(blocks_s[f], PIECES)):
            blocks_o[n, f] = piece
    for n in (6, 7, 8):
        copies[n].wait()
    count = lower_s.shape[1]
    lane = lax.broadcasted_iota(jnp.int32, (count, LANES), 1)
    eye = lax.broadcasted_iota(jnp.int32, (count, count), 0) == lax.broadcasted_iota(
        jnp.int32, (count, count), 1
    )
    tile = jnp.zeros((count, LANES), F32)
    for n in range(count):
        tile = tile + jnp.where(lane == 112 + n, rows_s[:, n : n + 1], 0.0)
    for n, ref in ((120, lower_s), (121, upper_s)):
        column = jnp.sum(
            jnp.where(eye, jnp.broadcast_to(ref[...], (count, count)), 0.0), axis=1, keepdims=True
        )
        tile = tile + jnp.where(lane == n, column, 0.0)
    coefs_o[0:24, :] = jnp.zeros((24, LANES), F32)
    coefs_o[24:32, :] = tile


def k_first(place, shared, g0, g1, g2, g3, neumann, avg, r_o, share_o, prim_o, t_o, *sends):
    at = Place(place)
    rhs = r_o.shape[0]
    full = assembled(shared[...], (g0, g1, g2, g3), at, shared.shape[0], keep=False)
    share = shared[rhs : rhs + 1, :] / full[rhs : rhs + 1]
    south, north, west, east = faces_of(full[:rhs])
    r = jnp.concatenate([south * at.keep_south, north * at.keep_north, west, east], axis=1)
    r_o[...] = r
    share_o[...] = share
    weighted = share * r
    prim_o[...] = mm_t(avg[...], weighted)
    t = jnp.concatenate([share * product(weighted, held(neumann)), share * avg[...]], axis=0)
    t_o[...] = t
    put_sends(sends, t, at)


def k_schur(
    place, t, g0, g1, g2, g3, diag, couple, blocks, z_o, q_o, s0, s1, s2, s3, z_s, sem, *, rhs
):
    at = Place(place)
    z = assembled(t[...], (g0, g1, g2, g3), at, rhs)
    z_s[...] = z
    copy = pltpu.make_async_copy(z_s, z_o, sem.at[0])
    copy.start()
    q = schur(z, diag[...], held(couple), held(blocks))
    q_o[...] = q
    put_sends((s0, s1, s2, s3), q, at)
    copy.wait()


def k_second(place, q, g0, g1, g2, g3, r, share, neumann, avg, v_o, t_o, pr_o, *sends):
    at = Place(place)
    rhs = r.shape[0]
    w = assembled(q[...], (g0, g1, g2, g3), at, rhs)
    v = jnp.concatenate([w[:rhs] - SHIFT * r[...], w[rhs:]], axis=0)
    v_o[...] = v
    weighted = share[...] * v
    pr_o[...] = jnp.concatenate(
        [mm_t(avg[...], weighted[:rhs]), mm_t(avg[...], weighted[rhs:])], axis=1
    )
    t = share[...] * product(weighted, held(neumann))
    t_o[...] = t
    put_sends(sends, t, at)


def k_third(place, q, g0, g1, g2, g3, v, share, avg, prim0, prim1, v2_o, pay_o, v2_s, sem):
    at = Place(place)
    rhs = prim0.shape[1]
    w = assembled(q[...], (g0, g1, g2, g3), at, rhs)
    zero = jnp.zeros((16, w.shape[1]), F32)
    older = jnp.concatenate([v[...][:rhs], zero, v[...][rhs:], zero], axis=0)
    v2 = w - SHIFT * older
    v2_s[...] = v2
    copies = begin(v2_s, v2_o, sem, 4)
    weighted = share[...] * v2
    prim2 = mm_t(avg[...], weighted[:rhs])
    reach2 = mm_t(avg[...], weighted[rhs:])
    reach1 = prim1[...][:, rhs:]
    spare = jnp.zeros((8, LANES - reach1.shape[1] - reach2.shape[1]), F32)
    tail = jnp.concatenate([reach1, reach2, spare], axis=1)
    pay = jnp.concatenate([prim0[...], prim1[...][:, :rhs], prim2, tail], axis=0)
    for item in range(pay_o.shape[0]):
        pay_o[item] = pay
    finish(copies)


def summed(got):
    total = got[0]
    for item in range(1, got.shape[0]):
        total = total + got[item]
    return total


def k_sum_spread(got, coefs, out):
    total = summed(got) + coefs[...]
    for item in range(out.shape[0]):
        out[item] = total


def banded_product(pieces, value):
    first, second = cut(value, 2)
    return (narrow(pieces[1], first) + narrow(pieces[0], second)) + narrow(pieces[0], first)


def coarse_rows(totals, lowers, uppers):
    carry = jnp.zeros_like(totals[0])
    smooth = []
    for low, value in zip(lowers, [(1.0 - low) * value for low, value in zip(lowers, totals)]):
        carry = low * carry + value
        smooth.append(carry)
    carry = jnp.zeros_like(totals[0])
    tops = []
    smooth = [(1.0 - up) * value for up, value in zip(uppers, smooth)]
    for up, value in zip(uppers[::-1], smooth[::-1]):
        carry = up * carry + value
        tops.append(carry)
    return tops[::-1]


def k_fourth(place, v2, share, neumann, t_o, s0, s1, s2, s3, v2_s, t_s, sem):
    at = Place(place)
    finish(begin(v2, v2_s, sem.at[0], 4))
    t = share[...] * product(share[...] * v2_s[...], held(neumann))
    t_s[...] = t
    copies = begin(t_s, t_o, sem.at[1], 4)
    put_sends((s0, s1, s2, s3), t, at)
    finish(copies)


def lift(coefs, basis):
    spare = -coefs.shape[0] % 16
    if spare:
        coefs = jnp.concatenate([coefs, jnp.zeros((spare, coefs.shape[1]), F32)], axis=0)
        basis = jnp.concatenate([basis, jnp.zeros((spare, basis.shape[1]), F32)], axis=0)
    c, b = cut(coefs, 2), cut(basis, 2)

    def times(x, y):
        return lax.dot_general(x, y, (((0,), (0,)), ((), ())), preferred_element_type=F32)

    return (times(c[1], b[0]) + times(c[0], b[1])) + times(c[0], b[0])


def k_core(
    place, mine, other, t, g0, g1, g2, g3, z0, v1, z1, v2, r, diag, couple, blocks,
    z0_o, z1_o, z2_o, w0_o, w1_o, q_o, pay_o, s0, s1, s2, s3,
    band0, band1, band2, c0_s, c1_s, c2_s, full_s, t_s, z0_s, z1_s, v2_s, sem, in_sem,
):
    at = Place(place)
    loads = []
    for n, (source, target) in enumerate(((z0, z0_s), (z1, z1_s), (v2, v2_s), (t, t_s))):
        loads += begin(source, target, in_sem.at[n], 2)
    t, z0, z1, v2 = t_s, z0_s, z1_s, v2_s
    rhs = r.shape[0]
    rows = 2 * mine.shape[0]
    width = band0.shape[1]
    lane = lax.broadcasted_iota(jnp.int32, (8, width), 1)
    lowers, uppers = [], []
    for ref in (band0, band1, band2):
        if ref.shape[0] > rows * 8:
            ref[rows * 8 :, :] = jnp.zeros((ref.shape[0] - rows * 8, width), F32)
    pays = []
    for k in range(rows // 2):
        pays.append(jnp.where(at.even_row, mine[k], other[k]))
        pays.append(jnp.where(at.even_row, other[k], mine[k]))
    for k in range(rows):
        tail = pays[k][24:32]
        lowers.append(jnp.broadcast_to(tail[:, 120:121], (8, rhs)))
        uppers.append(jnp.broadcast_to(tail[:, 121:122], (8, rhs)))
        wide = tail
        if width > LANES:
            wide = jnp.concatenate([tail, jnp.zeros((8, width - LANES), F32)], axis=1)
        for ref, first, last, to in (
            (band1, 0, 40, 8 * (k - 2)),
            (band2, 40, 112, 8 * (k - 4)),
            (band0, 112, 120, 8 * k),
        ):
            picked = jnp.where((lane >= first) & (lane < last), wide, 0.0)
            ref[8 * k : 8 * k + 8, :] = pltpu.roll(picked, (to - first) % width, 1)

    def stacked(tiles):
        if width > rows * 8:
            tiles = tiles + [jnp.zeros((width - rows * 8, rhs), F32)]
        return jnp.concatenate(tiles, axis=0)

    own, near, wide = [cut(ref[...], 2) for ref in (band0, band1, band2)]

    def solve(total):
        tiles = [total[8 * k : 8 * k + 8] for k in range(rows)]
        return stacked(coarse_rows(tiles, lowers, uppers)) + banded_product(own, total)

    edge = jnp.zeros((40, rhs), F32)
    c0 = solve(stacked([part[0:8] for part in pays]))
    c1 = solve(stacked([part[8:16] for part in pays]) + banded_product(near, c0))
    c2 = solve(
        stacked([part[16:24] for part in pays])
        + banded_product(wide, c0)
        + banded_product(near, c1)
    )
    for ref, value in ((c0_s, c0), (c1_s, c1), (c2_s, c2)):
        ref[0:40, :] = edge
        ref[40 : 40 + width, :] = value
        ref[40 + width :, :] = edge
    start = at.row * 8
    c0 = c0_s[pl.ds(pl.multiple_of(start, 8), 88), :]
    c1 = c1_s[pl.ds(pl.multiple_of(start + 16, 8), 56), :]
    c2 = c2_s[pl.ds(pl.multiple_of(start + 32, 8), 24), :]
    r0 = r[...]
    finish(loads)
    z0f = z0[:rhs, :] + lift(c0[32:56], z0[rhs:, :])
    v1f = v1[:rhs, :] + lift(c0[24:64], v1[rhs:, :])
    z1f = z1[:rhs, :] + lift(
        jnp.concatenate([c0[16:72], c1[16:40]], axis=0),
        jnp.concatenate([z1[rhs:, :], z0[rhs:, :]], axis=0),
    )
    v2f = v2[:rhs, :] + lift(
        jnp.concatenate([c0[8:80], c1[8:48]], axis=0),
        jnp.concatenate([v2[rhs:, :], v1[rhs:, :]], axis=0),
    )
    copies = []

    def keep(n, value, out):
        full_s[n] = value
        copies.extend(begin(full_s.at[n], out, sem.at[n], 2))

    keep(0, z0f, z0_o)
    keep(1, z1f, z1_o)
    keep(2, v1f + SHIFT * r0, w0_o)
    keep(3, v2f + SHIFT * v1f, w1_o)
    z2 = assembled(t[...], (g0, g1, g2, g3), at, rhs)
    z2f = z2[:rhs] + lift(
        jnp.concatenate([c0, c1, c2], axis=0),
        jnp.concatenate([z2[rhs:], z1[rhs:, :], z0[rhs:, :]], axis=0),
    )
    keep(4, z2f, z2_o)
    q = schur(z2f, diag[...], held(couple), held(blocks))
    q_o[...] = q
    put_sends((s0, s1, s2, s3), q, at)
    table = dot_rows(
        [(r0, z0f), (r0, z1f), (v1f, z0f), (v1f, z1f), (v2f, z1f)]
        + [(r0, z2f), (v1f, z2f), (v2f, z2f), (z2f, q + q)]
    )
    line = jnp.concatenate([table[i : i + 1] for i in range(9)], axis=1)
    for item in range(pay_o.shape[0]):
        pay_o[item] = line
    finish(copies)


def dot_rows(pairs):
    parts = []
    for a, b in pairs:
        faces = faces_of(a * b)
        parts.append((faces[0] + faces[1]) + (faces[2] + faces[3]))
    wide = jnp.concatenate(parts, axis=1)
    shape = (16, wide.shape[1])
    pick = jnp.where(
        lax.broadcasted_iota(jnp.int32, shape, 0) == lax.broadcasted_iota(jnp.int32, shape, 1) // LANES,
        1.0,
        0.0,
    ).astype(BF16)
    high, middle, low = [narrow(pick, piece, True) for piece in cut(wide, 3)]
    return (low + middle) + high


def k_final(
    place, got, q, g0, g1, g2, g3, order, r0, z0, z1, z2, w0, w1, x_o, r_o, full_s, sem
):
    loads = []
    for n, source in enumerate((z0, z1, z2, w0, w1)):
        loads += begin(source, full_s.at[n], sem.at[n], 2)
    w2 = assembled(q[...], (g0, g1, g2, g3), Place(place), q.shape[0])
    total = summed(got)
    v0z0, v0z1, v1z0, v1z1, v2z1, v0z2, v1z2, v2z2, z2w2 = [
        total[:, i * LANES : (i + 1) * LANES] for i in range(9)
    ]
    z1w0 = v1z1 + SHIFT * v0z1
    z2w0 = v1z2 + SHIFT * v0z2
    z2w1 = v2z2 + SHIFT * v1z2
    zw = [
        [v1z0 + SHIFT * v0z0, z1w0, z2w0],
        [z1w0, v2z1 + SHIFT * v1z1, z2w1],
        [z2w0, z2w1, z2w2],
    ]
    vz = [[v0z0, v0z1, v0z2], [v1z0, v1z1, v1z2], [z1w0 - SHIFT * v1z0, v2z1, v2z2]]

    def form(left, table, right):
        value = None
        for i, a in enumerate(left):
            for j, b in enumerate(right):
                if a is None or b is None:
                    continue
                term = a * table[i][j] * b
                value = term if value is None else value + term
        return value

    one = jnp.ones_like(vz[0][0])
    zero = jnp.zeros_like(one)
    toward = [one, None, None]
    steps = [zero, zero, zero]
    drops = [zero, zero, zero]
    rz = vz[0][0]
    for iteration in range(3):
        alpha = rz / form(toward, zw, toward)
        for j in range(3):
            if toward[j] is not None:
                steps[j] = steps[j] + alpha * toward[j]
                drops[j] = drops[j] - alpha * toward[j]
        if iteration < 2:
            mix = [one + SHIFT * drops[0], drops[0] + SHIFT * drops[1], None]
            if iteration == 1:
                mix[2] = drops[1]
            new = form(mix, vz, mix)
            beta = new / rz
            toward = [
                m if d is None else (beta * d if m is None else m + beta * d)
                for m, d in zip(mix, toward)
            ]
            rz = new
    table = jnp.concatenate(steps + drops + [zero, zero], axis=0)
    eye = jnp.where(
        lax.broadcasted_iota(jnp.int32, (LANES, LANES), 0)
        == lax.broadcasted_iota(jnp.int32, (LANES, LANES), 1),
        1.0,
        0.0,
    ).astype(F32)
    columns = mm_t(eye, table)
    col = [columns[:, i : i + 1] for i in range(6)]
    hots = one_hot_faces(order[...])
    finish(loads)
    x = col[0] * full_s[0] + col[1] * full_s[1] + col[2] * full_s[2]
    r = r0[...] + col[3] * full_s[3] + col[4] * full_s[4] + col[5] * w2
    both = to_points(jnp.concatenate([x, r], axis=0), hots)
    rhs = x.shape[0]
    x_o[...] = both[:rhs]
    r_o[...] = both[rhs:]


def call(body, outs, place, *args, scratch=(), raw=(), raw_outs=(), flops=1_000_000):
    args = tuple(
        pltpu.with_memory_space_constraint(arg, pltpu.HBM) if n in raw else arg
        for n, arg in enumerate(args)
    )
    space = [pltpu.HBM if n in raw else pltpu.VMEM for n in range(len(args))]
    specs = [pl.BlockSpec(memory_space=kind) for kind in space]
    if place is not None:
        specs = [pl.BlockSpec(memory_space=pltpu.SMEM)] + specs
        args = (place,) + args
    return pl.pallas_call(
        body,
        out_shape=[
            out
            if isinstance(out, jax.ShapeDtypeStruct)
            else (pltpu.HBM(out, F32) if n in raw_outs else jax.ShapeDtypeStruct(out, F32))
            for n, out in enumerate(outs)
        ],
        in_specs=specs,
        out_specs=[
            pl.BlockSpec(memory_space=pltpu.HBM if n in raw_outs else pltpu.VMEM)
            for n in range(len(outs))
        ],
        scratch_shapes=list(scratch),
        compiler_params=pltpu.CompilerParams(vmem_limit_bytes=16 * 1024 * 1024),
        cost_estimate=pl.CostEstimate(flops=flops, bytes_accessed=1_000_000, transcendentals=0),
    )(*args)


def exchange_columns(sends, columns):
    near = [(i, i ^ 1) for i in range(columns)]
    far = [(i, (i + 1 if i % 2 else i - 1) % columns) for i in range(columns)]
    return [lax.ppermute(sends[0], "circ", far), lax.ppermute(sends[1], "circ", near)]


def exchange_rows(sends, rows):
    core = [(i, i ^ 1) for i in range(rows)]
    link = [(i, i + 1 if i % 2 else i - 1) for i in range(1, rows - 1)]
    return [lax.ppermute(sends[2], "axial", link), lax.ppermute(sends[3], "axial", core)]


def exchange(sends, rows, columns):
    return exchange_columns(sends, columns) + exchange_rows(sends, rows)


def spread(value, axis, groups=None):
    return lax.all_to_all(
        value, axis, split_axis=0, concat_axis=0, tiled=True, axis_index_groups=groups
    )


def local(
    load_terms, diffusivity, interface_diag, coupling, interior_inverse, neumann_solve,
    row_coarse, lower_coef, upper_coef, face_order, primal_lists,
):
    rows, columns = lax.axis_size("axial"), lax.axis_size("circ")
    rhs, points = load_terms.shape[2], load_terms.shape[3]
    place = jnp.stack(
        [lax.axis_index("axial"), jnp.int32(rows), lax.axis_index("circ")]
    ).astype(jnp.int32)
    swap = functools.partial(exchange, rows=rows, columns=columns)
    dma = pltpu.SemaphoreType.DMA

    def face(n):
        return [(n, LANES)] * 4

    def bf16(*shape):
        return jax.ShapeDtypeStruct((PIECES,) + shape, BF16)

    shared, order, *sends = call(
        k_prepare,
        [(rhs + 8, points), jax.ShapeDtypeStruct((1, points), jnp.int32)] + face(rhs + 8),
        place, load_terms[0, 0], diffusivity[0], face_order[0],
        raw=(0, 1, 2),
        scratch=[pltpu.VMEM((rhs, points), F32), pltpu.VMEM((1, points), F32), dma((3,))],
    )
    got = swap(sends)
    neumann, avg = call(
        k_neumann,
        [bf16(points, points), (8, points)],
        None, order, neumann_solve[0, 0], primal_lists[0, 0],
        raw=(1, 2),
        scratch=[
            pltpu.VMEM((points, points), F32),
            pltpu.VMEM(primal_lists.shape[2:], jnp.int32),
            dma((5,)),
        ],
        flops=2_000_000_000,
    )
    r0, share, prim0, t0, *sends = call(
        k_first,
        [(rhs, points), (1, points), (8, rhs), (rhs + 8, points)] + face(rhs + 8),
        place, shared, *got, neumann, avg,
    )
    got = swap(sends)
    inner = interior_inverse.shape[2:]
    diag, couple, blocks, coefs = call(
        k_couple,
        [(1, points), bf16(points, points), bf16(*inner), (32, LANES)],
        None, order, share, interface_diag[0], coupling[0, 0], interior_inverse[0, 0],
        row_coarse[0], lower_coef, upper_coef,
        raw=(2, 3, 4, 5, 6, 7),
        scratch=[
            pltpu.VMEM((1, points), F32),
            pltpu.VMEM((points, points), F32),
            pltpu.VMEM(inner, F32),
            pltpu.VMEM(row_coarse.shape[1:], F32),
            pltpu.VMEM(lower_coef.shape, F32),
            pltpu.VMEM(upper_coef.shape, F32),
            dma((9,)),
        ],
        flops=2_000_000_000,
    )
    n = rhs + 24
    z0, q0, *sends = call(
        functools.partial(k_schur, rhs=rhs), [(n, points)] * 2 + face(n),
        place, t0, *got, diag, couple, blocks,
        raw_outs=(0,), scratch=[pltpu.VMEM((n, points), F32), dma((1,))],
    )
    got = swap(sends)
    n = rhs + 40
    v1, t1, prim1, *sends = call(
        k_second, [(n, points)] * 2 + [(8, n)] + face(n), place, q0, *got, r0, share, neumann, avg
    )
    got = swap(sends)
    n = rhs + 56
    z1, q1, *sends = call(
        functools.partial(k_schur, rhs=rhs), [(n, points)] * 2 + face(n),
        place, t1, *got, diag, couple, blocks,
        raw_outs=(0,), scratch=[pltpu.VMEM((n, points), F32), dma((1,))],
    )
    got = swap(sends)
    n = rhs + 72
    v2, pay = call(
        k_third, [(n, points), (columns, 32, LANES)], place, q1, *got, v1, share, avg, prim0, prim1,
        raw_outs=(0,), scratch=[pltpu.VMEM((n, points), F32), dma((4,))],
    )
    got = spread(pay, "circ")
    t2, *sends = call(
        k_fourth, [(n, points)] + face(n), place, v2, share, neumann,
        raw=(0,), raw_outs=(0,),
        scratch=[pltpu.VMEM((n, points), F32)] * 2 + [dma((2, 4))],
        flops=500_000_000,
    )
    got, t2 = lax.optimization_barrier((got, t2))
    (pay,) = call(k_sum_spread, [(rows // 2, 32, LANES)], None, got, coefs)
    pay, *sends = lax.optimization_barrier((pay, *sends))
    along = [list(range(core, rows, 2)) for core in range(2)]
    mine = spread(pay, "axial", along)
    mine, *got = lax.optimization_barrier((mine, *swap(sends)))
    other = lax.ppermute(mine, "axial", [(i, i ^ 1) for i in range(rows)])
    width = max(LANES, 8 * rows)
    z0f, z1f, z2f, w0f, w1f, q2, pay, *sends = call(
        k_core,
        [(rhs, points)] * 6 + [(2 * columns, 1, 9 * LANES)] + face(rhs),
        place, mine, other, t2, *got, z0, v1, z1, v2, r0, diag, couple, blocks,
        raw=(2, 7, 9, 10),
        raw_outs=(0, 1, 2, 3, 4),
        scratch=[pltpu.VMEM((width, width), F32)] * 3
        + [pltpu.VMEM((width + 80, rhs), F32)] * 3
        + [pltpu.VMEM((5, rhs, points), F32)]
        + [pltpu.VMEM((rhs + m, points), F32) for m in (72, 24, 56, 72)]
        + [dma((5, 2)), dma((4, 2))],
    )
    chips = [
        [row * columns + column for row in (pair, pair + 1) for column in range(columns)]
        for pair in range(0, rows, 2)
    ]
    dots = spread(pay, ("axial", "circ"), chips)
    got = exchange_columns(sends, columns)
    dots, *got = lax.optimization_barrier((dots, *got))
    blank = jnp.zeros((1, 9 * LANES), F32)
    (pay,) = call(k_sum_spread, [(rows // 2, 1, 9 * LANES)], None, dots, blank)
    pay, *sends = lax.optimization_barrier((pay, *sends))
    dots = spread(pay, "axial", along)
    got = got + exchange_rows(sends, rows)
    x, r = call(
        k_final, [(rhs, points)] * 2,
        place, dots, q2, *got, order, r0, z0f, z1f, z2f, w0f, w1f,
        raw=(8, 9, 10, 11, 12),
        scratch=[pltpu.VMEM((5, rhs, points), F32), dma((5, 2))],
    )
    return (x[None, None], r[None, None])


def solution(mesh):
    in_specs = (
        P("axial", "circ", None, None),
        P("axial", "circ", None),
        P("axial", "circ", None),
        P("axial", "circ", None, None),
        P("axial", "circ", None, None, None),
        P("axial", "circ", None, None),
        P("axial", None, None),
        P("axial", None),
        P("axial", None),
        P("axial", "circ", None),
        P("axial", "circ", None, None),
    )
    out_specs = (P("axial", "circ", None, None), P("axial", "circ", None, None))
    return jax.shard_map(local, mesh=mesh, in_specs=in_specs, out_specs=out_specs, check_vma=False)
```

```python
import functools

import jax
import jax.numpy as jnp
from jax import lax
from jax.experimental import pallas as pl
from jax.experimental.pallas import tpu as pltpu
from jax.sharding import PartitionSpec as P

SHIFT = 12.0
HIGHEST = lax.Precision.HIGHEST
F32 = jnp.float32
BF16 = jnp.bfloat16
LANES = 128
PIECES = 2


def mm_t(a, b):
    return lax.dot_general(
        a, b, (((1,), (1,)), ((), ())), precision=HIGHEST, preferred_element_type=F32
    )


def cut(value, count):
    pieces = []
    for _ in range(count):
        piece = value.astype(BF16)
        pieces.append(piece)
        value = value - piece.astype(F32)
    return pieces


def narrow(a, b, transposed=False):
    return lax.dot_general(
        a, b, (((1,), (1 if transposed else 0,)), ((), ())), preferred_element_type=F32
    )


def product(a, pieces, transposed=False):
    count = a.shape[0]
    levels = len(pieces)
    if count % 16:
        a = jnp.concatenate([a, jnp.zeros((16 - count % 16, a.shape[1]), F32)], axis=0)
    tall = a.shape[0]
    left = cut(a, levels)
    by_level = [None] * levels
    for n, piece in enumerate(pieces):
        used = left[: levels - n]
        stack = used[0] if len(used) == 1 else jnp.concatenate(used, axis=0)
        out = narrow(stack, piece, transposed)
        for m in range(len(used)):
            part = out[m * tall : (m + 1) * tall]
            level = n + m
            by_level[level] = part if by_level[level] is None else by_level[level] + part
    total = by_level[-1]
    for part in by_level[-2::-1]:
        total = total + part
    return total[:count]


def select_columns(a, hot, transposed):
    count = a.shape[0]
    if count % 16:
        a = jnp.concatenate([a, jnp.zeros((16 - count % 16, a.shape[1]), F32)], axis=0)
    tall = a.shape[0]
    out = narrow(jnp.concatenate(cut(a, 3), axis=0), hot, transposed)
    return ((out[2 * tall :] + out[tall : 2 * tall]) + out[:tall])[:count]


def faces_of(full):
    return [full[:, f * LANES : (f + 1) * LANES] for f in range(4)]


def one_hot_faces(order):
    rows = lax.broadcasted_iota(jnp.int32, (LANES, LANES), 0)
    return [
        jnp.where(order[:, f * LANES : (f + 1) * LANES] - f * LANES == rows, 1.0, 0.0)
        .astype(F32)
        .astype(BF16)
        for f in range(4)
    ]


def to_shared(full, hots):
    return jnp.concatenate(
        [select_columns(part, hot, True) for part, hot in zip(faces_of(full), hots)], axis=1
    )


def to_points(full, hots):
    return jnp.concatenate(
        [select_columns(part, hot, False) for part, hot in zip(faces_of(full), hots)], axis=1
    )


class Place:
    def __init__(self, place):
        row, rows, column = place[0], place[1], place[2]
        self.row = row
        self.even_row = lax.rem(row, 2) == 0
        self.even_column = lax.rem(column, 2) == 0
        self.keep_south = jnp.where(row > 0, 1.0, 0.0).astype(F32)
        self.keep_north = jnp.where(row < rows - 1, 1.0, 0.0).astype(F32)


def put_sends(sends, full, at):
    south, north, west, east = faces_of(full)
    sends[0][...] = jnp.where(at.even_column, west, east)
    sends[1][...] = jnp.where(at.even_column, east, west)
    sends[2][...] = jnp.where(at.even_row, south, north)
    sends[3][...] = jnp.where(at.even_row, north, south)


def neighbours(got, at):
    far, near, link, core = [ref[...] for ref in got]
    above = jnp.where(at.even_row, core, link)
    below = jnp.where(at.even_row, link, core)
    right = jnp.where(at.even_column, near, far)
    left = jnp.where(at.even_column, far, near)
    return below, above, left, right


def assembled(full, got, at, rhs, keep=True):
    count = full.shape[0]
    extra = count - rhs
    own = faces_of(full)
    other = neighbours(got, at)
    scale = (at.keep_south, at.keep_north, None, None)
    shift = (0, 16, 8, 8)
    out = []
    for f in range(4):
        part = own[f][:rhs] + other[f][:rhs]
        if extra:
            zero = jnp.zeros((8, LANES), F32)
            mine = jnp.concatenate([zero, own[f][rhs:], zero], axis=0)
            pieces = [jnp.zeros((shift[f], LANES), F32)] if shift[f] else []
            pieces.append(other[f][rhs:])
            if shift[f] < 16:
                pieces.append(jnp.zeros((16 - shift[f], LANES), F32))
            part = jnp.concatenate([part, mine + jnp.concatenate(pieces, axis=0)], axis=0)
        if keep and scale[f] is not None:
            part = part * scale[f]
        out.append(part)
    return jnp.concatenate(out, axis=1)


def held(ref):
    return [ref[n] for n in range(ref.shape[0])]


def schur(z, diag, couple, blocks):
    inner = product(z, couple)
    solved = jnp.concatenate(
        [
            product(part, [piece[n] for piece in blocks])
            for n, part in enumerate(faces_of(inner))
        ],
        axis=1,
    )
    return diag * z - product(solved, couple, True)


def begin(source, target, sems, parts):
    rows = source.shape[0] // 8
    edges = [8 * (rows * n // parts) for n in range(parts)] + [source.shape[0]]
    copies = []
    for n in range(parts):
        band = pl.ds(edges[n], edges[n + 1] - edges[n])
        copies.append(pltpu.make_async_copy(source.at[band], target.at[band], sems.at[n]))
        copies[n].start()
    return copies


def finish(copies):
    for copy in copies:
        copy.wait()


def k_prepare(
    place, load, rho, order, neumann, shared_o, order_o, s0, s1, s2, s3, neumann_o, load_s, rho_s, sem, far_sem
):
    at = Place(place)
    copies = [
        pltpu.make_async_copy(source, target, sem.at[n])
        for n, (source, target) in enumerate(((order, order_o), (load, load_s), (rho, rho_s)))
    ]
    for copy in copies:
        copy.start()
    ahead = begin(neumann, neumann_o, far_sem, 4)
    copies[0].wait()
    hots = one_hot_faces(order_o[...])
    copies[1].wait()
    copies[2].wait()
    pad = jnp.zeros((7, rho_s.shape[1]), F32)
    full = to_shared(jnp.concatenate([load_s[...], rho_s[...], pad], axis=0), hots)
    shared_o[...] = full
    put_sends((s0, s1, s2, s3), full, at)
    finish(ahead)


def k_neumann(order, neumann_s, lists, couple, neumann_o, avg_o, couple_o, lists_s, sem):
    listed = pltpu.make_async_copy(lists, lists_s, sem.at[4])
    listed.start()
    ahead = begin(couple, couple_o, sem, 4)
    hots = one_hot_faces(order[...])
    points = order.shape[1]
    listed.wait()
    named = lists_s[...]
    position = lax.broadcasted_iota(jnp.int32, (8, points), 1)
    total = jnp.zeros((8, points), F32)
    length = named.shape[1]
    for item in range(length):
        total = total + jnp.where(named[:, item : item + 1] == position, 1.0, 0.0)
    avg_o[...] = to_shared(total * (1.0 / length), hots)
    for f in range(4):
        rows = slice(f * LANES, (f + 1) * LANES)
        for n, piece in enumerate(cut(neumann_s[rows, :], PIECES)):
            half = narrow(hots[f], piece).astype(BF16)
            neumann_o[n, rows, :] = jnp.concatenate(
                [narrow(part, hot, True) for part, hot in zip(faces_of(half), hots)], axis=1
            ).astype(BF16)
    finish(ahead)


def k_couple(
    order, after, couple_s, diag, blocks, row_coarse, lower, upper,
    diag_o, couple_o, blocks_o, coefs_o,
    diag_s, blocks_s, rows_s, lower_s, upper_s, sem,
):
    copies = [None] * 4
    copies.append(pltpu.make_async_copy(blocks, blocks_s, sem.at[4]))
    copies.append(pltpu.make_async_copy(diag, diag_s, sem.at[5]))
    copies.append(pltpu.make_async_copy(row_coarse, rows_s, sem.at[6]))
    copies.append(pltpu.make_async_copy(lower, lower_s, sem.at[7]))
    copies.append(pltpu.make_async_copy(upper, upper_s, sem.at[8]))
    for copy in copies[4:]:
        copy.start()
    hots = one_hot_faces(order[...])
    copies[5].wait()
    diag_o[...] = to_shared(jnp.broadcast_to(diag_s[...], (8, diag_s.shape[1])), hots)[:1]
    for f in range(4):
        rows = slice(f * LANES, (f + 1) * LANES)
        for n, piece in enumerate(cut(couple_s[rows, :], PIECES)):
            couple_o[n, rows, :] = narrow(hots[f], piece).astype(BF16)
    copies[4].wait()
    for f in range(4):
        for n, piece in enumerate(cut(blocks_s[f], PIECES)):
            blocks_o[n, f] = piece
    for n in (6, 7, 8):
        copies[n].wait()
    count = lower_s.shape[1]
    lane = lax.broadcasted_iota(jnp.int32, (count, LANES), 1)
    eye = lax.broadcasted_iota(jnp.int32, (count, count), 0) == lax.broadcasted_iota(
        jnp.int32, (count, count), 1
    )
    tile = jnp.zeros((count, LANES), F32)
    for n in range(count):
        tile = tile + jnp.where(lane == 112 + n, rows_s[:, n : n + 1], 0.0)
    for n, ref in ((120, lower_s), (121, upper_s)):
        column = jnp.sum(
            jnp.where(eye, jnp.broadcast_to(ref[...], (count, count)), 0.0), axis=1, keepdims=True
        )
        tile = tile + jnp.where(lane == n, column, 0.0)
    coefs_o[0:24, :] = jnp.zeros((24, LANES), F32)
    coefs_o[24:32, :] = tile


def k_first(place, shared, g0, g1, g2, g3, neumann, avg, r_o, share_o, prim_o, t_o, *sends):
    at = Place(place)
    rhs = r_o.shape[0]
    full = assembled(shared[...], (g0, g1, g2, g3), at, shared.shape[0], keep=False)
    share = shared[rhs : rhs + 1, :] / full[rhs : rhs + 1]
    south, north, west, east = faces_of(full[:rhs])
    r = jnp.concatenate([south * at.keep_south, north * at.keep_north, west, east], axis=1)
    r_o[...] = r
    share_o[...] = share
    weighted = share * r
    prim_o[...] = mm_t(avg[...], weighted)
    t = jnp.concatenate([share * product(weighted, held(neumann)), share * avg[...]], axis=0)
    t_o[...] = t
    put_sends(sends, t, at)


def k_schur(
    place, t, g0, g1, g2, g3, diag, couple, blocks, z_o, q_o, s0, s1, s2, s3, z_s, sem, *, rhs
):
    at = Place(place)
    z = assembled(t[...], (g0, g1, g2, g3), at, rhs)
    z_s[...] = z
    copy = pltpu.make_async_copy(z_s, z_o, sem.at[0])
    copy.start()
    q = schur(z, diag[...], held(couple), held(blocks))
    q_o[...] = q
    put_sends((s0, s1, s2, s3), q, at)
    copy.wait()


def k_second(place, q, g0, g1, g2, g3, r, share, neumann, avg, v_o, t_o, pr_o, *sends):
    at = Place(place)
    rhs = r.shape[0]
    w = assembled(q[...], (g0, g1, g2, g3), at, rhs)
    v = jnp.concatenate([w[:rhs] - SHIFT * r[...], w[rhs:]], axis=0)
    v_o[...] = v
    weighted = share[...] * v
    pr_o[...] = jnp.concatenate(
        [mm_t(avg[...], weighted[:rhs]), mm_t(avg[...], weighted[rhs:])], axis=1
    )
    t = share[...] * product(weighted, held(neumann))
    t_o[...] = t
    put_sends(sends, t, at)


def k_third(place, q, g0, g1, g2, g3, v, share, avg, prim0, prim1, v2_o, pay_o, v2_s, sem):
    at = Place(place)
    rhs = prim0.shape[1]
    w = assembled(q[...], (g0, g1, g2, g3), at, rhs)
    zero = jnp.zeros((16, w.shape[1]), F32)
    older = jnp.concatenate([v[...][:rhs], zero, v[...][rhs:], zero], axis=0)
    v2 = w - SHIFT * older
    v2_s[...] = v2
    copies = begin(v2_s, v2_o, sem, 4)
    weighted = share[...] * v2
    prim2 = mm_t(avg[...], weighted[:rhs])
    reach2 = mm_t(avg[...], weighted[rhs:])
    reach1 = prim1[...][:, rhs:]
    spare = jnp.zeros((8, LANES - reach1.shape[1] - reach2.shape[1]), F32)
    tail = jnp.concatenate([reach1, reach2, spare], axis=1)
    pay = jnp.concatenate([prim0[...], prim1[...][:, :rhs], prim2, tail], axis=0)
    for item in range(pay_o.shape[0]):
        pay_o[item] = pay
    finish(copies)


def summed(got):
    total = got[0]
    for item in range(1, got.shape[0]):
        total = total + got[item]
    return total


def k_sum_spread(got, coefs, out):
    total = summed(got) + coefs[...]
    for item in range(out.shape[0]):
        out[item] = total


def banded_product(pieces, value):
    first, second = cut(value, 2)
    return (narrow(pieces[1], first) + narrow(pieces[0], second)) + narrow(pieces[0], first)


def coarse_rows(totals, lowers, uppers):
    carry = jnp.zeros_like(totals[0])
    smooth = []
    for low, value in zip(lowers, [(1.0 - low) * value for low, value in zip(lowers, totals)]):
        carry = low * carry + value
        smooth.append(carry)
    carry = jnp.zeros_like(totals[0])
    tops = []
    smooth = [(1.0 - up) * value for up, value in zip(uppers, smooth)]
    for up, value in zip(uppers[::-1], smooth[::-1]):
        carry = up * carry + value
        tops.append(carry)
    return tops[::-1]


def k_fourth(place, v2, share, neumann, t_o, s0, s1, s2, s3, v2_s, t_s, sem):
    at = Place(place)
    finish(begin(v2, v2_s, sem.at[0], 4))
    t = share[...] * product(share[...] * v2_s[...], held(neumann))
    t_s[...] = t
    copies = begin(t_s, t_o, sem.at[1], 4)
    put_sends((s0, s1, s2, s3), t, at)
    finish(copies)


def lift(coefs, basis):
    spare = -coefs.shape[0] % 16
    if spare:
        coefs = jnp.concatenate([coefs, jnp.zeros((spare, coefs.shape[1]), F32)], axis=0)
        basis = jnp.concatenate([basis, jnp.zeros((spare, basis.shape[1]), F32)], axis=0)
    c, b = cut(coefs, 2), cut(basis, 2)

    def times(x, y):
        return lax.dot_general(x, y, (((0,), (0,)), ((), ())), preferred_element_type=F32)

    return (times(c[1], b[0]) + times(c[0], b[1])) + times(c[0], b[0])


def k_core(
    place, mine, other, t, g0, g1, g2, g3, z0, v1, z1, v2, r, diag, couple, blocks,
    z0_o, z1_o, z2_o, w0_o, w1_o, q_o, pay_o, s0, s1, s2, s3,
    band0, band1, band2, c0_s, c1_s, c2_s, full_s, t_s, z0_s, z1_s, v2_s, sem, in_sem,
):
    at = Place(place)
    loads = []
    for n, (source, target) in enumerate(((z0, z0_s), (z1, z1_s), (v2, v2_s), (t, t_s))):
        loads += begin(source, target, in_sem.at[n], 2)
    t, z0, z1, v2 = t_s, z0_s, z1_s, v2_s
    rhs = r.shape[0]
    rows = 2 * mine.shape[0]
    width = band0.shape[1]
    lane = lax.broadcasted_iota(jnp.int32, (8, width), 1)
    lowers, uppers = [], []
    for ref in (band0, band1, band2):
        if ref.shape[0] > rows * 8:
            ref[rows * 8 :, :] = jnp.zeros((ref.shape[0] - rows * 8, width), F32)
    pays = []
    for k in range(rows // 2):
        pays.append(jnp.where(at.even_row, mine[k], other[k]))
        pays.append(jnp.where(at.even_row, other[k], mine[k]))
    for k in range(rows):
        tail = pays[k][24:32]
        lowers.append(jnp.broadcast_to(tail[:, 120:121], (8, rhs)))
        uppers.append(jnp.broadcast_to(tail[:, 121:122], (8, rhs)))
        wide = tail
        if width > LANES:
            wide = jnp.concatenate([tail, jnp.zeros((8, width - LANES), F32)], axis=1)
        for ref, first, last, to in (
            (band1, 0, 40, 8 * (k - 2)),
            (band2, 40, 112, 8 * (k - 4)),
            (band0, 112, 120, 8 * k),
        ):
            picked = jnp.where((lane >= first) & (lane < last), wide, 0.0)
            ref[8 * k : 8 * k + 8, :] = pltpu.roll(picked, (to - first) % width, 1)

    def stacked(tiles):
        if width > rows * 8:
            tiles = tiles + [jnp.zeros((width - rows * 8, rhs), F32)]
        return jnp.concatenate(tiles, axis=0)

    own, near, wide = [cut(ref[...], 2) for ref in (band0, band1, band2)]

    def solve(total):
        tiles = [total[8 * k : 8 * k + 8] for k in range(rows)]
        return stacked(coarse_rows(tiles, lowers, uppers)) + banded_product(own, total)

    edge = jnp.zeros((40, rhs), F32)
    c0 = solve(stacked([part[0:8] for part in pays]))
    c1 = solve(stacked([part[8:16] for part in pays]) + banded_product(near, c0))
    c2 = solve(
        stacked([part[16:24] for part in pays])
        + banded_product(wide, c0)
        + banded_product(near, c1)
    )
    for ref, value in ((c0_s, c0), (c1_s, c1), (c2_s, c2)):
        ref[0:40, :] = edge
        ref[40 : 40 + width, :] = value
        ref[40 + width :, :] = edge
    start = at.row * 8
    c0 = c0_s[pl.ds(pl.multiple_of(start, 8), 88), :]
    c1 = c1_s[pl.ds(pl.multiple_of(start + 16, 8), 56), :]
    c2 = c2_s[pl.ds(pl.multiple_of(start + 32, 8), 24), :]
    r0 = r[...]
    finish(loads[0:2])
    z0f = z0[:rhs, :] + lift(c0[32:56], z0[rhs:, :])
    v1f = v1[:rhs, :] + lift(c0[24:64], v1[rhs:, :])
    finish(loads[2:4])
    z1f = z1[:rhs, :] + lift(
        jnp.concatenate([c0[16:72], c1[16:40]], axis=0),
        jnp.concatenate([z1[rhs:, :], z0[rhs:, :]], axis=0),
    )
    finish(loads[4:6])
    v2f = v2[:rhs, :] + lift(
        jnp.concatenate([c0[8:80], c1[8:48]], axis=0),
        jnp.concatenate([v2[rhs:, :], v1[rhs:, :]], axis=0),
    )
    copies = []

    def keep(n, value, out):
        full_s[n] = value
        copies.extend(begin(full_s.at[n], out, sem.at[n], 2))

    keep(0, z0f, z0_o)
    keep(1, z1f, z1_o)
    keep(2, v1f + SHIFT * r0, w0_o)
    keep(3, v2f + SHIFT * v1f, w1_o)
    finish(loads[6:8])
    z2 = assembled(t[...], (g0, g1, g2, g3), at, rhs)
    z2f = z2[:rhs] + lift(
        jnp.concatenate([c0, c1, c2], axis=0),
        jnp.concatenate([z2[rhs:], z1[rhs:, :], z0[rhs:, :]], axis=0),
    )
    keep(4, z2f, z2_o)
    q = schur(z2f, diag[...], held(couple), held(blocks))
    q_o[...] = q
    put_sends((s0, s1, s2, s3), q, at)
    table = dot_rows(
        [(r0, z0f), (r0, z1f), (v1f, z0f), (v1f, z1f), (v2f, z1f)]
        + [(r0, z2f), (v1f, z2f), (v2f, z2f), (z2f, q + q)]
    )
    line = jnp.concatenate([table[i : i + 1] for i in range(9)], axis=1)
    for item in range(pay_o.shape[0]):
        pay_o[item] = line
    finish(copies)


def dot_rows(pairs):
    parts = []
    for a, b in pairs:
        faces = faces_of(a * b)
        parts.append((faces[0] + faces[1]) + (faces[2] + faces[3]))
    wide = jnp.concatenate(parts, axis=1)
    shape = (16, wide.shape[1])
    pick = jnp.where(
        lax.broadcasted_iota(jnp.int32, shape, 0) == lax.broadcasted_iota(jnp.int32, shape, 1) // LANES,
        1.0,
        0.0,
    ).astype(BF16)
    high, middle, low = [narrow(pick, piece, True) for piece in cut(wide, 3)]
    return (low + middle) + high


def k_final(
    place, got, q, g0, g1, g2, g3, order, r0, z0, z1, z2, w0, w1, x_o, r_o, full_s, sem
):
    loads = []
    for n, source in enumerate((z0, z1, z2, w0, w1)):
        loads += begin(source, full_s.at[n], sem.at[n], 2)
    w2 = assembled(q[...], (g0, g1, g2, g3), Place(place), q.shape[0])
    total = summed(got)
    v0z0, v0z1, v1z0, v1z1, v2z1, v0z2, v1z2, v2z2, z2w2 = [
        total[:, i * LANES : (i + 1) * LANES] for i in range(9)
    ]
    z1w0 = v1z1 + SHIFT * v0z1
    z2w0 = v1z2 + SHIFT * v0z2
    z2w1 = v2z2 + SHIFT * v1z2
    zw = [
        [v1z0 + SHIFT * v0z0, z1w0, z2w0],
        [z1w0, v2z1 + SHIFT * v1z1, z2w1],
        [z2w0, z2w1, z2w2],
    ]
    vz = [[v0z0, v0z1, v0z2], [v1z0, v1z1, v1z2], [z1w0 - SHIFT * v1z0, v2z1, v2z2]]

    def form(left, table, right):
        value = None
        for i, a in enumerate(left):
            for j, b in enumerate(right):
                if a is None or b is None:
                    continue
                term = a * table[i][j] * b
                value = term if value is None else value + term
        return value

    one = jnp.ones_like(vz[0][0])
    zero = jnp.zeros_like(one)
    toward = [one, None, None]
    steps = [zero, zero, zero]
    drops = [zero, zero, zero]
    rz = vz[0][0]
    for iteration in range(3):
        alpha = rz / form(toward, zw, toward)
        for j in range(3):
            if toward[j] is not None:
                steps[j] = steps[j] + alpha * toward[j]
                drops[j] = drops[j] - alpha * toward[j]
        if iteration < 2:
            mix = [one + SHIFT * drops[0], drops[0] + SHIFT * drops[1], None]
            if iteration == 1:
                mix[2] = drops[1]
            new = form(mix, vz, mix)
            beta = new / rz
            toward = [
                m if d is None else (beta * d if m is None else m + beta * d)
                for m, d in zip(mix, toward)
            ]
            rz = new
    table = jnp.concatenate(steps + drops + [zero, zero], axis=0)
    eye = jnp.where(
        lax.broadcasted_iota(jnp.int32, (LANES, LANES), 0)
        == lax.broadcasted_iota(jnp.int32, (LANES, LANES), 1),
        1.0,
        0.0,
    ).astype(F32)
    columns = mm_t(eye, table)
    col = [columns[:, i : i + 1] for i in range(6)]
    hots = one_hot_faces(order[...])
    finish(loads[:6])
    x = col[0] * full_s[0] + col[1] * full_s[1] + col[2] * full_s[2]
    x_o[...] = to_points(x, hots)
    finish(loads[6:])
    r = r0[...] + col[3] * full_s[3] + col[4] * full_s[4] + col[5] * w2
    r_o[...] = to_points(r, hots)


def call(body, outs, place, *args, scratch=(), raw=(), raw_outs=(), flops=1_000_000):
    args = tuple(
        pltpu.with_memory_space_constraint(arg, pltpu.HBM) if n in raw else arg
        for n, arg in enumerate(args)
    )
    space = [pltpu.HBM if n in raw else pltpu.VMEM for n in range(len(args))]
    specs = [pl.BlockSpec(memory_space=kind) for kind in space]
    if place is not None:
        specs = [pl.BlockSpec(memory_space=pltpu.SMEM)] + specs
        args = (place,) + args
    return pl.pallas_call(
        body,
        out_shape=[
            out
            if isinstance(out, jax.ShapeDtypeStruct)
            else (pltpu.HBM(out, F32) if n in raw_outs else jax.ShapeDtypeStruct(out, F32))
            for n, out in enumerate(outs)
        ],
        in_specs=specs,
        out_specs=[
            pl.BlockSpec(memory_space=pltpu.HBM if n in raw_outs else pltpu.VMEM)
            for n in range(len(outs))
        ],
        scratch_shapes=list(scratch),
        compiler_params=pltpu.CompilerParams(vmem_limit_bytes=16 * 1024 * 1024),
        cost_estimate=pl.CostEstimate(flops=flops, bytes_accessed=1_000_000, transcendentals=0),
    )(*args)


def exchange_columns(sends, columns):
    near = [(i, i ^ 1) for i in range(columns)]
    far = [(i, (i + 1 if i % 2 else i - 1) % columns) for i in range(columns)]
    return [lax.ppermute(sends[0], "circ", far), lax.ppermute(sends[1], "circ", near)]


def exchange_rows(sends, rows):
    core = [(i, i ^ 1) for i in range(rows)]
    link = [(i, i + 1 if i % 2 else i - 1) for i in range(1, rows - 1)]
    return [lax.ppermute(sends[2], "axial", link), lax.ppermute(sends[3], "axial", core)]


def exchange(sends, rows, columns):
    return exchange_columns(sends, columns) + exchange_rows(sends, rows)


def spread(value, axis, groups=None):
    return lax.all_to_all(
        value, axis, split_axis=0, concat_axis=0, tiled=True, axis_index_groups=groups
    )


def local(
    load_terms, diffusivity, interface_diag, coupling, interior_inverse, neumann_solve,
    row_coarse, lower_coef, upper_coef, face_order, primal_lists,
):
    rows, columns = lax.axis_size("axial"), lax.axis_size("circ")
    rhs, points = load_terms.shape[2], load_terms.shape[3]
    place = jnp.stack(
        [lax.axis_index("axial"), jnp.int32(rows), lax.axis_index("circ")]
    ).astype(jnp.int32)
    swap = functools.partial(exchange, rows=rows, columns=columns)
    dma = pltpu.SemaphoreType.DMA

    def face(n):
        return [(n, LANES)] * 4

    def bf16(*shape):
        return jax.ShapeDtypeStruct((PIECES,) + shape, BF16)

    shared, order, *sends, neumann = call(
        k_prepare,
        [(rhs + 8, points), jax.ShapeDtypeStruct((1, points), jnp.int32)]
        + face(rhs + 8)
        + [(points, points)],
        place, load_terms[0, 0], diffusivity[0], face_order[0], neumann_solve[0, 0],
        raw=(0, 1, 2, 3),
        scratch=[
            pltpu.VMEM((rhs, points), F32),
            pltpu.VMEM((1, points), F32),
            dma((3,)),
            dma((4,)),
        ],
    )
    got = swap(sends)
    neumann, avg, couple = call(
        k_neumann,
        [bf16(points, points), (8, points), (points, points)],
        None, order, neumann, primal_lists[0, 0], coupling[0, 0],
        raw=(2, 3),
        scratch=[
            pltpu.VMEM(primal_lists.shape[2:], jnp.int32),
            dma((5,)),
        ],
        flops=2_000_000_000,
    )
    r0, share, prim0, t0, *sends = call(
        k_first,
        [(rhs, points), (1, points), (8, rhs), (rhs + 8, points)] + face(rhs + 8),
        place, shared, *got, neumann, avg,
    )
    got = swap(sends)
    inner = interior_inverse.shape[2:]
    diag, couple, blocks, coefs = call(
        k_couple,
        [(1, points), bf16(points, points), bf16(*inner), (32, LANES)],
        None, order, share, couple, interface_diag[0], interior_inverse[0, 0],
        row_coarse[0], lower_coef, upper_coef,
        raw=(3, 4, 5, 6, 7),
        scratch=[
            pltpu.VMEM((1, points), F32),
            pltpu.VMEM(inner, F32),
            pltpu.VMEM(row_coarse.shape[1:], F32),
            pltpu.VMEM(lower_coef.shape, F32),
            pltpu.VMEM(upper_coef.shape, F32),
            dma((9,)),
        ],
        flops=2_000_000_000,
    )
    n = rhs + 24
    z0, q0, *sends = call(
        functools.partial(k_schur, rhs=rhs), [(n, points)] * 2 + face(n),
        place, t0, *got, diag, couple, blocks,
        raw_outs=(0,), scratch=[pltpu.VMEM((n, points), F32), dma((1,))],
    )
    got = swap(sends)
    n = rhs + 40
    v1, t1, prim1, *sends = call(
        k_second, [(n, points)] * 2 + [(8, n)] + face(n), place, q0, *got, r0, share, neumann, avg
    )
    got = swap(sends)
    n = rhs + 56
    z1, q1, *sends = call(
        functools.partial(k_schur, rhs=rhs), [(n, points)] * 2 + face(n),
        place, t1, *got, diag, couple, blocks,
        raw_outs=(0,), scratch=[pltpu.VMEM((n, points), F32), dma((1,))],
    )
    got = swap(sends)
    n = rhs + 72
    v2, pay = call(
        k_third, [(n, points), (columns, 32, LANES)], place, q1, *got, v1, share, avg, prim0, prim1,
        raw_outs=(0,), scratch=[pltpu.VMEM((n, points), F32), dma((4,))],
    )
    got = spread(pay, "circ")
    t2, *sends = call(
        k_fourth, [(n, points)] + face(n), place, v2, share, neumann,
        raw=(0,), raw_outs=(0,),
        scratch=[pltpu.VMEM((n, points), F32)] * 2 + [dma((2, 4))],
        flops=500_000_000,
    )
    got, t2 = lax.optimization_barrier((got, t2))
    (pay,) = call(k_sum_spread, [(rows // 2, 32, LANES)], None, got, coefs)
    pay, *sends = lax.optimization_barrier((pay, *sends))
    along = [list(range(core, rows, 2)) for core in range(2)]
    mine = spread(pay, "axial", along)
    mine, *got = lax.optimization_barrier((mine, *swap(sends)))
    other = lax.ppermute(mine, "axial", [(i, i ^ 1) for i in range(rows)])
    width = max(LANES, 8 * rows)
    z0f, z1f, z2f, w0f, w1f, q2, pay, *sends = call(
        k_core,
        [(rhs, points)] * 6 + [(2 * columns, 1, 9 * LANES)] + face(rhs),
        place, mine, other, t2, *got, z0, v1, z1, v2, r0, diag, couple, blocks,
        raw=(2, 7, 9, 10),
        raw_outs=(0, 1, 2, 3, 4),
        scratch=[pltpu.VMEM((width, width), F32)] * 3
        + [pltpu.VMEM((width + 80, rhs), F32)] * 3
        + [pltpu.VMEM((5, rhs, points), F32)]
        + [pltpu.VMEM((rhs + m, points), F32) for m in (72, 24, 56, 72)]
        + [dma((5, 2)), dma((4, 2))],
    )
    chips = [
        [row * columns + column for row in (pair, pair + 1) for column in range(columns)]
        for pair in range(0, rows, 2)
    ]
    dots = spread(pay, ("axial", "circ"), chips)
    got = exchange_columns(sends, columns)
    dots, *got = lax.optimization_barrier((dots, *got))
    blank = jnp.zeros((1, 9 * LANES), F32)
    (pay,) = call(k_sum_spread, [(rows // 2, 1, 9 * LANES)], None, dots, blank)
    pay, *sends = lax.optimization_barrier((pay, *sends))
    dots = spread(pay, "axial", along)
    got = got + exchange_rows(sends, rows)
    x, r = call(
        k_final, [(rhs, points)] * 2,
        place, dots, q2, *got, order, r0, z0f, z1f, z2f, w0f, w1f,
        raw=(8, 9, 10, 11, 12),
        scratch=[pltpu.VMEM((5, rhs, points), F32), dma((5, 2))],
    )
    return (x[None, None], r[None, None])


def solution(mesh):
    in_specs = (
        P("axial", "circ", None, None),
        P("axial", "circ", None),
        P("axial", "circ", None),
        P("axial", "circ", None, None),
        P("axial", "circ", None, None, None),
        P("axial", "circ", None, None),
        P("axial", None, None),
        P("axial", None),
        P("axial", None),
        P("axial", "circ", None),
        P("axial", "circ", None, None),
    )
    out_specs = (P("axial", "circ", None, None), P("axial", "circ", None, None))
    return jax.shard_map(local, mesh=mesh, in_specs=in_specs, out_specs=out_specs, check_vma=False)
```

```python
import functools

import jax
import jax.numpy as jnp
from jax import lax
from jax.experimental import pallas as pl
from jax.experimental.pallas import tpu as pltpu
from jax.sharding import PartitionSpec as P

SHIFT = 12.0
HIGHEST = lax.Precision.HIGHEST
F32 = jnp.float32
BF16 = jnp.bfloat16
LANES = 128
PIECES = 2


def mm_t(a, b):
    return lax.dot_general(
        a, b, (((1,), (1,)), ((), ())), precision=HIGHEST, preferred_element_type=F32
    )


def cut(value, count):
    pieces = []
    for _ in range(count):
        piece = value.astype(BF16)
        pieces.append(piece)
        value = value - piece.astype(F32)
    return pieces


def narrow(a, b, transposed=False):
    return lax.dot_general(
        a, b, (((1,), (1 if transposed else 0,)), ((), ())), preferred_element_type=F32
    )


def product(a, pieces, transposed=False):
    count = a.shape[0]
    levels = len(pieces)
    if count % 16:
        a = jnp.concatenate([a, jnp.zeros((16 - count % 16, a.shape[1]), F32)], axis=0)
    tall = a.shape[0]
    left = cut(a, levels)
    by_level = [None] * levels
    for n, piece in enumerate(pieces):
        used = left[: levels - n]
        stack = used[0] if len(used) == 1 else jnp.concatenate(used, axis=0)
        out = narrow(stack, piece, transposed)
        for m in range(len(used)):
            part = out[m * tall : (m + 1) * tall]
            level = n + m
            by_level[level] = part if by_level[level] is None else by_level[level] + part
    total = by_level[-1]
    for part in by_level[-2::-1]:
        total = total + part
    return total[:count]


def select_columns(a, hot, transposed):
    count = a.shape[0]
    if count % 16:
        a = jnp.concatenate([a, jnp.zeros((16 - count % 16, a.shape[1]), F32)], axis=0)
    tall = a.shape[0]
    out = narrow(jnp.concatenate(cut(a, 3), axis=0), hot, transposed)
    return ((out[2 * tall :] + out[tall : 2 * tall]) + out[:tall])[:count]


def faces_of(full):
    return [full[:, f * LANES : (f + 1) * LANES] for f in range(4)]


def one_hot_faces(order):
    rows = lax.broadcasted_iota(jnp.int32, (LANES, LANES), 0)
    return [
        jnp.where(order[:, f * LANES : (f + 1) * LANES] - f * LANES == rows, 1.0, 0.0)
        .astype(F32)
        .astype(BF16)
        for f in range(4)
    ]


def to_shared(full, hots):
    return jnp.concatenate(
        [select_columns(part, hot, True) for part, hot in zip(faces_of(full), hots)], axis=1
    )


def to_points(full, hots):
    return jnp.concatenate(
        [select_columns(part, hot, False) for part, hot in zip(faces_of(full), hots)], axis=1
    )


class Place:
    def __init__(self, place):
        row, rows, column = place[0], place[1], place[2]
        self.row = row
        self.even_row = lax.rem(row, 2) == 0
        self.even_column = lax.rem(column, 2) == 0
        self.keep_south = jnp.where(row > 0, 1.0, 0.0).astype(F32)
        self.keep_north = jnp.where(row < rows - 1, 1.0, 0.0).astype(F32)


def put_sends(sends, full, at):
    south, north, west, east = faces_of(full)
    sends[0][...] = jnp.where(at.even_column, west, east)
    sends[1][...] = jnp.where(at.even_column, east, west)
    sends[2][...] = jnp.where(at.even_row, south, north)
    sends[3][...] = jnp.where(at.even_row, north, south)


def neighbours(got, at):
    far, near, link, core = [ref[...] for ref in got]
    above = jnp.where(at.even_row, core, link)
    below = jnp.where(at.even_row, link, core)
    right = jnp.where(at.even_column, near, far)
    left = jnp.where(at.even_column, far, near)
    return below, above, left, right


def assembled(full, got, at, rhs, keep=True):
    count = full.shape[0]
    extra = count - rhs
    own = faces_of(full)
    other = neighbours(got, at)
    scale = (at.keep_south, at.keep_north, None, None)
    shift = (0, 16, 8, 8)
    out = []
    for f in range(4):
        part = own[f][:rhs] + other[f][:rhs]
        if extra:
            zero = jnp.zeros((8, LANES), F32)
            mine = jnp.concatenate([zero, own[f][rhs:], zero], axis=0)
            pieces = [jnp.zeros((shift[f], LANES), F32)] if shift[f] else []
            pieces.append(other[f][rhs:])
            if shift[f] < 16:
                pieces.append(jnp.zeros((16 - shift[f], LANES), F32))
            part = jnp.concatenate([part, mine + jnp.concatenate(pieces, axis=0)], axis=0)
        if keep and scale[f] is not None:
            part = part * scale[f]
        out.append(part)
    return jnp.concatenate(out, axis=1)


def held(ref):
    return [ref[n] for n in range(ref.shape[0])]


def schur(z, diag, couple, blocks):
    inner = product(z, couple)
    solved = jnp.concatenate(
        [
            product(part, [piece[n] for piece in blocks])
            for n, part in enumerate(faces_of(inner))
        ],
        axis=1,
    )
    return diag * z - product(solved, couple, True)


def begin(source, target, sems, parts):
    rows = source.shape[0] // 8
    edges = [8 * (rows * n // parts) for n in range(parts)] + [source.shape[0]]
    copies = []
    for n in range(parts):
        band = pl.ds(edges[n], edges[n + 1] - edges[n])
        copies.append(pltpu.make_async_copy(source.at[band], target.at[band], sems.at[n]))
        copies[n].start()
    return copies


def finish(copies):
    for copy in copies:
        copy.wait()


def k_prepare(
    place, load, rho, order, neumann, shared_o, order_o, s0, s1, s2, s3, neumann_o, load_s, rho_s, sem, far_sem
):
    at = Place(place)
    copies = [
        pltpu.make_async_copy(source, target, sem.at[n])
        for n, (source, target) in enumerate(((order, order_o), (load, load_s), (rho, rho_s)))
    ]
    for copy in copies:
        copy.start()
    ahead = begin(neumann, neumann_o, far_sem, 4)
    copies[0].wait()
    hots = one_hot_faces(order_o[...])
    copies[1].wait()
    copies[2].wait()
    pad = jnp.zeros((7, rho_s.shape[1]), F32)
    full = to_shared(jnp.concatenate([load_s[...], rho_s[...], pad], axis=0), hots)
    shared_o[...] = full
    put_sends((s0, s1, s2, s3), full, at)
    finish(ahead)


def k_neumann(order, neumann_s, lists, couple, neumann_o, avg_o, couple_o, lists_s, sem):
    listed = pltpu.make_async_copy(lists, lists_s, sem.at[4])
    listed.start()
    ahead = begin(couple, couple_o, sem, 4)
    hots = one_hot_faces(order[...])
    points = order.shape[1]
    listed.wait()
    named = lists_s[...]
    position = lax.broadcasted_iota(jnp.int32, (8, points), 1)
    total = jnp.zeros((8, points), F32)
    length = named.shape[1]
    for item in range(length):
        total = total + jnp.where(named[:, item : item + 1] == position, 1.0, 0.0)
    avg_o[...] = to_shared(total * (1.0 / length), hots)
    for f in range(4):
        rows = slice(f * LANES, (f + 1) * LANES)
        for n, piece in enumerate(cut(neumann_s[rows, :], PIECES)):
            half = narrow(hots[f], piece).astype(BF16)
            neumann_o[n, rows, :] = jnp.concatenate(
                [narrow(part, hot, True) for part, hot in zip(faces_of(half), hots)], axis=1
            ).astype(BF16)
    finish(ahead)


def k_couple(
    order, after, couple_s, diag, blocks, row_coarse, lower, upper,
    diag_o, couple_o, blocks_o, coefs_o,
    diag_s, blocks_s, rows_s, lower_s, upper_s, sem,
):
    copies = [None] * 4
    copies.append(pltpu.make_async_copy(blocks, blocks_s, sem.at[4]))
    copies.append(pltpu.make_async_copy(diag, diag_s, sem.at[5]))
    copies.append(pltpu.make_async_copy(row_coarse, rows_s, sem.at[6]))
    copies.append(pltpu.make_async_copy(lower, lower_s, sem.at[7]))
    copies.append(pltpu.make_async_copy(upper, upper_s, sem.at[8]))
    for copy in copies[4:]:
        copy.start()
    hots = one_hot_faces(order[...])
    copies[5].wait()
    diag_o[...] = to_shared(jnp.broadcast_to(diag_s[...], (8, diag_s.shape[1])), hots)[:1]
    for f in range(4):
        rows = slice(f * LANES, (f + 1) * LANES)
        for n, piece in enumerate(cut(couple_s[rows, :], PIECES)):
            couple_o[n, rows, :] = narrow(hots[f], piece).astype(BF16)
    copies[4].wait()
    for f in range(4):
        for n, piece in enumerate(cut(blocks_s[f], PIECES)):
            blocks_o[n, f] = piece
    for n in (6, 7, 8):
        copies[n].wait()
    count = lower_s.shape[1]
    lane = lax.broadcasted_iota(jnp.int32, (count, LANES), 1)
    eye = lax.broadcasted_iota(jnp.int32, (count, count), 0) == lax.broadcasted_iota(
        jnp.int32, (count, count), 1
    )
    tile = jnp.zeros((count, LANES), F32)
    for n in range(count):
        tile = tile + jnp.where(lane == 112 + n, rows_s[:, n : n + 1], 0.0)
    for n, ref in ((120, lower_s), (121, upper_s)):
        column = jnp.sum(
            jnp.where(eye, jnp.broadcast_to(ref[...], (count, count)), 0.0), axis=1, keepdims=True
        )
        tile = tile + jnp.where(lane == n, column, 0.0)
    coefs_o[0:24, :] = jnp.zeros((24, LANES), F32)
    coefs_o[24:32, :] = tile


def k_first(place, shared, g0, g1, g2, g3, neumann, avg, r_o, share_o, prim_o, t_o, *sends):
    at = Place(place)
    rhs = r_o.shape[0]
    full = assembled(shared[...], (g0, g1, g2, g3), at, shared.shape[0], keep=False)
    share = shared[rhs : rhs + 1, :] / full[rhs : rhs + 1]
    south, north, west, east = faces_of(full[:rhs])
    r = jnp.concatenate([south * at.keep_south, north * at.keep_north, west, east], axis=1)
    r_o[...] = r
    share_o[...] = share
    weighted = share * r
    prim_o[...] = mm_t(avg[...], weighted)
    t = jnp.concatenate([share * product(weighted, held(neumann)), share * avg[...]], axis=0)
    t_o[...] = t
    put_sends(sends, t, at)


def k_schur(
    place, t, g0, g1, g2, g3, diag, couple, blocks, z_o, q_o, s0, s1, s2, s3, z_s, sem, *, rhs
):
    at = Place(place)
    z = assembled(t[...], (g0, g1, g2, g3), at, rhs)
    z_s[...] = z
    copy = pltpu.make_async_copy(z_s, z_o, sem.at[0])
    copy.start()
    q = schur(z, diag[...], held(couple), held(blocks))
    q_o[...] = q
    put_sends((s0, s1, s2, s3), q, at)
    copy.wait()


def k_second(place, q, g2, g3, g0, g1, r, share, neumann, avg, v_o, t_o, pr_o, *sends):
    at = Place(place)
    rhs = r.shape[0]
    w = assembled(q[...], (g0, g1, g2, g3), at, rhs)
    v = jnp.concatenate([w[:rhs] - SHIFT * r[...], w[rhs:]], axis=0)
    v_o[...] = v
    weighted = share[...] * v
    pr_o[...] = jnp.concatenate(
        [mm_t(avg[...], weighted[:rhs]), mm_t(avg[...], weighted[rhs:])], axis=1
    )
    t = share[...] * product(weighted, held(neumann))
    t_o[...] = t
    put_sends(sends, t, at)


def k_third(place, q, g0, g1, g2, g3, v, share, avg, prim0, prim1, v2_o, pay_o, v2_s, sem):
    at = Place(place)
    rhs = prim0.shape[1]
    w = assembled(q[...], (g0, g1, g2, g3), at, rhs)
    zero = jnp.zeros((16, w.shape[1]), F32)
    older = jnp.concatenate([v[...][:rhs], zero, v[...][rhs:], zero], axis=0)
    v2 = w - SHIFT * older
    v2_s[...] = v2
    copies = begin(v2_s, v2_o, sem, 4)
    weighted = share[...] * v2
    prim2 = mm_t(avg[...], weighted[:rhs])
    reach2 = mm_t(avg[...], weighted[rhs:])
    reach1 = prim1[...][:, rhs:]
    spare = jnp.zeros((8, LANES - reach1.shape[1] - reach2.shape[1]), F32)
    tail = jnp.concatenate([reach1, reach2, spare], axis=1)
    pay = jnp.concatenate([prim0[...], prim1[...][:, :rhs], prim2, tail], axis=0)
    for item in range(pay_o.shape[0]):
        pay_o[item] = pay
    finish(copies)


def summed(got):
    total = got[0]
    for item in range(1, got.shape[0]):
        total = total + got[item]
    return total


def k_sum_spread(got, coefs, out):
    total = summed(got) + coefs[...]
    for item in range(out.shape[0]):
        out[item] = total


def banded_product(pieces, value):
    first, second = cut(value, 2)
    return (narrow(pieces[1], first) + narrow(pieces[0], second)) + narrow(pieces[0], first)


def coarse_rows(totals, lowers, uppers):
    carry = jnp.zeros_like(totals[0])
    smooth = []
    for low, value in zip(lowers, [(1.0 - low) * value for low, value in zip(lowers, totals)]):
        carry = low * carry + value
        smooth.append(carry)
    carry = jnp.zeros_like(totals[0])
    tops = []
    smooth = [(1.0 - up) * value for up, value in zip(uppers, smooth)]
    for up, value in zip(uppers[::-1], smooth[::-1]):
        carry = up * carry + value
        tops.append(carry)
    return tops[::-1]


def k_fourth(place, v2, share, neumann, t_o, s0, s1, s2, s3, v2_s, t_s, sem):
    at = Place(place)
    finish(begin(v2, v2_s, sem.at[0], 4))
    t = share[...] * product(share[...] * v2_s[...], held(neumann))
    t_s[...] = t
    copies = begin(t_s, t_o, sem.at[1], 4)
    put_sends((s0, s1, s2, s3), t, at)
    finish(copies)


def lift(coefs, basis):
    spare = -coefs.shape[0] % 16
    if spare:
        coefs = jnp.concatenate([coefs, jnp.zeros((spare, coefs.shape[1]), F32)], axis=0)
        basis = jnp.concatenate([basis, jnp.zeros((spare, basis.shape[1]), F32)], axis=0)
    c, b = cut(coefs, 2), cut(basis, 2)

    def times(x, y):
        return lax.dot_general(x, y, (((0,), (0,)), ((), ())), preferred_element_type=F32)

    return (times(c[1], b[0]) + times(c[0], b[1])) + times(c[0], b[0])


def k_core(
    place, mine, other, t, g0, g1, g2, g3, z0, v1, z1, v2, r, diag, couple, blocks,
    z0_o, z1_o, z2_o, w0_o, w1_o, q_o, pay_o, s0, s1, s2, s3,
    band0, band1, band2, c0_s, c1_s, c2_s, full_s, t_s, z1_s, v2_s, sem, in_sem,
):
    at = Place(place)
    loads = []
    for n, (source, target) in enumerate(((z1, z1_s), (v2, v2_s), (t, t_s))):
        loads += begin(source, target, in_sem.at[n], 2)
    t, z1, v2 = t_s, z1_s, v2_s
    rhs = r.shape[0]
    rows = 2 * mine.shape[0]
    width = band0.shape[1]
    lane = lax.broadcasted_iota(jnp.int32, (8, width), 1)
    lowers, uppers = [], []
    for ref in (band0, band1, band2):
        if ref.shape[0] > rows * 8:
            ref[rows * 8 :, :] = jnp.zeros((ref.shape[0] - rows * 8, width), F32)
    pays = []
    for k in range(rows // 2):
        pays.append(jnp.where(at.even_row, mine[k], other[k]))
        pays.append(jnp.where(at.even_row, other[k], mine[k]))
    for k in range(rows):
        tail = pays[k][24:32]
        lowers.append(jnp.broadcast_to(tail[:, 120:121], (8, rhs)))
        uppers.append(jnp.broadcast_to(tail[:, 121:122], (8, rhs)))
        wide = tail
        if width > LANES:
            wide = jnp.concatenate([tail, jnp.zeros((8, width - LANES), F32)], axis=1)
        for ref, first, last, to in (
            (band1, 0, 40, 8 * (k - 2)),
            (band2, 40, 112, 8 * (k - 4)),
            (band0, 112, 120, 8 * k),
        ):
            picked = jnp.where((lane >= first) & (lane < last), wide, 0.0)
            ref[8 * k : 8 * k + 8, :] = pltpu.roll(picked, (to - first) % width, 1)

    def stacked(tiles):
        if width > rows * 8:
            tiles = tiles + [jnp.zeros((width - rows * 8, rhs), F32)]
        return jnp.concatenate(tiles, axis=0)

    own, near, wide = [cut(ref[...], 2) for ref in (band0, band1, band2)]

    def solve(total):
        tiles = [total[8 * k : 8 * k + 8] for k in range(rows)]
        return stacked(coarse_rows(tiles, lowers, uppers)) + banded_product(own, total)

    edge = jnp.zeros((40, rhs), F32)
    c0 = solve(stacked([part[0:8] for part in pays]))
    c1 = solve(stacked([part[8:16] for part in pays]) + banded_product(near, c0))
    c2 = solve(
        stacked([part[16:24] for part in pays])
        + banded_product(wide, c0)
        + banded_product(near, c1)
    )
    for ref, value in ((c0_s, c0), (c1_s, c1), (c2_s, c2)):
        ref[0:40, :] = edge
        ref[40 : 40 + width, :] = value
        ref[40 + width :, :] = edge
    start = at.row * 8
    c0 = c0_s[pl.ds(pl.multiple_of(start, 8), 88), :]
    c1 = c1_s[pl.ds(pl.multiple_of(start + 16, 8), 56), :]
    c2 = c2_s[pl.ds(pl.multiple_of(start + 32, 8), 24), :]
    r0 = r[...]
    z0f = z0[:rhs, :] + lift(c0[32:56], z0[rhs:, :])
    v1f = v1[:rhs, :] + lift(c0[24:64], v1[rhs:, :])
    finish(loads[0:2])
    z1f = z1[:rhs, :] + lift(
        jnp.concatenate([c0[16:72], c1[16:40]], axis=0),
        jnp.concatenate([z1[rhs:, :], z0[rhs:, :]], axis=0),
    )
    finish(loads[2:4])
    v2f = v2[:rhs, :] + lift(
        jnp.concatenate([c0[8:80], c1[8:48]], axis=0),
        jnp.concatenate([v2[rhs:, :], v1[rhs:, :]], axis=0),
    )
    copies = []

    def keep(n, value, out):
        full_s[n] = value
        copies.extend(begin(full_s.at[n], out, sem.at[n], 2))

    keep(0, z0f, z0_o)
    keep(1, z1f, z1_o)
    keep(2, v1f + SHIFT * r0, w0_o)
    keep(3, v2f + SHIFT * v1f, w1_o)
    finish(loads[4:6])
    z2 = assembled(t[...], (g0, g1, g2, g3), at, rhs)
    z2f = z2[:rhs] + lift(
        jnp.concatenate([c0, c1, c2], axis=0),
        jnp.concatenate([z2[rhs:], z1[rhs:, :], z0[rhs:, :]], axis=0),
    )
    keep(4, z2f, z2_o)
    q = schur(z2f, diag[...], held(couple), held(blocks))
    q_o[...] = q
    put_sends((s0, s1, s2, s3), q, at)
    table = dot_rows(
        [(r0, z0f), (r0, z1f), (v1f, z0f), (v1f, z1f), (v2f, z1f)]
        + [(r0, z2f), (v1f, z2f), (v2f, z2f), (z2f, q + q)]
    )
    line = jnp.concatenate([table[i : i + 1] for i in range(9)], axis=1)
    for item in range(pay_o.shape[0]):
        pay_o[item] = line
    finish(copies)


def dot_rows(pairs):
    parts = []
    for a, b in pairs:
        faces = faces_of(a * b)
        parts.append((faces[0] + faces[1]) + (faces[2] + faces[3]))
    wide = jnp.concatenate(parts, axis=1)
    shape = (16, wide.shape[1])
    pick = jnp.where(
        lax.broadcasted_iota(jnp.int32, shape, 0) == lax.broadcasted_iota(jnp.int32, shape, 1) // LANES,
        1.0,
        0.0,
    ).astype(BF16)
    high, middle, low = [narrow(pick, piece, True) for piece in cut(wide, 3)]
    return (low + middle) + high


def k_final(
    place, got, q, g0, g1, g2, g3, order, r0, z0, z1, z2, w0, w1, x_o, r_o, full_s, sem
):
    loads = []
    for n, source in enumerate((z2, w0, w1)):
        loads += begin(source, full_s.at[n], sem.at[n], 2)
    w2 = assembled(q[...], (g0, g1, g2, g3), Place(place), q.shape[0])
    total = summed(got)
    v0z0, v0z1, v1z0, v1z1, v2z1, v0z2, v1z2, v2z2, z2w2 = [
        total[:, i * LANES : (i + 1) * LANES] for i in range(9)
    ]
    z1w0 = v1z1 + SHIFT * v0z1
    z2w0 = v1z2 + SHIFT * v0z2
    z2w1 = v2z2 + SHIFT * v1z2
    zw = [
        [v1z0 + SHIFT * v0z0, z1w0, z2w0],
        [z1w0, v2z1 + SHIFT * v1z1, z2w1],
        [z2w0, z2w1, z2w2],
    ]
    vz = [[v0z0, v0z1, v0z2], [v1z0, v1z1, v1z2], [z1w0 - SHIFT * v1z0, v2z1, v2z2]]

    def form(left, table, right):
        value = None
        for i, a in enumerate(left):
            for j, b in enumerate(right):
                if a is None or b is None:
                    continue
                term = a * table[i][j] * b
                value = term if value is None else value + term
        return value

    one = jnp.ones_like(vz[0][0])
    zero = jnp.zeros_like(one)
    toward = [one, None, None]
    steps = [zero, zero, zero]
    drops = [zero, zero, zero]
    rz = vz[0][0]
    for iteration in range(3):
        alpha = rz / form(toward, zw, toward)
        for j in range(3):
            if toward[j] is not None:
                steps[j] = steps[j] + alpha * toward[j]
                drops[j] = drops[j] - alpha * toward[j]
        if iteration < 2:
            mix = [one + SHIFT * drops[0], drops[0] + SHIFT * drops[1], None]
            if iteration == 1:
                mix[2] = drops[1]
            new = form(mix, vz, mix)
            beta = new / rz
            toward = [
                m if d is None else (beta * d if m is None else m + beta * d)
                for m, d in zip(mix, toward)
            ]
            rz = new
    table = jnp.concatenate(steps + drops + [zero, zero], axis=0)
    eye = jnp.where(
        lax.broadcasted_iota(jnp.int32, (LANES, LANES), 0)
        == lax.broadcasted_iota(jnp.int32, (LANES, LANES), 1),
        1.0,
        0.0,
    ).astype(F32)
    columns = mm_t(eye, table)
    col = [columns[:, i : i + 1] for i in range(6)]
    hots = one_hot_faces(order[...])
    finish(loads)
    x = col[0] * z0[...] + col[1] * z1[...] + col[2] * full_s[0]
    r = r0[...] + col[3] * full_s[1] + col[4] * full_s[2] + col[5] * w2
    both = to_points(jnp.concatenate([x, r], axis=0), hots)
    rhs = x.shape[0]
    x_o[...] = both[:rhs]
    r_o[...] = both[rhs:]


def call(body, outs, place, *args, scratch=(), raw=(), raw_outs=(), flops=1_000_000):
    args = tuple(
        pltpu.with_memory_space_constraint(arg, pltpu.HBM) if n in raw else arg
        for n, arg in enumerate(args)
    )
    space = [pltpu.HBM if n in raw else pltpu.VMEM for n in range(len(args))]
    specs = [pl.BlockSpec(memory_space=kind) for kind in space]
    if place is not None:
        specs = [pl.BlockSpec(memory_space=pltpu.SMEM)] + specs
        args = (place,) + args
    return pl.pallas_call(
        body,
        out_shape=[
            out
            if isinstance(out, jax.ShapeDtypeStruct)
            else (pltpu.HBM(out, F32) if n in raw_outs else jax.ShapeDtypeStruct(out, F32))
            for n, out in enumerate(outs)
        ],
        in_specs=specs,
        out_specs=[
            pl.BlockSpec(memory_space=pltpu.HBM if n in raw_outs else pltpu.VMEM)
            for n in range(len(outs))
        ],
        scratch_shapes=list(scratch),
        compiler_params=pltpu.CompilerParams(vmem_limit_bytes=16 * 1024 * 1024),
        cost_estimate=pl.CostEstimate(flops=flops, bytes_accessed=1_000_000, transcendentals=0),
    )(*args)


def exchange_columns(sends, columns):
    near = [(i, i ^ 1) for i in range(columns)]
    far = [(i, (i + 1 if i % 2 else i - 1) % columns) for i in range(columns)]
    return [lax.ppermute(sends[0], "circ", far), lax.ppermute(sends[1], "circ", near)]


def exchange_rows(sends, rows):
    core = [(i, i ^ 1) for i in range(rows)]
    link = [(i, i + 1 if i % 2 else i - 1) for i in range(1, rows - 1)]
    return [lax.ppermute(sends[2], "axial", link), lax.ppermute(sends[3], "axial", core)]


def exchange(sends, rows, columns):
    return exchange_columns(sends, columns) + exchange_rows(sends, rows)


def spread(value, axis, groups=None):
    return lax.all_to_all(
        value, axis, split_axis=0, concat_axis=0, tiled=True, axis_index_groups=groups
    )


def local(
    load_terms, diffusivity, interface_diag, coupling, interior_inverse, neumann_solve,
    row_coarse, lower_coef, upper_coef, face_order, primal_lists,
):
    rows, columns = lax.axis_size("axial"), lax.axis_size("circ")
    rhs, points = load_terms.shape[2], load_terms.shape[3]
    place = jnp.stack(
        [lax.axis_index("axial"), jnp.int32(rows), lax.axis_index("circ")]
    ).astype(jnp.int32)
    swap = functools.partial(exchange, rows=rows, columns=columns)
    dma = pltpu.SemaphoreType.DMA

    def face(n):
        return [(n, LANES)] * 4

    def bf16(*shape):
        return jax.ShapeDtypeStruct((PIECES,) + shape, BF16)

    shared, order, *sends, neumann = call(
        k_prepare,
        [(rhs + 8, points), jax.ShapeDtypeStruct((1, points), jnp.int32)]
        + face(rhs + 8)
        + [(points, points)],
        place, load_terms[0, 0], diffusivity[0], face_order[0], neumann_solve[0, 0],
        raw=(0, 1, 2, 3),
        scratch=[
            pltpu.VMEM((rhs, points), F32),
            pltpu.VMEM((1, points), F32),
            dma((3,)),
            dma((4,)),
        ],
    )
    got = swap(sends)
    neumann, avg, couple = call(
        k_neumann,
        [bf16(points, points), (8, points), (points, points)],
        None, order, neumann, primal_lists[0, 0], coupling[0, 0],
        raw=(2, 3),
        scratch=[
            pltpu.VMEM(primal_lists.shape[2:], jnp.int32),
            dma((5,)),
        ],
        flops=2_000_000_000,
    )
    r0, share, prim0, t0, *sends = call(
        k_first,
        [(rhs, points), (1, points), (8, rhs), (rhs + 8, points)] + face(rhs + 8),
        place, shared, *got, neumann, avg,
    )
    got = swap(sends)
    inner = interior_inverse.shape[2:]
    diag, couple, blocks, coefs = call(
        k_couple,
        [(1, points), bf16(points, points), bf16(*inner), (32, LANES)],
        None, order, share, couple, interface_diag[0], interior_inverse[0, 0],
        row_coarse[0], lower_coef, upper_coef,
        raw=(3, 4, 5, 6, 7),
        scratch=[
            pltpu.VMEM((1, points), F32),
            pltpu.VMEM(inner, F32),
            pltpu.VMEM(row_coarse.shape[1:], F32),
            pltpu.VMEM(lower_coef.shape, F32),
            pltpu.VMEM(upper_coef.shape, F32),
            dma((9,)),
        ],
        flops=2_000_000_000,
    )
    n = rhs + 24
    z0, q0, *sends = call(
        functools.partial(k_schur, rhs=rhs), [(n, points)] * 2 + face(n),
        place, t0, *got, diag, couple, blocks,
        raw_outs=(0,), scratch=[pltpu.VMEM((n, points), F32), dma((1,))],
    )
    got = swap(sends)
    n = rhs + 40
    v1, t1, prim1, *sends = call(
        k_second, [(n, points)] * 2 + [(8, n)] + face(n), place, q0, *got[2:], *got[:2], r0, share, neumann, avg
    )
    got = swap(sends)
    n = rhs + 56
    z1, q1, *sends = call(
        functools.partial(k_schur, rhs=rhs), [(n, points)] * 2 + face(n),
        place, t1, *got, diag, couple, blocks,
        raw_outs=(0,), scratch=[pltpu.VMEM((n, points), F32), dma((1,))],
    )
    got = swap(sends)
    n = rhs + 72
    v2, pay = call(
        k_third, [(n, points), (columns, 32, LANES)], place, q1, *got, v1, share, avg, prim0, prim1,
        raw_outs=(0,), scratch=[pltpu.VMEM((n, points), F32), dma((4,))],
    )
    got = spread(pay, "circ")
    t2, *sends = call(
        k_fourth, [(n, points)] + face(n), place, v2, share, neumann,
        raw=(0,), raw_outs=(0,),
        scratch=[pltpu.VMEM((n, points), F32)] * 2 + [dma((2, 4))],
        flops=500_000_000,
    )
    got, t2 = lax.optimization_barrier((got, t2))
    (pay,) = call(k_sum_spread, [(rows // 2, 32, LANES)], None, got, coefs)
    pay, *sends = lax.optimization_barrier((pay, *sends))
    along = [list(range(core, rows, 2)) for core in range(2)]
    mine = spread(pay, "axial", along)
    mine, *got = lax.optimization_barrier((mine, *swap(sends)))
    other = lax.ppermute(mine, "axial", [(i, i ^ 1) for i in range(rows)])
    width = max(LANES, 8 * rows)
    z0f, z1f, z2f, w0f, w1f, q2, pay, *sends = call(
        k_core,
        [(rhs, points)] * 6 + [(2 * columns, 1, 9 * LANES)] + face(rhs),
        place, mine, other, t2, *got, z0, v1, z1, v2, r0, diag, couple, blocks,
        raw=(2, 9, 10),
        raw_outs=(0, 1, 2, 3, 4),
        scratch=[pltpu.VMEM((width, width), F32)] * 3
        + [pltpu.VMEM((width + 80, rhs), F32)] * 3
        + [pltpu.VMEM((5, rhs, points), F32)]
        + [pltpu.VMEM((rhs + m, points), F32) for m in (72, 56, 72)]
        + [dma((5, 2)), dma((3, 2))],
    )
    chips = [
        [row * columns + column for row in (pair, pair + 1) for column in range(columns)]
        for pair in range(0, rows, 2)
    ]
    dots = spread(pay, ("axial", "circ"), chips)
    got = exchange_columns(sends, columns)
    dots, *got = lax.optimization_barrier((dots, *got))
    blank = jnp.zeros((1, 9 * LANES), F32)
    (pay,) = call(k_sum_spread, [(rows // 2, 1, 9 * LANES)], None, dots, blank)
    pay, *sends = lax.optimization_barrier((pay, *sends))
    dots = spread(pay, "axial", along)
    got = got + exchange_rows(sends, rows)
    x, r = call(
        k_final, [(rhs, points)] * 2,
        place, dots, q2, *got, order, r0, z0f, z1f, z2f, w0f, w1f,
        raw=(10, 11, 12),
        scratch=[pltpu.VMEM((3, rhs, points), F32), dma((3, 2))],
    )
    return (x[None, None], r[None, None])


def solution(mesh):
    in_specs = (
        P("axial", "circ", None, None),
        P("axial", "circ", None),
        P("axial", "circ", None),
        P("axial", "circ", None, None),
        P("axial", "circ", None, None, None),
        P("axial", "circ", None, None),
        P("axial", None, None),
        P("axial", None),
        P("axial", None),
        P("axial", "circ", None),
        P("axial", "circ", None, None),
    )
    out_specs = (P("axial", "circ", None, None), P("axial", "circ", None, None))
    return jax.shard_map(local, mesh=mesh, in_specs=in_specs, out_specs=out_specs, check_vma=False)
```

```python
import functools

import jax
import jax.numpy as jnp
from jax import lax
from jax.experimental import pallas as pl
from jax.experimental.pallas import tpu as pltpu
from jax.sharding import PartitionSpec as P

SHIFT = 12.0
HIGHEST = lax.Precision.HIGHEST
F32 = jnp.float32
BF16 = jnp.bfloat16
LANES = 128
PIECES = 2


def mm_t(a, b):
    return lax.dot_general(
        a, b, (((1,), (1,)), ((), ())), precision=HIGHEST, preferred_element_type=F32
    )


def cut(value, count):
    pieces = []
    for _ in range(count):
        piece = value.astype(BF16)
        pieces.append(piece)
        value = value - piece.astype(F32)
    return pieces


def narrow(a, b, transposed=False):
    return lax.dot_general(
        a, b, (((1,), (1 if transposed else 0,)), ((), ())), preferred_element_type=F32
    )


def product(a, pieces, transposed=False):
    count = a.shape[0]
    levels = len(pieces)
    if count % 16:
        a = jnp.concatenate([a, jnp.zeros((16 - count % 16, a.shape[1]), F32)], axis=0)
    tall = a.shape[0]
    left = cut(a, levels)
    by_level = [None] * levels
    for n, piece in enumerate(pieces):
        used = left[: levels - n]
        stack = used[0] if len(used) == 1 else jnp.concatenate(used, axis=0)
        out = narrow(stack, piece, transposed)
        for m in range(len(used)):
            part = out[m * tall : (m + 1) * tall]
            level = n + m
            by_level[level] = part if by_level[level] is None else by_level[level] + part
    total = by_level[-1]
    for part in by_level[-2::-1]:
        total = total + part
    return total[:count]


def select_columns(a, hot, transposed):
    count = a.shape[0]
    if count % 16:
        a = jnp.concatenate([a, jnp.zeros((16 - count % 16, a.shape[1]), F32)], axis=0)
    tall = a.shape[0]
    out = narrow(jnp.concatenate(cut(a, 3), axis=0), hot, transposed)
    return ((out[2 * tall :] + out[tall : 2 * tall]) + out[:tall])[:count]


def faces_of(full):
    return [full[:, f * LANES : (f + 1) * LANES] for f in range(4)]


def one_hot_faces(order):
    rows = lax.broadcasted_iota(jnp.int32, (LANES, LANES), 0)
    return [
        jnp.where(order[:, f * LANES : (f + 1) * LANES] - f * LANES == rows, 1.0, 0.0)
        .astype(F32)
        .astype(BF16)
        for f in range(4)
    ]


def to_shared(full, hots):
    return jnp.concatenate(
        [select_columns(part, hot, True) for part, hot in zip(faces_of(full), hots)], axis=1
    )


def to_points(full, hots):
    return jnp.concatenate(
        [select_columns(part, hot, False) for part, hot in zip(faces_of(full), hots)], axis=1
    )


class Place:
    def __init__(self, place):
        row, rows, column = place[0], place[1], place[2]
        self.row = row
        self.even_row = lax.rem(row, 2) == 0
        self.even_column = lax.rem(column, 2) == 0
        self.keep_south = jnp.where(row > 0, 1.0, 0.0).astype(F32)
        self.keep_north = jnp.where(row < rows - 1, 1.0, 0.0).astype(F32)


def put_sends(sends, full, at):
    south, north, west, east = faces_of(full)
    sends[0][...] = jnp.where(at.even_column, west, east)
    sends[1][...] = jnp.where(at.even_column, east, west)
    sends[2][...] = jnp.where(at.even_row, south, north)
    sends[3][...] = jnp.where(at.even_row, north, south)


def neighbours(got, at):
    far, near, link, core = [ref[...] for ref in got]
    above = jnp.where(at.even_row, core, link)
    below = jnp.where(at.even_row, link, core)
    right = jnp.where(at.even_column, near, far)
    left = jnp.where(at.even_column, far, near)
    return below, above, left, right


def assembled(full, got, at, rhs, keep=True):
    count = full.shape[0]
    extra = count - rhs
    own = faces_of(full)
    other = neighbours(got, at)
    scale = (at.keep_south, at.keep_north, None, None)
    shift = (0, 16, 8, 8)
    out = []
    for f in range(4):
        part = own[f][:rhs] + other[f][:rhs]
        if extra:
            zero = jnp.zeros((8, LANES), F32)
            mine = jnp.concatenate([zero, own[f][rhs:], zero], axis=0)
            pieces = [jnp.zeros((shift[f], LANES), F32)] if shift[f] else []
            pieces.append(other[f][rhs:])
            if shift[f] < 16:
                pieces.append(jnp.zeros((16 - shift[f], LANES), F32))
            part = jnp.concatenate([part, mine + jnp.concatenate(pieces, axis=0)], axis=0)
        if keep and scale[f] is not None:
            part = part * scale[f]
        out.append(part)
    return jnp.concatenate(out, axis=1)


def held(ref):
    return [ref[n] for n in range(ref.shape[0])]


def schur(z, diag, couple, blocks):
    inner = product(z, couple)
    solved = jnp.concatenate(
        [
            product(part, [piece[n] for piece in blocks])
            for n, part in enumerate(faces_of(inner))
        ],
        axis=1,
    )
    return diag * z - product(solved, couple, True)


def begin(source, target, sems, parts):
    rows = source.shape[0] // 8
    edges = [8 * (rows * n // parts) for n in range(parts)] + [source.shape[0]]
    copies = []
    for n in range(parts):
        band = pl.ds(edges[n], edges[n + 1] - edges[n])
        copies.append(pltpu.make_async_copy(source.at[band], target.at[band], sems.at[n]))
        copies[n].start()
    return copies


def finish(copies):
    for copy in copies:
        copy.wait()


def k_prepare(
    place, load, rho, order, neumann, shared_o, order_o, s0, s1, s2, s3, neumann_o, load_s, rho_s, sem, far_sem
):
    at = Place(place)
    copies = [
        pltpu.make_async_copy(source, target, sem.at[n])
        for n, (source, target) in enumerate(((order, order_o), (load, load_s), (rho, rho_s)))
    ]
    for copy in copies:
        copy.start()
    ahead = begin(neumann, neumann_o, far_sem, 4)
    copies[0].wait()
    hots = one_hot_faces(order_o[...])
    copies[1].wait()
    copies[2].wait()
    pad = jnp.zeros((7, rho_s.shape[1]), F32)
    full = to_shared(jnp.concatenate([load_s[...], rho_s[...], pad], axis=0), hots)
    shared_o[...] = full
    put_sends((s0, s1, s2, s3), full, at)
    finish(ahead)


def k_neumann(order, neumann_s, lists, couple, neumann_o, avg_o, couple_o, lists_s, sem):
    listed = pltpu.make_async_copy(lists, lists_s, sem.at[4])
    listed.start()
    ahead = begin(couple, couple_o, sem, 4)
    hots = one_hot_faces(order[...])
    points = order.shape[1]
    listed.wait()
    named = lists_s[...]
    position = lax.broadcasted_iota(jnp.int32, (8, points), 1)
    total = jnp.zeros((8, points), F32)
    length = named.shape[1]
    for item in range(length):
        total = total + jnp.where(named[:, item : item + 1] == position, 1.0, 0.0)
    avg_o[...] = to_shared(total * (1.0 / length), hots)
    tall = jnp.concatenate(cut(neumann_s[...], PIECES), axis=0)
    half = jnp.concatenate(
        [narrow(part, hot, True).astype(BF16) for part, hot in zip(faces_of(tall), hots)], axis=1
    )
    for n in range(PIECES):
        for f in range(4):
            first = n * points + f * LANES
            neumann_o[n, f * LANES : (f + 1) * LANES, :] = narrow(
                hots[f], half[first : first + LANES]
            ).astype(BF16)
    finish(ahead)


def k_couple(
    order, after, couple_s, diag, blocks, row_coarse, lower, upper,
    diag_o, couple_o, blocks_o, coefs_o,
    diag_s, blocks_s, rows_s, lower_s, upper_s, sem,
):
    copies = [None] * 4
    copies.append(pltpu.make_async_copy(blocks, blocks_s, sem.at[4]))
    copies.append(pltpu.make_async_copy(diag, diag_s, sem.at[5]))
    copies.append(pltpu.make_async_copy(row_coarse, rows_s, sem.at[6]))
    copies.append(pltpu.make_async_copy(lower, lower_s, sem.at[7]))
    copies.append(pltpu.make_async_copy(upper, upper_s, sem.at[8]))
    for copy in copies[4:]:
        copy.start()
    hots = one_hot_faces(order[...])
    copies[5].wait()
    diag_o[...] = to_shared(jnp.broadcast_to(diag_s[...], (8, diag_s.shape[1])), hots)[:1]
    for f in range(4):
        rows = slice(f * LANES, (f + 1) * LANES)
        for n, piece in enumerate(cut(couple_s[rows, :], PIECES)):
            couple_o[n, rows, :] = narrow(hots[f], piece).astype(BF16)
    copies[4].wait()
    for f in range(4):
        for n, piece in enumerate(cut(blocks_s[f], PIECES)):
            blocks_o[n, f] = piece
    for n in (6, 7, 8):
        copies[n].wait()
    count = lower_s.shape[1]
    lane = lax.broadcasted_iota(jnp.int32, (count, LANES), 1)
    eye = lax.broadcasted_iota(jnp.int32, (count, count), 0) == lax.broadcasted_iota(
        jnp.int32, (count, count), 1
    )
    tile = jnp.zeros((count, LANES), F32)
    for n in range(count):
        tile = tile + jnp.where(lane == 112 + n, rows_s[:, n : n + 1], 0.0)
    for n, ref in ((120, lower_s), (121, upper_s)):
        column = jnp.sum(
            jnp.where(eye, jnp.broadcast_to(ref[...], (count, count)), 0.0), axis=1, keepdims=True
        )
        tile = tile + jnp.where(lane == n, column, 0.0)
    coefs_o[0:24, :] = jnp.zeros((24, LANES), F32)
    coefs_o[24:32, :] = tile


def k_first(place, shared, g0, g1, g2, g3, neumann, avg, r_o, share_o, prim_o, t_o, *sends):
    at = Place(place)
    rhs = r_o.shape[0]
    full = assembled(shared[...], (g0, g1, g2, g3), at, shared.shape[0], keep=False)
    share = shared[rhs : rhs + 1, :] / full[rhs : rhs + 1]
    south, north, west, east = faces_of(full[:rhs])
    r = jnp.concatenate([south * at.keep_south, north * at.keep_north, west, east], axis=1)
    r_o[...] = r
    share_o[...] = share
    weighted = share * r
    prim_o[...] = mm_t(avg[...], weighted)
    t = jnp.concatenate([share * product(weighted, held(neumann)), share * avg[...]], axis=0)
    t_o[...] = t
    put_sends(sends, t, at)


def k_schur(
    place, t, g0, g1, g2, g3, diag, couple, blocks, z_o, q_o, s0, s1, s2, s3, z_s, sem, *, rhs
):
    at = Place(place)
    z = assembled(t[...], (g0, g1, g2, g3), at, rhs)
    z_s[...] = z
    copy = pltpu.make_async_copy(z_s, z_o, sem.at[0])
    copy.start()
    q = schur(z, diag[...], held(couple), held(blocks))
    q_o[...] = q
    put_sends((s0, s1, s2, s3), q, at)
    copy.wait()


def k_second(place, q, g2, g3, g0, g1, r, share, neumann, avg, v_o, t_o, pr_o, *sends):
    at = Place(place)
    rhs = r.shape[0]
    w = assembled(q[...], (g0, g1, g2, g3), at, rhs)
    v = jnp.concatenate([w[:rhs] - SHIFT * r[...], w[rhs:]], axis=0)
    v_o[...] = v
    weighted = share[...] * v
    pr_o[...] = jnp.concatenate(
        [mm_t(avg[...], weighted[:rhs]), mm_t(avg[...], weighted[rhs:])], axis=1
    )
    t = share[...] * product(weighted, held(neumann))
    t_o[...] = t
    put_sends(sends, t, at)


def k_third(place, q, g0, g1, g2, g3, v, share, avg, prim0, prim1, v2_o, pay_o, v2_s, sem):
    at = Place(place)
    rhs = prim0.shape[1]
    w = assembled(q[...], (g0, g1, g2, g3), at, rhs)
    zero = jnp.zeros((16, w.shape[1]), F32)
    older = jnp.concatenate([v[...][:rhs], zero, v[...][rhs:], zero], axis=0)
    v2 = w - SHIFT * older
    v2_s[...] = v2
    copies = begin(v2_s, v2_o, sem, 4)
    weighted = share[...] * v2
    prim2 = mm_t(avg[...], weighted[:rhs])
    reach2 = mm_t(avg[...], weighted[rhs:])
    reach1 = prim1[...][:, rhs:]
    spare = jnp.zeros((8, LANES - reach1.shape[1] - reach2.shape[1]), F32)
    tail = jnp.concatenate([reach1, reach2, spare], axis=1)
    pay = jnp.concatenate([prim0[...], prim1[...][:, :rhs], prim2, tail], axis=0)
    for item in range(pay_o.shape[0]):
        pay_o[item] = pay
    finish(copies)


def summed(got):
    total = got[0]
    for item in range(1, got.shape[0]):
        total = total + got[item]
    return total


def k_sum_spread(got, coefs, out):
    total = summed(got) + coefs[...]
    for item in range(out.shape[0]):
        out[item] = total


def banded_product(pieces, value):
    first, second = cut(value, 2)
    return (narrow(pieces[1], first) + narrow(pieces[0], second)) + narrow(pieces[0], first)


def coarse_rows(totals, lowers, uppers):
    carry = jnp.zeros_like(totals[0])
    smooth = []
    for low, value in zip(lowers, [(1.0 - low) * value for low, value in zip(lowers, totals)]):
        carry = low * carry + value
        smooth.append(carry)
    carry = jnp.zeros_like(totals[0])
    tops = []
    smooth = [(1.0 - up) * value for up, value in zip(uppers, smooth)]
    for up, value in zip(uppers[::-1], smooth[::-1]):
        carry = up * carry + value
        tops.append(carry)
    return tops[::-1]


def k_fourth(place, v2, share, neumann, t_o, s0, s1, s2, s3, v2_s, t_s, sem):
    at = Place(place)
    finish(begin(v2, v2_s, sem.at[0], 4))
    t = share[...] * product(share[...] * v2_s[...], held(neumann))
    t_s[...] = t
    copies = begin(t_s, t_o, sem.at[1], 4)
    put_sends((s0, s1, s2, s3), t, at)
    finish(copies)


def lift(coefs, basis):
    spare = -coefs.shape[0] % 16
    if spare:
        coefs = jnp.concatenate([coefs, jnp.zeros((spare, coefs.shape[1]), F32)], axis=0)
        basis = jnp.concatenate([basis, jnp.zeros((spare, basis.shape[1]), F32)], axis=0)
    c, b = cut(coefs, 2), cut(basis, 2)

    def times(x, y):
        return lax.dot_general(x, y, (((0,), (0,)), ((), ())), preferred_element_type=F32)

    return (times(c[1], b[0]) + times(c[0], b[1])) + times(c[0], b[0])


def k_core(
    place, mine, other, t, g0, g1, g2, g3, z0, v1, z1, v2, r, diag, couple, blocks,
    z0_o, z1_o, z2_o, w0_o, w1_o, q_o, pay_o, s0, s1, s2, s3,
    band0, band1, band2, c0_s, c1_s, c2_s, full_s, t_s, z1_s, v2_s, sem, in_sem,
):
    at = Place(place)
    loads = []
    for n, (source, target) in enumerate(((z1, z1_s), (v2, v2_s), (t, t_s))):
        loads += begin(source, target, in_sem.at[n], 2)
    t, z1, v2 = t_s, z1_s, v2_s
    rhs = r.shape[0]
    rows = 2 * mine.shape[0]
    width = band0.shape[1]
    lane = lax.broadcasted_iota(jnp.int32, (8, width), 1)
    lowers, uppers = [], []
    for ref in (band0, band1, band2):
        if ref.shape[0] > rows * 8:
            ref[rows * 8 :, :] = jnp.zeros((ref.shape[0] - rows * 8, width), F32)
    pays = []
    for k in range(rows // 2):
        pays.append(jnp.where(at.even_row, mine[k], other[k]))
        pays.append(jnp.where(at.even_row, other[k], mine[k]))
    for k in range(rows):
        tail = pays[k][24:32]
        lowers.append(jnp.broadcast_to(tail[:, 120:121], (8, rhs)))
        uppers.append(jnp.broadcast_to(tail[:, 121:122], (8, rhs)))
        wide = tail
        if width > LANES:
            wide = jnp.concatenate([tail, jnp.zeros((8, width - LANES), F32)], axis=1)
        for ref, first, last, to in (
            (band1, 0, 40, 8 * (k - 2)),
            (band2, 40, 112, 8 * (k - 4)),
            (band0, 112, 120, 8 * k),
        ):
            picked = jnp.where((lane >= first) & (lane < last), wide, 0.0)
            ref[8 * k : 8 * k + 8, :] = pltpu.roll(picked, (to - first) % width, 1)

    def stacked(tiles):
        if width > rows * 8:
            tiles = tiles + [jnp.zeros((width - rows * 8, rhs), F32)]
        return jnp.concatenate(tiles, axis=0)

    own, near, wide = [cut(ref[...], 2) for ref in (band0, band1, band2)]

    def solve(total):
        tiles = [total[8 * k : 8 * k + 8] for k in range(rows)]
        return stacked(coarse_rows(tiles, lowers, uppers)) + banded_product(own, total)

    edge = jnp.zeros((40, rhs), F32)
    c0 = solve(stacked([part[0:8] for part in pays]))
    c1 = solve(stacked([part[8:16] for part in pays]) + banded_product(near, c0))
    c2 = solve(
        stacked([part[16:24] for part in pays])
        + banded_product(wide, c0)
        + banded_product(near, c1)
    )
    for ref, value in ((c0_s, c0), (c1_s, c1), (c2_s, c2)):
        ref[0:40, :] = edge
        ref[40 : 40 + width, :] = value
        ref[40 + width :, :] = edge
    start = at.row * 8
    c0 = c0_s[pl.ds(pl.multiple_of(start, 8), 88), :]
    c1 = c1_s[pl.ds(pl.multiple_of(start + 16, 8), 56), :]
    c2 = c2_s[pl.ds(pl.multiple_of(start + 32, 8), 24), :]
    r0 = r[...]
    z0f = z0[:rhs, :] + lift(c0[32:56], z0[rhs:, :])
    v1f = v1[:rhs, :] + lift(c0[24:64], v1[rhs:, :])
    finish(loads[0:2])
    z1f = z1[:rhs, :] + lift(
        jnp.concatenate([c0[16:72], c1[16:40]], axis=0),
        jnp.concatenate([z1[rhs:, :], z0[rhs:, :]], axis=0),
    )
    finish(loads[2:4])
    v2f = v2[:rhs, :] + lift(
        jnp.concatenate([c0[8:80], c1[8:48]], axis=0),
        jnp.concatenate([v2[rhs:, :], v1[rhs:, :]], axis=0),
    )
    copies = []

    def keep(n, value, out):
        full_s[n] = value
        copies.extend(begin(full_s.at[n], out, sem.at[n], 2))

    keep(0, z0f, z0_o)
    keep(1, z1f, z1_o)
    keep(2, v1f + SHIFT * r0, w0_o)
    keep(3, v2f + SHIFT * v1f, w1_o)
    finish(loads[4:6])
    z2 = assembled(t[...], (g0, g1, g2, g3), at, rhs)
    z2f = z2[:rhs] + lift(
        jnp.concatenate([c0, c1, c2], axis=0),
        jnp.concatenate([z2[rhs:], z1[rhs:, :], z0[rhs:, :]], axis=0),
    )
    keep(4, z2f, z2_o)
    q = schur(z2f, diag[...], held(couple), held(blocks))
    q_o[...] = q
    put_sends((s0, s1, s2, s3), q, at)
    table = dot_rows(
        [(r0, z0f), (r0, z1f), (v1f, z0f), (v1f, z1f), (v2f, z1f)]
        + [(r0, z2f), (v1f, z2f), (v2f, z2f), (z2f, q + q)]
    )
    line = jnp.concatenate([table[i : i + 1] for i in range(9)], axis=1)
    for item in range(pay_o.shape[0]):
        pay_o[item] = line
    finish(copies)


def dot_rows(pairs):
    parts = []
    for a, b in pairs:
        faces = faces_of(a * b)
        parts.append((faces[0] + faces[1]) + (faces[2] + faces[3]))
    wide = jnp.concatenate(parts, axis=1)
    shape = (16, wide.shape[1])
    pick = jnp.where(
        lax.broadcasted_iota(jnp.int32, shape, 0) == lax.broadcasted_iota(jnp.int32, shape, 1) // LANES,
        1.0,
        0.0,
    ).astype(BF16)
    high, middle, low = [narrow(pick, piece, True) for piece in cut(wide, 3)]
    return (low + middle) + high


def k_final(
    place, got, q, g0, g1, g2, g3, order, r0, z0, z1, z2, w0, w1, x_o, r_o, full_s, both_s, sem, out_sem
):
    loads = []
    for n, source in enumerate((z2, w0, w1)):
        loads += begin(source, full_s.at[n], sem.at[n], 2)
    w2 = assembled(q[...], (g0, g1, g2, g3), Place(place), q.shape[0])
    total = summed(got)
    v0z0, v0z1, v1z0, v1z1, v2z1, v0z2, v1z2, v2z2, z2w2 = [
        total[:, i * LANES : (i + 1) * LANES] for i in range(9)
    ]
    z1w0 = v1z1 + SHIFT * v0z1
    z2w0 = v1z2 + SHIFT * v0z2
    z2w1 = v2z2 + SHIFT * v1z2
    zw = [
        [v1z0 + SHIFT * v0z0, z1w0, z2w0],
        [z1w0, v2z1 + SHIFT * v1z1, z2w1],
        [z2w0, z2w1, z2w2],
    ]
    vz = [[v0z0, v0z1, v0z2], [v1z0, v1z1, v1z2], [z1w0 - SHIFT * v1z0, v2z1, v2z2]]

    def form(left, table, right):
        value = None
        for i, a in enumerate(left):
            for j, b in enumerate(right):
                if a is None or b is None:
                    continue
                term = a * table[i][j] * b
                value = term if value is None else value + term
        return value

    one = jnp.ones_like(vz[0][0])
    zero = jnp.zeros_like(one)
    toward = [one, None, None]
    steps = [zero, zero, zero]
    drops = [zero, zero, zero]
    rz = vz[0][0]
    for iteration in range(3):
        alpha = rz / form(toward, zw, toward)
        for j in range(3):
            if toward[j] is not None:
                steps[j] = steps[j] + alpha * toward[j]
                drops[j] = drops[j] - alpha * toward[j]
        if iteration < 2:
            mix = [one + SHIFT * drops[0], drops[0] + SHIFT * drops[1], None]
            if iteration == 1:
                mix[2] = drops[1]
            new = form(mix, vz, mix)
            beta = new / rz
            toward = [
                m if d is None else (beta * d if m is None else m + beta * d)
                for m, d in zip(mix, toward)
            ]
            rz = new
    table = jnp.concatenate(steps + drops + [zero, zero], axis=0)
    eye = jnp.where(
        lax.broadcasted_iota(jnp.int32, (LANES, LANES), 0)
        == lax.broadcasted_iota(jnp.int32, (LANES, LANES), 1),
        1.0,
        0.0,
    ).astype(F32)
    columns = mm_t(eye, table)
    col = [columns[:, i : i + 1] for i in range(6)]
    hots = one_hot_faces(order[...])
    finish(loads)
    x = col[0] * z0[...] + col[1] * z1[...] + col[2] * full_s[0]
    both_s[0] = to_points(x, hots)
    copies = begin(both_s.at[0], x_o, out_sem.at[0], 2)
    r = r0[...] + col[3] * full_s[1] + col[4] * full_s[2] + col[5] * w2
    both_s[1] = to_points(r, hots)
    copies += begin(both_s.at[1], r_o, out_sem.at[1], 2)
    finish(copies)


def call(body, outs, place, *args, scratch=(), raw=(), raw_outs=(), flops=1_000_000):
    args = tuple(
        pltpu.with_memory_space_constraint(arg, pltpu.HBM) if n in raw else arg
        for n, arg in enumerate(args)
    )
    space = [pltpu.HBM if n in raw else pltpu.VMEM for n in range(len(args))]
    specs = [pl.BlockSpec(memory_space=kind) for kind in space]
    if place is not None:
        specs = [pl.BlockSpec(memory_space=pltpu.SMEM)] + specs
        args = (place,) + args
    return pl.pallas_call(
        body,
        out_shape=[
            out
            if isinstance(out, jax.ShapeDtypeStruct)
            else (pltpu.HBM(out, F32) if n in raw_outs else jax.ShapeDtypeStruct(out, F32))
            for n, out in enumerate(outs)
        ],
        in_specs=specs,
        out_specs=[
            pl.BlockSpec(memory_space=pltpu.HBM if n in raw_outs else pltpu.VMEM)
            for n in range(len(outs))
        ],
        scratch_shapes=list(scratch),
        compiler_params=pltpu.CompilerParams(vmem_limit_bytes=16 * 1024 * 1024),
        cost_estimate=pl.CostEstimate(flops=flops, bytes_accessed=1_000_000, transcendentals=0),
    )(*args)


def exchange_columns(sends, columns):
    near = [(i, i ^ 1) for i in range(columns)]
    far = [(i, (i + 1 if i % 2 else i - 1) % columns) for i in range(columns)]
    return [lax.ppermute(sends[0], "circ", far), lax.ppermute(sends[1], "circ", near)]


def exchange_rows(sends, rows):
    core = [(i, i ^ 1) for i in range(rows)]
    link = [(i, i + 1 if i % 2 else i - 1) for i in range(1, rows - 1)]
    return [lax.ppermute(sends[2], "axial", link), lax.ppermute(sends[3], "axial", core)]


def exchange(sends, rows, columns):
    return exchange_columns(sends, columns) + exchange_rows(sends, rows)


def spread(value, axis, groups=None):
    return lax.all_to_all(
        value, axis, split_axis=0, concat_axis=0, tiled=True, axis_index_groups=groups
    )


def local(
    load_terms, diffusivity, interface_diag, coupling, interior_inverse, neumann_solve,
    row_coarse, lower_coef, upper_coef, face_order, primal_lists,
):
    rows, columns = lax.axis_size("axial"), lax.axis_size("circ")
    rhs, points = load_terms.shape[2], load_terms.shape[3]
    place = jnp.stack(
        [lax.axis_index("axial"), jnp.int32(rows), lax.axis_index("circ")]
    ).astype(jnp.int32)
    swap = functools.partial(exchange, rows=rows, columns=columns)
    dma = pltpu.SemaphoreType.DMA

    def face(n):
        return [(n, LANES)] * 4

    def bf16(*shape):
        return jax.ShapeDtypeStruct((PIECES,) + shape, BF16)

    shared, order, *sends, neumann = call(
        k_prepare,
        [(rhs + 8, points), jax.ShapeDtypeStruct((1, points), jnp.int32)]
        + face(rhs + 8)
        + [(points, points)],
        place, load_terms[0, 0], diffusivity[0], face_order[0], neumann_solve[0, 0],
        raw=(0, 1, 2, 3),
        scratch=[
            pltpu.VMEM((rhs, points), F32),
            pltpu.VMEM((1, points), F32),
            dma((3,)),
            dma((4,)),
        ],
    )
    got = swap(sends)
    neumann, avg, couple = call(
        k_neumann,
        [bf16(points, points), (8, points), (points, points)],
        None, order, neumann, primal_lists[0, 0], coupling[0, 0],
        raw=(2, 3),
        scratch=[
            pltpu.VMEM(primal_lists.shape[2:], jnp.int32),
            dma((5,)),
        ],
        flops=2_000_000_000,
    )
    r0, share, prim0, t0, *sends = call(
        k_first,
        [(rhs, points), (1, points), (8, rhs), (rhs + 8, points)] + face(rhs + 8),
        place, shared, *got, neumann, avg,
    )
    got = swap(sends)
    inner = interior_inverse.shape[2:]
    diag, couple, blocks, coefs = call(
        k_couple,
        [(1, points), bf16(points, points), bf16(*inner), (32, LANES)],
        None, order, share, couple, interface_diag[0], interior_inverse[0, 0],
        row_coarse[0], lower_coef, upper_coef,
        raw=(3, 4, 5, 6, 7),
        scratch=[
            pltpu.VMEM((1, points), F32),
            pltpu.VMEM(inner, F32),
            pltpu.VMEM(row_coarse.shape[1:], F32),
            pltpu.VMEM(lower_coef.shape, F32),
            pltpu.VMEM(upper_coef.shape, F32),
            dma((9,)),
        ],
        flops=2_000_000_000,
    )
    n = rhs + 24
    z0, q0, *sends = call(
        functools.partial(k_schur, rhs=rhs), [(n, points)] * 2 + face(n),
        place, t0, *got, diag, couple, blocks,
        raw_outs=(0,), scratch=[pltpu.VMEM((n, points), F32), dma((1,))],
    )
    got = swap(sends)
    n = rhs + 40
    v1, t1, prim1, *sends = call(
        k_second, [(n, points)] * 2 + [(8, n)] + face(n), place, q0, *got[2:], *got[:2], r0, share, neumann, avg
    )
    got = swap(sends)
    n = rhs + 56
    z1, q1, *sends = call(
        functools.partial(k_schur, rhs=rhs), [(n, points)] * 2 + face(n),
        place, t1, *got, diag, couple, blocks,
        raw_outs=(0,), scratch=[pltpu.VMEM((n, points), F32), dma((1,))],
    )
    got = swap(sends)
    n = rhs + 72
    v2, pay = call(
        k_third, [(n, points), (columns, 32, LANES)], place, q1, *got, v1, share, avg, prim0, prim1,
        raw_outs=(0,), scratch=[pltpu.VMEM((n, points), F32), dma((4,))],
    )
    got = spread(pay, "circ")
    t2, *sends = call(
        k_fourth, [(n, points)] + face(n), place, v2, share, neumann,
        raw=(0,), raw_outs=(0,),
        scratch=[pltpu.VMEM((n, points), F32)] * 2 + [dma((2, 4))],
        flops=500_000_000,
    )
    got, t2 = lax.optimization_barrier((got, t2))
    (pay,) = call(k_sum_spread, [(rows // 2, 32, LANES)], None, got, coefs)
    pay, *sends = lax.optimization_barrier((pay, *sends))
    along = [list(range(core, rows, 2)) for core in range(2)]
    mine = spread(pay, "axial", along)
    mine, *got = lax.optimization_barrier((mine, *swap(sends)))
    other = lax.ppermute(mine, "axial", [(i, i ^ 1) for i in range(rows)])
    width = max(LANES, 8 * rows)
    z0f, z1f, z2f, w0f, w1f, q2, pay, *sends = call(
        k_core,
        [(rhs, points)] * 6 + [(2 * columns, 1, 9 * LANES)] + face(rhs),
        place, mine, other, t2, *got, z0, v1, z1, v2, r0, diag, couple, blocks,
        raw=(2, 9, 10),
        raw_outs=(0, 1, 2, 3, 4),
        scratch=[pltpu.VMEM((width, width), F32)] * 3
        + [pltpu.VMEM((width + 80, rhs), F32)] * 3
        + [pltpu.VMEM((5, rhs, points), F32)]
        + [pltpu.VMEM((rhs + m, points), F32) for m in (72, 56, 72)]
        + [dma((5, 2)), dma((3, 2))],
    )
    chips = [
        [row * columns + column for row in (pair, pair + 1) for column in range(columns)]
        for pair in range(0, rows, 2)
    ]
    dots = spread(pay, ("axial", "circ"), chips)
    got = exchange_columns(sends, columns)
    dots, *got = lax.optimization_barrier((dots, *got))
    blank = jnp.zeros((1, 9 * LANES), F32)
    (pay,) = call(k_sum_spread, [(rows // 2, 1, 9 * LANES)], None, dots, blank)
    pay, *sends = lax.optimization_barrier((pay, *sends))
    dots = spread(pay, "axial", along)
    got = got + exchange_rows(sends, rows)
    x, r = call(
        k_final, [(rhs, points)] * 2,
        place, dots, q2, *got, order, r0, z0f, z1f, z2f, w0f, w1f,
        raw=(10, 11, 12),
        raw_outs=(0, 1),
        scratch=[
            pltpu.VMEM((3, rhs, points), F32),
            pltpu.VMEM((2, rhs, points), F32),
            dma((3, 2)),
            dma((2, 2)),
        ],
    )
    return (x[None, None], r[None, None])


def solution(mesh):
    in_specs = (
        P("axial", "circ", None, None),
        P("axial", "circ", None),
        P("axial", "circ", None),
        P("axial", "circ", None, None),
        P("axial", "circ", None, None, None),
        P("axial", "circ", None, None),
        P("axial", None, None),
        P("axial", None),
        P("axial", None),
        P("axial", "circ", None),
        P("axial", "circ", None, None),
    )
    out_specs = (P("axial", "circ", None, None), P("axial", "circ", None, None))
    return jax.shard_map(local, mesh=mesh, in_specs=in_specs, out_specs=out_specs, check_vma=False)
```

```python
import functools

import jax
import jax.numpy as jnp
from jax import lax
from jax.experimental import pallas as pl
from jax.experimental.pallas import tpu as pltpu
from jax.sharding import PartitionSpec as P

SHIFT = 12.0
HIGHEST = lax.Precision.HIGHEST
F32 = jnp.float32
BF16 = jnp.bfloat16
LANES = 128
PIECES = 2


def mm_t(a, b):
    return lax.dot_general(
        a, b, (((1,), (1,)), ((), ())), precision=HIGHEST, preferred_element_type=F32
    )


def cut(value, count):
    pieces = []
    for _ in range(count):
        piece = value.astype(BF16)
        pieces.append(piece)
        value = value - piece.astype(F32)
    return pieces


def narrow(a, b, transposed=False):
    return lax.dot_general(
        a, b, (((1,), (1 if transposed else 0,)), ((), ())), preferred_element_type=F32
    )


def product(a, pieces, transposed=False):
    count = a.shape[0]
    levels = len(pieces)
    if count % 16:
        a = jnp.concatenate([a, jnp.zeros((16 - count % 16, a.shape[1]), F32)], axis=0)
    tall = a.shape[0]
    left = cut(a, levels)
    by_level = [None] * levels
    for n, piece in enumerate(pieces):
        used = left[: levels - n]
        stack = used[0] if len(used) == 1 else jnp.concatenate(used, axis=0)
        out = narrow(stack, piece, transposed)
        for m in range(len(used)):
            part = out[m * tall : (m + 1) * tall]
            level = n + m
            by_level[level] = part if by_level[level] is None else by_level[level] + part
    total = by_level[-1]
    for part in by_level[-2::-1]:
        total = total + part
    return total[:count]


def select_columns(a, hot, transposed):
    count = a.shape[0]
    if count % 16:
        a = jnp.concatenate([a, jnp.zeros((16 - count % 16, a.shape[1]), F32)], axis=0)
    tall = a.shape[0]
    out = narrow(jnp.concatenate(cut(a, 3), axis=0), hot, transposed)
    return ((out[2 * tall :] + out[tall : 2 * tall]) + out[:tall])[:count]


def faces_of(full):
    return [full[:, f * LANES : (f + 1) * LANES] for f in range(4)]


def one_hot_faces(order):
    rows = lax.broadcasted_iota(jnp.int32, (LANES, LANES), 0)
    return [
        jnp.where(order[:, f * LANES : (f + 1) * LANES] - f * LANES == rows, 1.0, 0.0)
        .astype(F32)
        .astype(BF16)
        for f in range(4)
    ]


def to_shared(full, hots):
    return jnp.concatenate(
        [select_columns(part, hot, True) for part, hot in zip(faces_of(full), hots)], axis=1
    )


def to_points(full, hots):
    return jnp.concatenate(
        [select_columns(part, hot, False) for part, hot in zip(faces_of(full), hots)], axis=1
    )


class Place:
    def __init__(self, place):
        row, rows, column = place[0], place[1], place[2]
        self.row = row
        self.even_row = lax.rem(row, 2) == 0
        self.even_column = lax.rem(column, 2) == 0
        self.keep_south = jnp.where(row > 0, 1.0, 0.0).astype(F32)
        self.keep_north = jnp.where(row < rows - 1, 1.0, 0.0).astype(F32)


def put_sends(sends, full, at):
    south, north, west, east = faces_of(full)
    sends[0][...] = jnp.where(at.even_column, west, east)
    sends[1][...] = jnp.where(at.even_column, east, west)
    sends[2][...] = jnp.where(at.even_row, south, north)
    sends[3][...] = jnp.where(at.even_row, north, south)


def neighbours(got, at):
    far, near, link, core = [ref[...] for ref in got]
    above = jnp.where(at.even_row, core, link)
    below = jnp.where(at.even_row, link, core)
    right = jnp.where(at.even_column, near, far)
    left = jnp.where(at.even_column, far, near)
    return below, above, left, right


def assembled(full, got, at, rhs, keep=True):
    count = full.shape[0]
    extra = count - rhs
    own = faces_of(full)
    other = neighbours(got, at)
    scale = (at.keep_south, at.keep_north, None, None)
    shift = (0, 16, 8, 8)
    out = []
    for f in range(4):
        part = own[f][:rhs] + other[f][:rhs]
        if extra:
            zero = jnp.zeros((8, LANES), F32)
            mine = jnp.concatenate([zero, own[f][rhs:], zero], axis=0)
            pieces = [jnp.zeros((shift[f], LANES), F32)] if shift[f] else []
            pieces.append(other[f][rhs:])
            if shift[f] < 16:
                pieces.append(jnp.zeros((16 - shift[f], LANES), F32))
            part = jnp.concatenate([part, mine + jnp.concatenate(pieces, axis=0)], axis=0)
        if keep and scale[f] is not None:
            part = part * scale[f]
        out.append(part)
    return jnp.concatenate(out, axis=1)


def held(ref):
    return [ref[n] for n in range(ref.shape[0])]


def schur(z, diag, couple, blocks):
    inner = product(z, couple)
    solved = jnp.concatenate(
        [
            product(part, [piece[n] for piece in blocks])
            for n, part in enumerate(faces_of(inner))
        ],
        axis=1,
    )
    return diag * z - product(solved, couple, True)


def begin(source, target, sems, parts):
    rows = source.shape[0] // 8
    edges = [8 * (rows * n // parts) for n in range(parts)] + [source.shape[0]]
    copies = []
    for n in range(parts):
        band = pl.ds(edges[n], edges[n + 1] - edges[n])
        copies.append(pltpu.make_async_copy(source.at[band], target.at[band], sems.at[n]))
        copies[n].start()
    return copies


def finish(copies):
    for copy in copies:
        copy.wait()


def k_prepare(
    place, load, rho, order, neumann, shared_o, order_o, s0, s1, s2, s3, neumann_o, load_s, rho_s, sem, far_sem
):
    at = Place(place)
    copies = [
        pltpu.make_async_copy(source, target, sem.at[n])
        for n, (source, target) in enumerate(((order, order_o), (load, load_s), (rho, rho_s)))
    ]
    for copy in copies:
        copy.start()
    ahead = begin(neumann, neumann_o, far_sem, 4)
    copies[0].wait()
    hots = one_hot_faces(order_o[...])
    copies[1].wait()
    copies[2].wait()
    pad = jnp.zeros((7, rho_s.shape[1]), F32)
    full = to_shared(jnp.concatenate([load_s[...], rho_s[...], pad], axis=0), hots)
    shared_o[...] = full
    put_sends((s0, s1, s2, s3), full, at)
    finish(ahead)


def k_neumann(order, neumann_s, lists, couple, neumann_o, avg_o, couple_o, lists_s, sem):
    listed = pltpu.make_async_copy(lists, lists_s, sem.at[4])
    listed.start()
    ahead = begin(couple, couple_o, sem, 4)
    hots = one_hot_faces(order[...])
    points = order.shape[1]
    listed.wait()
    named = lists_s[...]
    position = lax.broadcasted_iota(jnp.int32, (8, points), 1)
    total = jnp.zeros((8, points), F32)
    length = named.shape[1]
    for item in range(length):
        total = total + jnp.where(named[:, item : item + 1] == position, 1.0, 0.0)
    avg_o[...] = to_shared(total * (1.0 / length), hots)
    tall = jnp.concatenate(cut(neumann_s[...], PIECES), axis=0)
    half = jnp.concatenate(
        [narrow(part, hot, True).astype(BF16) for part, hot in zip(faces_of(tall), hots)], axis=1
    )
    for n in range(PIECES):
        for f in range(4):
            first = n * points + f * LANES
            neumann_o[n, f * LANES : (f + 1) * LANES, :] = narrow(
                hots[f], half[first : first + LANES]
            ).astype(BF16)
    finish(ahead)


def k_couple(
    order, after, couple_s, diag, blocks, row_coarse, lower, upper,
    diag_o, couple_o, blocks_o, coefs_o,
    diag_s, blocks_s, rows_s, lower_s, upper_s, sem,
):
    copies = [None] * 4
    copies.append(pltpu.make_async_copy(blocks, blocks_s, sem.at[4]))
    copies.append(pltpu.make_async_copy(diag, diag_s, sem.at[5]))
    copies.append(pltpu.make_async_copy(row_coarse, rows_s, sem.at[6]))
    copies.append(pltpu.make_async_copy(lower, lower_s, sem.at[7]))
    copies.append(pltpu.make_async_copy(upper, upper_s, sem.at[8]))
    for copy in copies[4:]:
        copy.start()
    hots = one_hot_faces(order[...])
    copies[5].wait()
    diag_o[...] = to_shared(jnp.broadcast_to(diag_s[...], (8, diag_s.shape[1])), hots)[:1]
    for f in range(4):
        rows = slice(f * LANES, (f + 1) * LANES)
        for n, piece in enumerate(cut(couple_s[rows, :], PIECES)):
            couple_o[n, rows, :] = narrow(hots[f], piece).astype(BF16)
    copies[4].wait()
    for f in range(4):
        for n, piece in enumerate(cut(blocks_s[f], PIECES)):
            blocks_o[n, f] = piece
    for n in (6, 7, 8):
        copies[n].wait()
    count = lower_s.shape[1]
    lane = lax.broadcasted_iota(jnp.int32, (count, LANES), 1)
    eye = lax.broadcasted_iota(jnp.int32, (count, count), 0) == lax.broadcasted_iota(
        jnp.int32, (count, count), 1
    )
    tile = jnp.zeros((count, LANES), F32)
    for n in range(count):
        tile = tile + jnp.where(lane == 112 + n, rows_s[:, n : n + 1], 0.0)
    for n, ref in ((120, lower_s), (121, upper_s)):
        column = jnp.sum(
            jnp.where(eye, jnp.broadcast_to(ref[...], (count, count)), 0.0), axis=1, keepdims=True
        )
        tile = tile + jnp.where(lane == n, column, 0.0)
    coefs_o[0:24, :] = jnp.zeros((24, LANES), F32)
    coefs_o[24:32, :] = tile


def k_first(place, shared, g0, g1, g2, g3, neumann, avg, r_o, share_o, prim_o, t_o, *sends):
    at = Place(place)
    rhs = r_o.shape[0]
    full = assembled(shared[...], (g0, g1, g2, g3), at, shared.shape[0], keep=False)
    share = shared[rhs : rhs + 1, :] / full[rhs : rhs + 1]
    south, north, west, east = faces_of(full[:rhs])
    r = jnp.concatenate([south * at.keep_south, north * at.keep_north, west, east], axis=1)
    r_o[...] = r
    share_o[...] = share
    weighted = share * r
    prim_o[...] = mm_t(avg[...], weighted)
    t = jnp.concatenate([share * product(weighted, held(neumann)), share * avg[...]], axis=0)
    t_o[...] = t
    put_sends(sends, t, at)


def k_schur(
    place, t, g0, g1, g2, g3, diag, couple, blocks, z_o, q_o, s0, s1, s2, s3, z_s, sem, *, rhs
):
    at = Place(place)
    z = assembled(t[...], (g0, g1, g2, g3), at, rhs)
    z_s[...] = z
    copy = pltpu.make_async_copy(z_s, z_o, sem.at[0])
    copy.start()
    q = schur(z, diag[...], held(couple), held(blocks))
    q_o[...] = q
    put_sends((s0, s1, s2, s3), q, at)
    copy.wait()


def k_second(place, q, g2, g3, g0, g1, r, share, neumann, avg, v_o, t_o, pr_o, *sends):
    at = Place(place)
    rhs = r.shape[0]
    w = assembled(q[...], (g0, g1, g2, g3), at, rhs)
    v = jnp.concatenate([w[:rhs] - SHIFT * r[...], w[rhs:]], axis=0)
    v_o[...] = v
    weighted = share[...] * v
    pr_o[...] = jnp.concatenate(
        [mm_t(avg[...], weighted[:rhs]), mm_t(avg[...], weighted[rhs:])], axis=1
    )
    t = share[...] * product(weighted, held(neumann))
    t_o[...] = t
    put_sends(sends, t, at)


def k_third(place, q, g0, g1, g2, g3, v, share, avg, prim0, prim1, v2_o, pay_o, v2_s, sem):
    at = Place(place)
    rhs = prim0.shape[1]
    w = assembled(q[...], (g0, g1, g2, g3), at, rhs)
    zero = jnp.zeros((16, w.shape[1]), F32)
    older = jnp.concatenate([v[...][:rhs], zero, v[...][rhs:], zero], axis=0)
    v2 = w - SHIFT * older
    v2_s[...] = v2
    copies = begin(v2_s, v2_o, sem, 4)
    weighted = share[...] * v2
    prim2 = mm_t(avg[...], weighted[:rhs])
    reach2 = mm_t(avg[...], weighted[rhs:])
    reach1 = prim1[...][:, rhs:]
    spare = jnp.zeros((8, LANES - reach1.shape[1] - reach2.shape[1]), F32)
    tail = jnp.concatenate([reach1, reach2, spare], axis=1)
    pay = jnp.concatenate([prim0[...], prim1[...][:, :rhs], prim2, tail], axis=0)
    for item in range(pay_o.shape[0]):
        pay_o[item] = pay
    finish(copies)


def summed(got):
    total = got[0]
    for item in range(1, got.shape[0]):
        total = total + got[item]
    return total


def k_sum_spread(got, coefs, out):
    total = summed(got) + coefs[...]
    for item in range(out.shape[0]):
        out[item] = total


def banded_product(pieces, value):
    first, second = cut(value, 2)
    return (narrow(pieces[1], first) + narrow(pieces[0], second)) + narrow(pieces[0], first)


def coarse_rows(totals, lowers, uppers):
    carry = jnp.zeros_like(totals[0])
    smooth = []
    for low, value in zip(lowers, [(1.0 - low) * value for low, value in zip(lowers, totals)]):
        carry = low * carry + value
        smooth.append(carry)
    carry = jnp.zeros_like(totals[0])
    tops = []
    smooth = [(1.0 - up) * value for up, value in zip(uppers, smooth)]
    for up, value in zip(uppers[::-1], smooth[::-1]):
        carry = up * carry + value
        tops.append(carry)
    return tops[::-1]


def k_fourth(place, v2, share, neumann, t_o, s0, s1, s2, s3, v2_s, t_s, sem):
    at = Place(place)
    finish(begin(v2, v2_s, sem.at[0], 4))
    t = share[...] * product(share[...] * v2_s[...], held(neumann))
    t_s[...] = t
    copies = begin(t_s, t_o, sem.at[1], 4)
    put_sends((s0, s1, s2, s3), t, at)
    finish(copies)


def lift(coefs, basis):
    spare = -coefs.shape[0] % 16
    if spare:
        coefs = jnp.concatenate([coefs, jnp.zeros((spare, coefs.shape[1]), F32)], axis=0)
        basis = jnp.concatenate([basis, jnp.zeros((spare, basis.shape[1]), F32)], axis=0)
    c, b = cut(coefs, 2), cut(basis, 2)

    def times(x, y):
        return lax.dot_general(x, y, (((0,), (0,)), ((), ())), preferred_element_type=F32)

    return (times(c[1], b[0]) + times(c[0], b[1])) + times(c[0], b[0])


def k_core(
    place, mine, other, t, g0, g1, g2, g3, z0, v1, z1, v2, r, diag, couple, blocks,
    z0_o, z1_o, z2_o, w0_o, w1_o, q_o, pay_o, s0, s1, s2, s3,
    band0, band1, band2, c0_s, c1_s, c2_s, full_s, t_s, z1_s, v2_s, sem, in_sem,
):
    at = Place(place)
    loads = []
    for n, (source, target) in enumerate(((z1, z1_s), (v2, v2_s), (t, t_s))):
        loads += begin(source, target, in_sem.at[n], 2)
    t, z1, v2 = t_s, z1_s, v2_s
    rhs = r.shape[0]
    rows = 2 * mine.shape[0]
    width = band0.shape[1]
    lane = lax.broadcasted_iota(jnp.int32, (8, width), 1)
    lowers, uppers = [], []
    for ref in (band0, band1, band2):
        if ref.shape[0] > rows * 8:
            ref[rows * 8 :, :] = jnp.zeros((ref.shape[0] - rows * 8, width), F32)
    pays = []
    for k in range(rows // 2):
        pays.append(jnp.where(at.even_row, mine[k], other[k]))
        pays.append(jnp.where(at.even_row, other[k], mine[k]))
    point = lax.broadcasted_iota(jnp.int32, (8, width), 0)
    units = []
    for k in range(rows):
        tail = pays[k][24:32]
        lowers.append(jnp.broadcast_to(tail[:, 120:121], (8, width)))
        uppers.append(jnp.broadcast_to(tail[:, 121:122], (8, width)))
        units.append(jnp.where(lane == point + 8 * k, 1.0, 0.0).astype(F32))
    tops = coarse_rows(units, lowers, uppers)
    for k in range(rows):
        wide = pays[k][24:32]
        if width > LANES:
            wide = jnp.concatenate([wide, jnp.zeros((8, width - LANES), F32)], axis=1)
        for ref, first, last, to in (
            (band1, 0, 40, 8 * (k - 2)),
            (band2, 40, 112, 8 * (k - 4)),
            (band0, 112, 120, 8 * k),
        ):
            picked = jnp.where((lane >= first) & (lane < last), wide, 0.0)
            placed = pltpu.roll(picked, (to - first) % width, 1)
            ref[8 * k : 8 * k + 8, :] = placed + tops[k] if ref is band0 else placed

    def stacked(tiles):
        if width > rows * 8:
            tiles = tiles + [jnp.zeros((width - rows * 8, rhs), F32)]
        return jnp.concatenate(tiles, axis=0)

    own, near, wide = [cut(ref[...], 2) for ref in (band0, band1, band2)]

    def solve(total):
        return banded_product(own, total)

    edge = jnp.zeros((40, rhs), F32)
    c0 = solve(stacked([part[0:8] for part in pays]))
    c1 = solve(stacked([part[8:16] for part in pays]) + banded_product(near, c0))
    c2 = solve(
        stacked([part[16:24] for part in pays])
        + banded_product(wide, c0)
        + banded_product(near, c1)
    )
    for ref, value in ((c0_s, c0), (c1_s, c1), (c2_s, c2)):
        ref[0:40, :] = edge
        ref[40 : 40 + width, :] = value
        ref[40 + width :, :] = edge
    start = at.row * 8
    c0 = c0_s[pl.ds(pl.multiple_of(start, 8), 88), :]
    c1 = c1_s[pl.ds(pl.multiple_of(start + 16, 8), 56), :]
    c2 = c2_s[pl.ds(pl.multiple_of(start + 32, 8), 24), :]
    r0 = r[...]
    z0f = z0[:rhs, :] + lift(c0[32:56], z0[rhs:, :])
    v1f = v1[:rhs, :] + lift(c0[24:64], v1[rhs:, :])
    finish(loads[0:2])
    z1f = z1[:rhs, :] + lift(
        jnp.concatenate([c0[16:72], c1[16:40]], axis=0),
        jnp.concatenate([z1[rhs:, :], z0[rhs:, :]], axis=0),
    )
    finish(loads[2:4])
    v2f = v2[:rhs, :] + lift(
        jnp.concatenate([c0[8:80], c1[8:48]], axis=0),
        jnp.concatenate([v2[rhs:, :], v1[rhs:, :]], axis=0),
    )
    copies = []

    def keep(n, value, out):
        full_s[n] = value
        copies.extend(begin(full_s.at[n], out, sem.at[n], 2))

    keep(0, z0f, z0_o)
    keep(1, z1f, z1_o)
    keep(2, v1f + SHIFT * r0, w0_o)
    keep(3, v2f + SHIFT * v1f, w1_o)
    finish(loads[4:6])
    z2 = assembled(t[...], (g0, g1, g2, g3), at, rhs)
    z2f = z2[:rhs] + lift(
        jnp.concatenate([c0, c1, c2], axis=0),
        jnp.concatenate([z2[rhs:], z1[rhs:, :], z0[rhs:, :]], axis=0),
    )
    keep(4, z2f, z2_o)
    q = schur(z2f, diag[...], held(couple), held(blocks))
    q_o[...] = q
    put_sends((s0, s1, s2, s3), q, at)
    table = dot_rows(
        [(r0, z0f), (r0, z1f), (v1f, z0f), (v1f, z1f), (v2f, z1f)]
        + [(r0, z2f), (v1f, z2f), (v2f, z2f), (z2f, q + q)]
    )
    line = jnp.concatenate([table[i : i + 1] for i in range(9)], axis=1)
    for item in range(pay_o.shape[0]):
        pay_o[item] = line
    finish(copies)


def dot_rows(pairs):
    parts = []
    for a, b in pairs:
        faces = faces_of(a * b)
        parts.append((faces[0] + faces[1]) + (faces[2] + faces[3]))
    wide = jnp.concatenate(parts, axis=1)
    shape = (16, wide.shape[1])
    pick = jnp.where(
        lax.broadcasted_iota(jnp.int32, shape, 0) == lax.broadcasted_iota(jnp.int32, shape, 1) // LANES,
        1.0,
        0.0,
    ).astype(BF16)
    high, middle, low = [narrow(pick, piece, True) for piece in cut(wide, 3)]
    return (low + middle) + high


def k_final(
    place, got, q, g0, g1, g2, g3, order, r0, z0, z1, z2, w0, w1, x_o, r_o, full_s, both_s, sem, out_sem
):
    loads = []
    for n, source in enumerate((z2, w0, w1)):
        loads += begin(source, full_s.at[n], sem.at[n], 2)
    w2 = assembled(q[...], (g0, g1, g2, g3), Place(place), q.shape[0])
    total = summed(got)
    v0z0, v0z1, v1z0, v1z1, v2z1, v0z2, v1z2, v2z2, z2w2 = [
        total[:, i * LANES : (i + 1) * LANES] for i in range(9)
    ]
    z1w0 = v1z1 + SHIFT * v0z1
    z2w0 = v1z2 + SHIFT * v0z2
    z2w1 = v2z2 + SHIFT * v1z2
    zw = [
        [v1z0 + SHIFT * v0z0, z1w0, z2w0],
        [z1w0, v2z1 + SHIFT * v1z1, z2w1],
        [z2w0, z2w1, z2w2],
    ]
    vz = [[v0z0, v0z1, v0z2], [v1z0, v1z1, v1z2], [z1w0 - SHIFT * v1z0, v2z1, v2z2]]

    def form(left, table, right):
        value = None
        for i, a in enumerate(left):
            for j, b in enumerate(right):
                if a is None or b is None:
                    continue
                term = a * table[i][j] * b
                value = term if value is None else value + term
        return value

    one = jnp.ones_like(vz[0][0])
    zero = jnp.zeros_like(one)
    toward = [one, None, None]
    steps = [zero, zero, zero]
    drops = [zero, zero, zero]
    rz = vz[0][0]
    for iteration in range(3):
        alpha = rz / form(toward, zw, toward)
        for j in range(3):
            if toward[j] is not None:
                steps[j] = steps[j] + alpha * toward[j]
                drops[j] = drops[j] - alpha * toward[j]
        if iteration < 2:
            mix = [one + SHIFT * drops[0], drops[0] + SHIFT * drops[1], None]
            if iteration == 1:
                mix[2] = drops[1]
            new = form(mix, vz, mix)
            beta = new / rz
            toward = [
                m if d is None else (beta * d if m is None else m + beta * d)
                for m, d in zip(mix, toward)
            ]
            rz = new
    table = jnp.concatenate(steps + drops + [zero, zero], axis=0)
    eye = jnp.where(
        lax.broadcasted_iota(jnp.int32, (LANES, LANES), 0)
        == lax.broadcasted_iota(jnp.int32, (LANES, LANES), 1),
        1.0,
        0.0,
    ).astype(F32)
    columns = mm_t(eye, table)
    col = [columns[:, i : i + 1] for i in range(6)]
    hots = one_hot_faces(order[...])
    finish(loads)
    x = col[0] * z0[...] + col[1] * z1[...] + col[2] * full_s[0]
    both_s[0] = to_points(x, hots)
    copies = begin(both_s.at[0], x_o, out_sem.at[0], 2)
    r = r0[...] + col[3] * full_s[1] + col[4] * full_s[2] + col[5] * w2
    both_s[1] = to_points(r, hots)
    copies += begin(both_s.at[1], r_o, out_sem.at[1], 2)
    finish(copies)


def call(body, outs, place, *args, scratch=(), raw=(), raw_outs=(), flops=1_000_000):
    args = tuple(
        pltpu.with_memory_space_constraint(arg, pltpu.HBM) if n in raw else arg
        for n, arg in enumerate(args)
    )
    space = [pltpu.HBM if n in raw else pltpu.VMEM for n in range(len(args))]
    specs = [pl.BlockSpec(memory_space=kind) for kind in space]
    if place is not None:
        specs = [pl.BlockSpec(memory_space=pltpu.SMEM)] + specs
        args = (place,) + args
    return pl.pallas_call(
        body,
        out_shape=[
            out
            if isinstance(out, jax.ShapeDtypeStruct)
            else (pltpu.HBM(out, F32) if n in raw_outs else jax.ShapeDtypeStruct(out, F32))
            for n, out in enumerate(outs)
        ],
        in_specs=specs,
        out_specs=[
            pl.BlockSpec(memory_space=pltpu.HBM if n in raw_outs else pltpu.VMEM)
            for n in range(len(outs))
        ],
        scratch_shapes=list(scratch),
        compiler_params=pltpu.CompilerParams(vmem_limit_bytes=16 * 1024 * 1024),
        cost_estimate=pl.CostEstimate(flops=flops, bytes_accessed=1_000_000, transcendentals=0),
    )(*args)


def exchange_columns(sends, columns):
    near = [(i, i ^ 1) for i in range(columns)]
    far = [(i, (i + 1 if i % 2 else i - 1) % columns) for i in range(columns)]
    return [lax.ppermute(sends[0], "circ", far), lax.ppermute(sends[1], "circ", near)]


def exchange_rows(sends, rows):
    core = [(i, i ^ 1) for i in range(rows)]
    link = [(i, i + 1 if i % 2 else i - 1) for i in range(1, rows - 1)]
    return [lax.ppermute(sends[2], "axial", link), lax.ppermute(sends[3], "axial", core)]


def exchange(sends, rows, columns):
    return exchange_columns(sends, columns) + exchange_rows(sends, rows)


def spread(value, axis, groups=None):
    return lax.all_to_all(
        value, axis, split_axis=0, concat_axis=0, tiled=True, axis_index_groups=groups
    )


def local(
    load_terms, diffusivity, interface_diag, coupling, interior_inverse, neumann_solve,
    row_coarse, lower_coef, upper_coef, face_order, primal_lists,
):
    rows, columns = lax.axis_size("axial"), lax.axis_size("circ")
    rhs, points = load_terms.shape[2], load_terms.shape[3]
    place = jnp.stack(
        [lax.axis_index("axial"), jnp.int32(rows), lax.axis_index("circ")]
    ).astype(jnp.int32)
    swap = functools.partial(exchange, rows=rows, columns=columns)
    dma = pltpu.SemaphoreType.DMA

    def face(n):
        return [(n, LANES)] * 4

    def bf16(*shape):
        return jax.ShapeDtypeStruct((PIECES,) + shape, BF16)

    shared, order, *sends, neumann = call(
        k_prepare,
        [(rhs + 8, points), jax.ShapeDtypeStruct((1, points), jnp.int32)]
        + face(rhs + 8)
        + [(points, points)],
        place, load_terms[0, 0], diffusivity[0], face_order[0], neumann_solve[0, 0],
        raw=(0, 1, 2, 3),
        scratch=[
            pltpu.VMEM((rhs, points), F32),
            pltpu.VMEM((1, points), F32),
            dma((3,)),
            dma((4,)),
        ],
    )
    got = swap(sends)
    neumann, avg, couple = call(
        k_neumann,
        [bf16(points, points), (8, points), (points, points)],
        None, order, neumann, primal_lists[0, 0], coupling[0, 0],
        raw=(2, 3),
        scratch=[
            pltpu.VMEM(primal_lists.shape[2:], jnp.int32),
            dma((5,)),
        ],
        flops=2_000_000_000,
    )
    r0, share, prim0, t0, *sends = call(
        k_first,
        [(rhs, points), (1, points), (8, rhs), (rhs + 8, points)] + face(rhs + 8),
        place, shared, *got, neumann, avg,
    )
    got = swap(sends)
    inner = interior_inverse.shape[2:]
    diag, couple, blocks, coefs = call(
        k_couple,
        [(1, points), bf16(points, points), bf16(*inner), (32, LANES)],
        None, order, share, couple, interface_diag[0], interior_inverse[0, 0],
        row_coarse[0], lower_coef, upper_coef,
        raw=(3, 4, 5, 6, 7),
        scratch=[
            pltpu.VMEM((1, points), F32),
            pltpu.VMEM(inner, F32),
            pltpu.VMEM(row_coarse.shape[1:], F32),
            pltpu.VMEM(lower_coef.shape, F32),
            pltpu.VMEM(upper_coef.shape, F32),
            dma((9,)),
        ],
        flops=2_000_000_000,
    )
    n = rhs + 24
    z0, q0, *sends = call(
        functools.partial(k_schur, rhs=rhs), [(n, points)] * 2 + face(n),
        place, t0, *got, diag, couple, blocks,
        raw_outs=(0,), scratch=[pltpu.VMEM((n, points), F32), dma((1,))],
    )
    got = swap(sends)
    n = rhs + 40
    v1, t1, prim1, *sends = call(
        k_second, [(n, points)] * 2 + [(8, n)] + face(n), place, q0, *got[2:], *got[:2], r0, share, neumann, avg
    )
    got = swap(sends)
    n = rhs + 56
    z1, q1, *sends = call(
        functools.partial(k_schur, rhs=rhs), [(n, points)] * 2 + face(n),
        place, t1, *got, diag, couple, blocks,
        raw_outs=(0,), scratch=[pltpu.VMEM((n, points), F32), dma((1,))],
    )
    got = swap(sends)
    n = rhs + 72
    v2, pay = call(
        k_third, [(n, points), (columns, 32, LANES)], place, q1, *got, v1, share, avg, prim0, prim1,
        raw_outs=(0,), scratch=[pltpu.VMEM((n, points), F32), dma((4,))],
    )
    got = spread(pay, "circ")
    t2, *sends = call(
        k_fourth, [(n, points)] + face(n), place, v2, share, neumann,
        raw=(0,), raw_outs=(0,),
        scratch=[pltpu.VMEM((n, points), F32)] * 2 + [dma((2, 4))],
        flops=500_000_000,
    )
    got, t2 = lax.optimization_barrier((got, t2))
    (pay,) = call(k_sum_spread, [(rows // 2, 32, LANES)], None, got, coefs)
    pay, *sends = lax.optimization_barrier((pay, *sends))
    along = [list(range(core, rows, 2)) for core in range(2)]
    mine = spread(pay, "axial", along)
    mine, *got = lax.optimization_barrier((mine, *swap(sends)))
    other = lax.ppermute(mine, "axial", [(i, i ^ 1) for i in range(rows)])
    width = max(LANES, 8 * rows)
    z0f, z1f, z2f, w0f, w1f, q2, pay, *sends = call(
        k_core,
        [(rhs, points)] * 6 + [(2 * columns, 1, 9 * LANES)] + face(rhs),
        place, mine, other, t2, *got, z0, v1, z1, v2, r0, diag, couple, blocks,
        raw=(2, 9, 10),
        raw_outs=(0, 1, 2, 3, 4),
        scratch=[pltpu.VMEM((width, width), F32)] * 3
        + [pltpu.VMEM((width + 80, rhs), F32)] * 3
        + [pltpu.VMEM((5, rhs, points), F32)]
        + [pltpu.VMEM((rhs + m, points), F32) for m in (72, 56, 72)]
        + [dma((5, 2)), dma((3, 2))],
    )
    chips = [
        [row * columns + column for row in (pair, pair + 1) for column in range(columns)]
        for pair in range(0, rows, 2)
    ]
    dots = spread(pay, ("axial", "circ"), chips)
    got = exchange_columns(sends, columns)
    dots, *got = lax.optimization_barrier((dots, *got))
    blank = jnp.zeros((1, 9 * LANES), F32)
    (pay,) = call(k_sum_spread, [(rows // 2, 1, 9 * LANES)], None, dots, blank)
    pay, *sends = lax.optimization_barrier((pay, *sends))
    dots = spread(pay, "axial", along)
    got = got + exchange_rows(sends, rows)
    x, r = call(
        k_final, [(rhs, points)] * 2,
        place, dots, q2, *got, order, r0, z0f, z1f, z2f, w0f, w1f,
        raw=(10, 11, 12),
        raw_outs=(0, 1),
        scratch=[
            pltpu.VMEM((3, rhs, points), F32),
            pltpu.VMEM((2, rhs, points), F32),
            dma((3, 2)),
            dma((2, 2)),
        ],
    )
    return (x[None, None], r[None, None])


def solution(mesh):
    in_specs = (
        P("axial", "circ", None, None),
        P("axial", "circ", None),
        P("axial", "circ", None),
        P("axial", "circ", None, None),
        P("axial", "circ", None, None, None),
        P("axial", "circ", None, None),
        P("axial", None, None),
        P("axial", None),
        P("axial", None),
        P("axial", "circ", None),
        P("axial", "circ", None, None),
    )
    out_specs = (P("axial", "circ", None, None), P("axial", "circ", None, None))
    return jax.shard_map(local, mesh=mesh, in_specs=in_specs, out_specs=out_specs, check_vma=False)
```

```python
import functools

import jax
import jax.numpy as jnp
from jax import lax
from jax.experimental import pallas as pl
from jax.experimental.pallas import tpu as pltpu
from jax.sharding import PartitionSpec as P

SHIFT = 12.0
HIGHEST = lax.Precision.HIGHEST
F32 = jnp.float32
BF16 = jnp.bfloat16
LANES = 128
PIECES = 2


def mm_t(a, b):
    return lax.dot_general(
        a, b, (((1,), (1,)), ((), ())), precision=HIGHEST, preferred_element_type=F32
    )


def cut(value, count):
    pieces = []
    for _ in range(count):
        piece = value.astype(BF16)
        pieces.append(piece)
        value = value - piece.astype(F32)
    return pieces


def narrow(a, b, transposed=False):
    return lax.dot_general(
        a, b, (((1,), (1 if transposed else 0,)), ((), ())), preferred_element_type=F32
    )


def product(a, pieces, transposed=False):
    count = a.shape[0]
    levels = len(pieces)
    if count % 16:
        a = jnp.concatenate([a, jnp.zeros((16 - count % 16, a.shape[1]), F32)], axis=0)
    tall = a.shape[0]
    left = cut(a, levels)
    by_level = [None] * levels
    for n, piece in enumerate(pieces):
        used = left[: levels - n]
        stack = used[0] if len(used) == 1 else jnp.concatenate(used, axis=0)
        out = narrow(stack, piece, transposed)
        for m in range(len(used)):
            part = out[m * tall : (m + 1) * tall]
            level = n + m
            by_level[level] = part if by_level[level] is None else by_level[level] + part
    total = by_level[-1]
    for part in by_level[-2::-1]:
        total = total + part
    return total[:count]


def select_columns(a, hot, transposed):
    count = a.shape[0]
    if count % 16:
        a = jnp.concatenate([a, jnp.zeros((16 - count % 16, a.shape[1]), F32)], axis=0)
    tall = a.shape[0]
    out = narrow(jnp.concatenate(cut(a, 3), axis=0), hot, transposed)
    return ((out[2 * tall :] + out[tall : 2 * tall]) + out[:tall])[:count]


def faces_of(full):
    return [full[:, f * LANES : (f + 1) * LANES] for f in range(4)]


def one_hot_faces(order):
    rows = lax.broadcasted_iota(jnp.int32, (LANES, LANES), 0)
    return [
        jnp.where(order[:, f * LANES : (f + 1) * LANES] - f * LANES == rows, 1.0, 0.0)
        .astype(F32)
        .astype(BF16)
        for f in range(4)
    ]


def to_shared(full, hots):
    return jnp.concatenate(
        [select_columns(part, hot, True) for part, hot in zip(faces_of(full), hots)], axis=1
    )


def to_points(full, hots):
    return jnp.concatenate(
        [select_columns(part, hot, False) for part, hot in zip(faces_of(full), hots)], axis=1
    )


class Place:
    def __init__(self, place):
        row, rows, column = place[0], place[1], place[2]
        self.row = row
        self.even_row = lax.rem(row, 2) == 0
        self.even_column = lax.rem(column, 2) == 0
        self.keep_south = jnp.where(row > 0, 1.0, 0.0).astype(F32)
        self.keep_north = jnp.where(row < rows - 1, 1.0, 0.0).astype(F32)


def put_sends(sends, full, at):
    south, north, west, east = faces_of(full)
    sends[0][...] = jnp.where(at.even_column, west, east)
    sends[1][...] = jnp.where(at.even_column, east, west)
    sends[2][...] = jnp.where(at.even_row, south, north)
    sends[3][...] = jnp.where(at.even_row, north, south)


def neighbours(got, at):
    far, near, link, core = [ref[...] for ref in got]
    above = jnp.where(at.even_row, core, link)
    below = jnp.where(at.even_row, link, core)
    right = jnp.where(at.even_column, near, far)
    left = jnp.where(at.even_column, far, near)
    return below, above, left, right


def assembled(full, got, at, rhs, keep=True):
    count = full.shape[0]
    extra = count - rhs
    own = faces_of(full)
    other = neighbours(got, at)
    scale = (at.keep_south, at.keep_north, None, None)
    shift = (0, 16, 8, 8)
    out = []
    for f in range(4):
        part = own[f][:rhs] + other[f][:rhs]
        if extra:
            zero = jnp.zeros((8, LANES), F32)
            mine = jnp.concatenate([zero, own[f][rhs:], zero], axis=0)
            pieces = [jnp.zeros((shift[f], LANES), F32)] if shift[f] else []
            pieces.append(other[f][rhs:])
            if shift[f] < 16:
                pieces.append(jnp.zeros((16 - shift[f], LANES), F32))
            part = jnp.concatenate([part, mine + jnp.concatenate(pieces, axis=0)], axis=0)
        if keep and scale[f] is not None:
            part = part * scale[f]
        out.append(part)
    return jnp.concatenate(out, axis=1)


def held(ref):
    return [ref[n] for n in range(ref.shape[0])]


def averages(avg, value):
    pick = jnp.concatenate([avg, jnp.zeros_like(avg)], axis=0).astype(BF16)
    high, middle, low = [narrow(pick, piece, True) for piece in cut(value, 3)]
    return ((low + middle) + high)[: avg.shape[0]]


def schur(z, diag, couple, blocks):
    inner = product(z, couple)
    solved = jnp.concatenate(
        [
            product(part, [piece[n] for piece in blocks])
            for n, part in enumerate(faces_of(inner))
        ],
        axis=1,
    )
    return diag * z - product(solved, couple, True)


def begin(source, target, sems, parts):
    rows = source.shape[0] // 8
    edges = [8 * (rows * n // parts) for n in range(parts)] + [source.shape[0]]
    copies = []
    for n in range(parts):
        band = pl.ds(edges[n], edges[n + 1] - edges[n])
        copies.append(pltpu.make_async_copy(source.at[band], target.at[band], sems.at[n]))
        copies[n].start()
    return copies


def finish(copies):
    for copy in copies:
        copy.wait()


def k_prepare(
    place, load, rho, order, neumann, shared_o, order_o, s0, s1, s2, s3, neumann_o, load_s, rho_s, sem, far_sem
):
    at = Place(place)
    copies = [
        pltpu.make_async_copy(source, target, sem.at[n])
        for n, (source, target) in enumerate(((order, order_o), (load, load_s), (rho, rho_s)))
    ]
    for copy in copies:
        copy.start()
    ahead = begin(neumann, neumann_o, far_sem, 4)
    copies[0].wait()
    hots = one_hot_faces(order_o[...])
    copies[1].wait()
    copies[2].wait()
    pad = jnp.zeros((7, rho_s.shape[1]), F32)
    full = to_shared(jnp.concatenate([load_s[...], rho_s[...], pad], axis=0), hots)
    shared_o[...] = full
    put_sends((s0, s1, s2, s3), full, at)
    finish(ahead)


def k_neumann(order, neumann_s, lists, couple, neumann_o, avg_o, couple_o, lists_s, sem):
    listed = pltpu.make_async_copy(lists, lists_s, sem.at[4])
    listed.start()
    ahead = begin(couple, couple_o, sem, 4)
    hots = one_hot_faces(order[...])
    points = order.shape[1]
    listed.wait()
    named = lists_s[...]
    position = lax.broadcasted_iota(jnp.int32, (8, points), 1)
    total = jnp.zeros((8, points), F32)
    length = named.shape[1]
    for item in range(length):
        total = total + jnp.where(named[:, item : item + 1] == position, 1.0, 0.0)
    avg_o[...] = to_shared(total * (1.0 / length), hots)
    tall = jnp.concatenate(cut(neumann_s[...], PIECES), axis=0)
    half = jnp.concatenate(
        [narrow(part, hot, True).astype(BF16) for part, hot in zip(faces_of(tall), hots)], axis=1
    )
    for n in range(PIECES):
        for f in range(4):
            first = n * points + f * LANES
            neumann_o[n, f * LANES : (f + 1) * LANES, :] = narrow(
                hots[f], half[first : first + LANES]
            ).astype(BF16)
    finish(ahead)


def k_couple(
    order, after, couple_s, diag, blocks, row_coarse, lower, upper,
    diag_o, couple_o, blocks_o, coefs_o,
    diag_s, blocks_s, rows_s, lower_s, upper_s, sem,
):
    copies = [None] * 4
    copies.append(pltpu.make_async_copy(blocks, blocks_s, sem.at[4]))
    copies.append(pltpu.make_async_copy(diag, diag_s, sem.at[5]))
    copies.append(pltpu.make_async_copy(row_coarse, rows_s, sem.at[6]))
    copies.append(pltpu.make_async_copy(lower, lower_s, sem.at[7]))
    copies.append(pltpu.make_async_copy(upper, upper_s, sem.at[8]))
    for copy in copies[4:]:
        copy.start()
    hots = one_hot_faces(order[...])
    copies[5].wait()
    diag_o[...] = to_shared(jnp.broadcast_to(diag_s[...], (8, diag_s.shape[1])), hots)[:1]
    for f in range(4):
        rows = slice(f * LANES, (f + 1) * LANES)
        for n, piece in enumerate(cut(couple_s[rows, :], PIECES)):
            couple_o[n, rows, :] = narrow(hots[f], piece).astype(BF16)
    copies[4].wait()
    for f in range(4):
        for n, piece in enumerate(cut(blocks_s[f], PIECES)):
            blocks_o[n, f] = piece
    for n in (6, 7, 8):
        copies[n].wait()
    count = lower_s.shape[1]
    lane = lax.broadcasted_iota(jnp.int32, (count, LANES), 1)
    eye = lax.broadcasted_iota(jnp.int32, (count, count), 0) == lax.broadcasted_iota(
        jnp.int32, (count, count), 1
    )
    tile = jnp.zeros((count, LANES), F32)
    for n in range(count):
        tile = tile + jnp.where(lane == 112 + n, rows_s[:, n : n + 1], 0.0)
    for n, ref in ((120, lower_s), (121, upper_s)):
        column = jnp.sum(
            jnp.where(eye, jnp.broadcast_to(ref[...], (count, count)), 0.0), axis=1, keepdims=True
        )
        tile = tile + jnp.where(lane == n, column, 0.0)
    coefs_o[0:24, :] = jnp.zeros((24, LANES), F32)
    coefs_o[24:32, :] = tile


def k_first(place, shared, g0, g1, g2, g3, neumann, avg, r_o, share_o, prim_o, t_o, *sends):
    at = Place(place)
    rhs = r_o.shape[0]
    full = assembled(shared[...], (g0, g1, g2, g3), at, shared.shape[0], keep=False)
    share = shared[rhs : rhs + 1, :] / full[rhs : rhs + 1]
    south, north, west, east = faces_of(full[:rhs])
    r = jnp.concatenate([south * at.keep_south, north * at.keep_north, west, east], axis=1)
    r_o[...] = r
    share_o[...] = share
    weighted = share * r
    prim_o[...] = averages(avg[...], weighted)
    t = jnp.concatenate([share * product(weighted, held(neumann)), share * avg[...]], axis=0)
    t_o[...] = t
    put_sends(sends, t, at)


def k_schur(
    place, t, g0, g1, g2, g3, diag, couple, blocks, z_o, q_o, s0, s1, s2, s3, z_s, sem, *, rhs
):
    at = Place(place)
    z = assembled(t[...], (g0, g1, g2, g3), at, rhs)
    z_s[...] = z
    copy = pltpu.make_async_copy(z_s, z_o, sem.at[0])
    copy.start()
    q = schur(z, diag[...], held(couple), held(blocks))
    q_o[...] = q
    put_sends((s0, s1, s2, s3), q, at)
    copy.wait()


def k_second(place, q, g2, g3, g0, g1, r, share, neumann, avg, v_o, t_o, pr_o, *sends):
    at = Place(place)
    rhs = r.shape[0]
    w = assembled(q[...], (g0, g1, g2, g3), at, rhs)
    v = jnp.concatenate([w[:rhs] - SHIFT * r[...], w[rhs:]], axis=0)
    v_o[...] = v
    weighted = share[...] * v
    pr_o[...] = jnp.concatenate(
        [averages(avg[...], weighted[:rhs]), averages(avg[...], weighted[rhs:])], axis=1
    )
    t = share[...] * product(weighted, held(neumann))
    t_o[...] = t
    put_sends(sends, t, at)


def k_third(place, q, g0, g1, g2, g3, v, share, avg, prim0, prim1, v2_o, pay_o, v2_s, sem):
    at = Place(place)
    rhs = prim0.shape[1]
    w = assembled(q[...], (g0, g1, g2, g3), at, rhs)
    fields = w[:rhs] - SHIFT * v[:rhs, :]
    v2_s[0:rhs, :] = fields
    copies = begin(v2_s.at[0:rhs], v2_o.at[0:rhs], sem.at[0], 2)
    prim2 = averages(avg[...], share[...] * fields)
    zero = jnp.zeros((16, w.shape[1]), F32)
    basis = w[rhs:] - SHIFT * jnp.concatenate([zero, v[rhs:, :], zero], axis=0)
    v2_s[rhs:, :] = basis
    copies += begin(v2_s.at[rhs:], v2_o.at[rhs:], sem.at[1], 2)
    reach2 = averages(avg[...], share[...] * basis)
    reach1 = prim1[...][:, rhs:]
    spare = jnp.zeros((8, LANES - reach1.shape[1] - reach2.shape[1]), F32)
    tail = jnp.concatenate([reach1, reach2, spare], axis=1)
    pay = jnp.concatenate([prim0[...], prim1[...][:, :rhs], prim2, tail], axis=0)
    for item in range(pay_o.shape[0]):
        pay_o[item] = pay
    finish(copies)


def summed(got):
    total = got[0]
    for item in range(1, got.shape[0]):
        total = total + got[item]
    return total


def k_sum_spread(got, coefs, out):
    total = summed(got) + coefs[...]
    for item in range(out.shape[0]):
        out[item] = total


def banded_product(pieces, value):
    first, second = cut(value, 2)
    return (narrow(pieces[1], first) + narrow(pieces[0], second)) + narrow(pieces[0], first)


def coarse_rows(totals, lowers, uppers):
    carry = jnp.zeros_like(totals[0])
    smooth = []
    for low, value in zip(lowers, [(1.0 - low) * value for low, value in zip(lowers, totals)]):
        carry = low * carry + value
        smooth.append(carry)
    carry = jnp.zeros_like(totals[0])
    tops = []
    smooth = [(1.0 - up) * value for up, value in zip(uppers, smooth)]
    for up, value in zip(uppers[::-1], smooth[::-1]):
        carry = up * carry + value
        tops.append(carry)
    return tops[::-1]


def k_fourth(place, v2, share, neumann, t_o, s0, s1, s2, s3, v2_s, t_s, sem):
    at = Place(place)
    half = v2_s.shape[0] // 16 * 8
    bands = (slice(0, half), slice(half, v2_s.shape[0]))
    loads = [begin(v2.at[band], v2_s.at[band], sem.at[n], 2) for n, band in enumerate(bands)]
    copies, done = [], []
    for n, band in enumerate(bands):
        finish(loads[n])
        part = share[...] * product(share[...] * v2_s[band, :], held(neumann))
        t_s[band, :] = part
        copies += begin(t_s.at[band], t_o.at[band], sem.at[2 + n], 2)
        done.append(part)
    put_sends((s0, s1, s2, s3), jnp.concatenate(done, axis=0), at)
    finish(copies)


def lift(coefs, basis):
    spare = -coefs.shape[0] % 16
    if spare:
        coefs = jnp.concatenate([coefs, jnp.zeros((spare, coefs.shape[1]), F32)], axis=0)
        basis = jnp.concatenate([basis, jnp.zeros((spare, basis.shape[1]), F32)], axis=0)
    c, b = cut(coefs, 2), cut(basis, 2)

    def times(x, y):
        return lax.dot_general(x, y, (((0,), (0,)), ((), ())), preferred_element_type=F32)

    return (times(c[1], b[0]) + times(c[0], b[1])) + times(c[0], b[0])


def k_core(
    place, mine, other, t, g0, g1, g2, g3, z0, v1, z1, v2, r, diag, couple, blocks,
    z0_o, z1_o, z2_o, w0_o, w1_o, q_o, pay_o, s0, s1, s2, s3,
    band0, band1, band2, c0_s, c1_s, c2_s, full_s, t_s, z1_s, v2_s, sem, in_sem,
):
    at = Place(place)
    loads = []
    for n, (source, target) in enumerate(((z1, z1_s), (v2, v2_s), (t, t_s))):
        loads += begin(source, target, in_sem.at[n], 2)
    t, z1, v2 = t_s, z1_s, v2_s
    rhs = r.shape[0]
    rows = 2 * mine.shape[0]
    width = band0.shape[1]
    lane = lax.broadcasted_iota(jnp.int32, (8, width), 1)
    lowers, uppers = [], []
    for ref in (band0, band1, band2):
        if ref.shape[0] > rows * 8:
            ref[rows * 8 :, :] = jnp.zeros((ref.shape[0] - rows * 8, width), F32)
    pays = []
    for k in range(rows // 2):
        pays.append(jnp.where(at.even_row, mine[k], other[k]))
        pays.append(jnp.where(at.even_row, other[k], mine[k]))
    for k in range(rows):
        tail = pays[k][24:32]
        lowers.append(jnp.broadcast_to(tail[:, 120:121], (8, rhs)))
        uppers.append(jnp.broadcast_to(tail[:, 121:122], (8, rhs)))
        wide = tail
        if width > LANES:
            wide = jnp.concatenate([tail, jnp.zeros((8, width - LANES), F32)], axis=1)
        for ref, first, last, to in (
            (band1, 0, 40, 8 * (k - 2)),
            (band2, 40, 112, 8 * (k - 4)),
            (band0, 112, 120, 8 * k),
        ):
            picked = jnp.where((lane >= first) & (lane < last), wide, 0.0)
            ref[8 * k : 8 * k + 8, :] = pltpu.roll(picked, (to - first) % width, 1)

    def stacked(tiles):
        if width > rows * 8:
            tiles = tiles + [jnp.zeros((width - rows * 8, rhs), F32)]
        return jnp.concatenate(tiles, axis=0)

    own, near, wide = [cut(ref[...], 2) for ref in (band0, band1, band2)]

    def solve(total):
        tiles = [total[8 * k : 8 * k + 8] for k in range(rows)]
        return stacked(coarse_rows(tiles, lowers, uppers)) + banded_product(own, total)

    edge = jnp.zeros((40, rhs), F32)
    c0 = solve(stacked([part[0:8] for part in pays]))
    c1 = solve(stacked([part[8:16] for part in pays]) + banded_product(near, c0))
    c2 = solve(
        stacked([part[16:24] for part in pays])
        + banded_product(wide, c0)
        + banded_product(near, c1)
    )
    for ref, value in ((c0_s, c0), (c1_s, c1), (c2_s, c2)):
        ref[0:40, :] = edge
        ref[40 : 40 + width, :] = value
        ref[40 + width :, :] = edge
    start = at.row * 8
    c0 = c0_s[pl.ds(pl.multiple_of(start, 8), 88), :]
    c1 = c1_s[pl.ds(pl.multiple_of(start + 16, 8), 56), :]
    c2 = c2_s[pl.ds(pl.multiple_of(start + 32, 8), 24), :]
    r0 = r[...]
    z0f = z0[:rhs, :] + lift(c0[32:56], z0[rhs:, :])
    v1f = v1[:rhs, :] + lift(c0[24:64], v1[rhs:, :])
    finish(loads[0:2])
    z1f = z1[:rhs, :] + lift(
        jnp.concatenate([c0[16:72], c1[16:40]], axis=0),
        jnp.concatenate([z1[rhs:, :], z0[rhs:, :]], axis=0),
    )
    finish(loads[2:4])
    v2f = v2[:rhs, :] + lift(
        jnp.concatenate([c0[8:80], c1[8:48]], axis=0),
        jnp.concatenate([v2[rhs:, :], v1[rhs:, :]], axis=0),
    )
    copies = []

    def keep(n, value, out):
        full_s[n] = value
        copies.extend(begin(full_s.at[n], out, sem.at[n], 2))

    keep(0, z0f, z0_o)
    keep(1, z1f, z1_o)
    keep(2, v1f + SHIFT * r0, w0_o)
    keep(3, v2f + SHIFT * v1f, w1_o)
    finish(loads[4:6])
    z2 = assembled(t[...], (g0, g1, g2, g3), at, rhs)
    z2f = z2[:rhs] + lift(
        jnp.concatenate([c0, c1, c2], axis=0),
        jnp.concatenate([z2[rhs:], z1[rhs:, :], z0[rhs:, :]], axis=0),
    )
    keep(4, z2f, z2_o)
    q = schur(z2f, diag[...], held(couple), held(blocks))
    q_o[...] = q
    put_sends((s0, s1, s2, s3), q, at)
    table = dot_rows(
        [(r0, z0f), (r0, z1f), (v1f, z0f), (v1f, z1f), (v2f, z1f)]
        + [(r0, z2f), (v1f, z2f), (v2f, z2f), (z2f, q + q)]
    )
    line = jnp.concatenate([table[i : i + 1] for i in range(9)], axis=1)
    for item in range(pay_o.shape[0]):
        pay_o[item] = line
    finish(copies)


def dot_rows(pairs):
    parts = []
    for a, b in pairs:
        faces = faces_of(a * b)
        parts.append((faces[0] + faces[1]) + (faces[2] + faces[3]))
    wide = jnp.concatenate(parts, axis=1)
    shape = (16, wide.shape[1])
    pick = jnp.where(
        lax.broadcasted_iota(jnp.int32, shape, 0) == lax.broadcasted_iota(jnp.int32, shape, 1) // LANES,
        1.0,
        0.0,
    ).astype(BF16)
    high, middle, low = [narrow(pick, piece, True) for piece in cut(wide, 3)]
    return (low + middle) + high


def k_final(
    place, got, q, g0, g1, g2, g3, order, r0, z0, z1, z2, w0, w1, x_o, r_o, full_s, both_s, sem, out_sem
):
    loads = []
    for n, source in enumerate((z2, w0, w1)):
        loads += begin(source, full_s.at[n], sem.at[n], 2)
    w2 = assembled(q[...], (g0, g1, g2, g3), Place(place), q.shape[0])
    total = summed(got)
    v0z0, v0z1, v1z0, v1z1, v2z1, v0z2, v1z2, v2z2, z2w2 = [
        total[:, i * LANES : (i + 1) * LANES] for i in range(9)
    ]
    z1w0 = v1z1 + SHIFT * v0z1
    z2w0 = v1z2 + SHIFT * v0z2
    z2w1 = v2z2 + SHIFT * v1z2
    zw = [
        [v1z0 + SHIFT * v0z0, z1w0, z2w0],
        [z1w0, v2z1 + SHIFT * v1z1, z2w1],
        [z2w0, z2w1, z2w2],
    ]
    vz = [[v0z0, v0z1, v0z2], [v1z0, v1z1, v1z2], [z1w0 - SHIFT * v1z0, v2z1, v2z2]]

    def form(left, table, right):
        value = None
        for i, a in enumerate(left):
            for j, b in enumerate(right):
                if a is None or b is None:
                    continue
                term = a * table[i][j] * b
                value = term if value is None else value + term
        return value

    one = jnp.ones_like(vz[0][0])
    zero = jnp.zeros_like(one)
    toward = [one, None, None]
    steps = [zero, zero, zero]
    drops = [zero, zero, zero]
    rz = vz[0][0]
    for iteration in range(3):
        alpha = rz / form(toward, zw, toward)
        for j in range(3):
            if toward[j] is not None:
                steps[j] = steps[j] + alpha * toward[j]
                drops[j] = drops[j] - alpha * toward[j]
        if iteration < 2:
            mix = [one + SHIFT * drops[0], drops[0] + SHIFT * drops[1], None]
            if iteration == 1:
                mix[2] = drops[1]
            new = form(mix, vz, mix)
            beta = new / rz
            toward = [
                m if d is None else (beta * d if m is None else m + beta * d)
                for m, d in zip(mix, toward)
            ]
            rz = new
    table = jnp.concatenate(steps + drops + [zero, zero], axis=0)
    eye = jnp.where(
        lax.broadcasted_iota(jnp.int32, (LANES, LANES), 0)
        == lax.broadcasted_iota(jnp.int32, (LANES, LANES), 1),
        1.0,
        0.0,
    ).astype(F32)
    columns = mm_t(eye, table)
    col = [columns[:, i : i + 1] for i in range(6)]
    hots = one_hot_faces(order[...])
    finish(loads)
    x = col[0] * z0[...] + col[1] * z1[...] + col[2] * full_s[0]
    both_s[0] = to_points(x, hots)
    copies = begin(both_s.at[0], x_o, out_sem.at[0], 2)
    r = r0[...] + col[3] * full_s[1] + col[4] * full_s[2] + col[5] * w2
    both_s[1] = to_points(r, hots)
    copies += begin(both_s.at[1], r_o, out_sem.at[1], 2)
    finish(copies)


def call(body, outs, place, *args, scratch=(), raw=(), raw_outs=(), flops=1_000_000):
    args = tuple(
        pltpu.with_memory_space_constraint(arg, pltpu.HBM) if n in raw else arg
        for n, arg in enumerate(args)
    )
    space = [pltpu.HBM if n in raw else pltpu.VMEM for n in range(len(args))]
    specs = [pl.BlockSpec(memory_space=kind) for kind in space]
    if place is not None:
        specs = [pl.BlockSpec(memory_space=pltpu.SMEM)] + specs
        args = (place,) + args
    return pl.pallas_call(
        body,
        out_shape=[
            out
            if isinstance(out, jax.ShapeDtypeStruct)
            else (pltpu.HBM(out, F32) if n in raw_outs else jax.ShapeDtypeStruct(out, F32))
            for n, out in enumerate(outs)
        ],
        in_specs=specs,
        out_specs=[
            pl.BlockSpec(memory_space=pltpu.HBM if n in raw_outs else pltpu.VMEM)
            for n in range(len(outs))
        ],
        scratch_shapes=list(scratch),
        compiler_params=pltpu.CompilerParams(vmem_limit_bytes=16 * 1024 * 1024),
        cost_estimate=pl.CostEstimate(flops=flops, bytes_accessed=1_000_000, transcendentals=0),
    )(*args)


def exchange_columns(sends, columns):
    near = [(i, i ^ 1) for i in range(columns)]
    far = [(i, (i + 1 if i % 2 else i - 1) % columns) for i in range(columns)]
    return [lax.ppermute(sends[0], "circ", far), lax.ppermute(sends[1], "circ", near)]


def exchange_rows(sends, rows):
    core = [(i, i ^ 1) for i in range(rows)]
    link = [(i, i + 1 if i % 2 else i - 1) for i in range(1, rows - 1)]
    return [lax.ppermute(sends[2], "axial", link), lax.ppermute(sends[3], "axial", core)]


def exchange(sends, rows, columns):
    return exchange_columns(sends, columns) + exchange_rows(sends, rows)


def spread(value, axis, groups=None):
    return lax.all_to_all(
        value, axis, split_axis=0, concat_axis=0, tiled=True, axis_index_groups=groups
    )


def local(
    load_terms, diffusivity, interface_diag, coupling, interior_inverse, neumann_solve,
    row_coarse, lower_coef, upper_coef, face_order, primal_lists,
):
    rows, columns = lax.axis_size("axial"), lax.axis_size("circ")
    rhs, points = load_terms.shape[2], load_terms.shape[3]
    place = jnp.stack(
        [lax.axis_index("axial"), jnp.int32(rows), lax.axis_index("circ")]
    ).astype(jnp.int32)
    swap = functools.partial(exchange, rows=rows, columns=columns)
    dma = pltpu.SemaphoreType.DMA

    def face(n):
        return [(n, LANES)] * 4

    def bf16(*shape):
        return jax.ShapeDtypeStruct((PIECES,) + shape, BF16)

    shared, order, *sends, neumann = call(
        k_prepare,
        [(rhs + 8, points), jax.ShapeDtypeStruct((1, points), jnp.int32)]
        + face(rhs + 8)
        + [(points, points)],
        place, load_terms[0, 0], diffusivity[0], face_order[0], neumann_solve[0, 0],
        raw=(0, 1, 2, 3),
        scratch=[
            pltpu.VMEM((rhs, points), F32),
            pltpu.VMEM((1, points), F32),
            dma((3,)),
            dma((4,)),
        ],
    )
    got = swap(sends)
    neumann, avg, couple = call(
        k_neumann,
        [bf16(points, points), (8, points), (points, points)],
        None, order, neumann, primal_lists[0, 0], coupling[0, 0],
        raw=(2, 3),
        scratch=[
            pltpu.VMEM(primal_lists.shape[2:], jnp.int32),
            dma((5,)),
        ],
        flops=2_000_000_000,
    )
    r0, share, prim0, t0, *sends = call(
        k_first,
        [(rhs, points), (1, points), (8, rhs), (rhs + 8, points)] + face(rhs + 8),
        place, shared, *got, neumann, avg,
    )
    got = swap(sends)
    inner = interior_inverse.shape[2:]
    diag, couple, blocks, coefs = call(
        k_couple,
        [(1, points), bf16(points, points), bf16(*inner), (32, LANES)],
        None, order, share, couple, interface_diag[0], interior_inverse[0, 0],
        row_coarse[0], lower_coef, upper_coef,
        raw=(3, 4, 5, 6, 7),
        scratch=[
            pltpu.VMEM((1, points), F32),
            pltpu.VMEM(inner, F32),
            pltpu.VMEM(row_coarse.shape[1:], F32),
            pltpu.VMEM(lower_coef.shape, F32),
            pltpu.VMEM(upper_coef.shape, F32),
            dma((9,)),
        ],
        flops=2_000_000_000,
    )
    n = rhs + 24
    z0, q0, *sends = call(
        functools.partial(k_schur, rhs=rhs), [(n, points)] * 2 + face(n),
        place, t0, *got, diag, couple, blocks,
        raw_outs=(0,), scratch=[pltpu.VMEM((n, points), F32), dma((1,))],
    )
    got = swap(sends)
    n = rhs + 40
    v1, t1, prim1, *sends = call(
        k_second, [(n, points)] * 2 + [(8, n)] + face(n), place, q0, *got[2:], *got[:2], r0, share, neumann, avg
    )
    got = swap(sends)
    n = rhs + 56
    z1, q1, *sends = call(
        functools.partial(k_schur, rhs=rhs), [(n, points)] * 2 + face(n),
        place, t1, *got, diag, couple, blocks,
        raw_outs=(0,), scratch=[pltpu.VMEM((n, points), F32), dma((1,))],
    )
    got = swap(sends)
    n = rhs + 72
    v2, pay = call(
        k_third, [(n, points), (columns, 32, LANES)], place, q1, *got, v1, share, avg, prim0, prim1,
        raw_outs=(0,), scratch=[pltpu.VMEM((n, points), F32), dma((2, 2))],
    )
    got = spread(pay, "circ")
    t2, *sends = call(
        k_fourth, [(n, points)] + face(n), place, v2, share, neumann,
        raw=(0,), raw_outs=(0,),
        scratch=[pltpu.VMEM((n, points), F32)] * 2 + [dma((4, 2))],
        flops=500_000_000,
    )
    got, t2 = lax.optimization_barrier((got, t2))
    (pay,) = call(k_sum_spread, [(rows // 2, 32, LANES)], None, got, coefs)
    pay, *sends = lax.optimization_barrier((pay, *sends))
    along = [list(range(core, rows, 2)) for core in range(2)]
    mine = spread(pay, "axial", along)
    mine, *got = lax.optimization_barrier((mine, *swap(sends)))
    other = lax.ppermute(mine, "axial", [(i, i ^ 1) for i in range(rows)])
    width = max(LANES, 8 * rows)
    z0f, z1f, z2f, w0f, w1f, q2, pay, *sends = call(
        k_core,
        [(rhs, points)] * 6 + [(2 * columns, 1, 9 * LANES)] + face(rhs),
        place, mine, other, t2, *got, z0, v1, z1, v2, r0, diag, couple, blocks,
        raw=(2, 9, 10),
        raw_outs=(0, 1, 2, 3, 4),
        scratch=[pltpu.VMEM((width, width), F32)] * 3
        + [pltpu.VMEM((width + 80, rhs), F32)] * 3
        + [pltpu.VMEM((5, rhs, points), F32)]
        + [pltpu.VMEM((rhs + m, points), F32) for m in (72, 56, 72)]
        + [dma((5, 2)), dma((3, 2))],
    )
    chips = [
        [row * columns + column for row in (pair, pair + 1) for column in range(columns)]
        for pair in range(0, rows, 2)
    ]
    dots = spread(pay, ("axial", "circ"), chips)
    got = exchange_columns(sends, columns)
    dots, *got = lax.optimization_barrier((dots, *got))
    blank = jnp.zeros((1, 9 * LANES), F32)
    (pay,) = call(k_sum_spread, [(rows // 2, 1, 9 * LANES)], None, dots, blank)
    pay, *sends = lax.optimization_barrier((pay, *sends))
    dots = spread(pay, "axial", along)
    got = got + exchange_rows(sends, rows)
    x, r = call(
        k_final, [(rhs, points)] * 2,
        place, dots, q2, *got, order, r0, z0f, z1f, z2f, w0f, w1f,
        raw=(10, 11, 12),
        raw_outs=(0, 1),
        scratch=[
            pltpu.VMEM((3, rhs, points), F32),
            pltpu.VMEM((2, rhs, points), F32),
            dma((3, 2)),
            dma((2, 2)),
        ],
    )
    return (x[None, None], r[None, None])


def solution(mesh):
    in_specs = (
        P("axial", "circ", None, None),
        P("axial", "circ", None),
        P("axial", "circ", None),
        P("axial", "circ", None, None),
        P("axial", "circ", None, None, None),
        P("axial", "circ", None, None),
        P("axial", None, None),
        P("axial", None),
        P("axial", None),
        P("axial", "circ", None),
        P("axial", "circ", None, None),
    )
    out_specs = (P("axial", "circ", None, None), P("axial", "circ", None, None))
    return jax.shard_map(local, mesh=mesh, in_specs=in_specs, out_specs=out_specs, check_vma=False)
```

```python
import functools

import jax
import jax.numpy as jnp
from jax import lax
from jax.experimental import pallas as pl
from jax.experimental.pallas import tpu as pltpu
from jax.sharding import PartitionSpec as P

SHIFT = 12.0
HIGHEST = lax.Precision.HIGHEST
F32 = jnp.float32
BF16 = jnp.bfloat16
LANES = 128
PIECES = 2


def mm_t(a, b):
    return lax.dot_general(
        a, b, (((1,), (1,)), ((), ())), precision=HIGHEST, preferred_element_type=F32
    )


def cut(value, count):
    pieces = []
    for _ in range(count):
        piece = value.astype(BF16)
        pieces.append(piece)
        value = value - piece.astype(F32)
    return pieces


def narrow(a, b, transposed=False):
    return lax.dot_general(
        a, b, (((1,), (1 if transposed else 0,)), ((), ())), preferred_element_type=F32
    )


def product(a, pieces, transposed=False):
    count = a.shape[0]
    levels = len(pieces)
    if count % 16:
        a = jnp.concatenate([a, jnp.zeros((16 - count % 16, a.shape[1]), F32)], axis=0)
    tall = a.shape[0]
    left = cut(a, levels)
    by_level = [None] * levels
    for n, piece in enumerate(pieces):
        used = left[: levels - n]
        stack = used[0] if len(used) == 1 else jnp.concatenate(used, axis=0)
        out = narrow(stack, piece, transposed)
        for m in range(len(used)):
            part = out[m * tall : (m + 1) * tall]
            level = n + m
            by_level[level] = part if by_level[level] is None else by_level[level] + part
    total = by_level[-1]
    for part in by_level[-2::-1]:
        total = total + part
    return total[:count]


def select_columns(a, hot, transposed):
    count = a.shape[0]
    if count % 16:
        a = jnp.concatenate([a, jnp.zeros((16 - count % 16, a.shape[1]), F32)], axis=0)
    tall = a.shape[0]
    out = narrow(jnp.concatenate(cut(a, 3), axis=0), hot, transposed)
    return ((out[2 * tall :] + out[tall : 2 * tall]) + out[:tall])[:count]


def faces_of(full):
    return [full[:, f * LANES : (f + 1) * LANES] for f in range(4)]


def one_hot_faces(order):
    rows = lax.broadcasted_iota(jnp.int32, (LANES, LANES), 0)
    return [
        jnp.where(order[:, f * LANES : (f + 1) * LANES] - f * LANES == rows, 1.0, 0.0)
        .astype(F32)
        .astype(BF16)
        for f in range(4)
    ]


def to_shared(full, hots):
    return jnp.concatenate(
        [select_columns(part, hot, True) for part, hot in zip(faces_of(full), hots)], axis=1
    )


def to_points(full, hots):
    return jnp.concatenate(
        [select_columns(part, hot, False) for part, hot in zip(faces_of(full), hots)], axis=1
    )


class Place:
    def __init__(self, place):
        row, rows, column = place[0], place[1], place[2]
        self.row = row
        self.even_row = lax.rem(row, 2) == 0
        self.even_column = lax.rem(column, 2) == 0
        self.keep_south = jnp.where(row > 0, 1.0, 0.0).astype(F32)
        self.keep_north = jnp.where(row < rows - 1, 1.0, 0.0).astype(F32)


def put_sends(sends, full, at):
    south, north, west, east = faces_of(full)
    sends[0][...] = jnp.where(at.even_column, west, east)
    sends[1][...] = jnp.where(at.even_column, east, west)
    sends[2][...] = jnp.where(at.even_row, south, north)
    sends[3][...] = jnp.where(at.even_row, north, south)


def neighbours(got, at):
    far, near, link, core = [ref[...] for ref in got]
    above = jnp.where(at.even_row, core, link)
    below = jnp.where(at.even_row, link, core)
    right = jnp.where(at.even_column, near, far)
    left = jnp.where(at.even_column, far, near)
    return below, above, left, right


def assembled(full, got, at, rhs, keep=True):
    count = full.shape[0]
    extra = count - rhs
    own = faces_of(full)
    other = neighbours(got, at)
    scale = (at.keep_south, at.keep_north, None, None)
    shift = (0, 16, 8, 8)
    out = []
    for f in range(4):
        part = own[f][:rhs] + other[f][:rhs]
        if extra:
            zero = jnp.zeros((8, LANES), F32)
            mine = jnp.concatenate([zero, own[f][rhs:], zero], axis=0)
            pieces = [jnp.zeros((shift[f], LANES), F32)] if shift[f] else []
            pieces.append(other[f][rhs:])
            if shift[f] < 16:
                pieces.append(jnp.zeros((16 - shift[f], LANES), F32))
            part = jnp.concatenate([part, mine + jnp.concatenate(pieces, axis=0)], axis=0)
        if keep and scale[f] is not None:
            part = part * scale[f]
        out.append(part)
    return jnp.concatenate(out, axis=1)


def held(ref):
    return [ref[n] for n in range(ref.shape[0])]


def averages(avg, value):
    pick = jnp.concatenate([avg, jnp.zeros_like(avg)], axis=0).astype(BF16)
    high, middle, low = [narrow(pick, piece, True) for piece in cut(value, 3)]
    return ((low + middle) + high)[: avg.shape[0]]


def schur(z, diag, couple, blocks):
    inner = product(z, couple)
    solved = jnp.concatenate(
        [
            product(part, [piece[n] for piece in blocks])
            for n, part in enumerate(faces_of(inner))
        ],
        axis=1,
    )
    return diag * z - product(solved, couple, True)


def begin(source, target, sems, parts):
    rows = source.shape[0] // 8
    edges = [8 * (rows * n // parts) for n in range(parts)] + [source.shape[0]]
    copies = []
    for n in range(parts):
        band = pl.ds(edges[n], edges[n + 1] - edges[n])
        copies.append(pltpu.make_async_copy(source.at[band], target.at[band], sems.at[n]))
        copies[n].start()
    return copies


def finish(copies):
    for copy in copies:
        copy.wait()


def k_prepare(
    place, load, rho, order, neumann, shared_o, order_o, s0, s1, s2, s3, neumann_o, load_s, rho_s, sem, far_sem
):
    at = Place(place)
    copies = [
        pltpu.make_async_copy(source, target, sem.at[n])
        for n, (source, target) in enumerate(((order, order_o), (load, load_s), (rho, rho_s)))
    ]
    for copy in copies:
        copy.start()
    ahead = begin(neumann, neumann_o, far_sem, 4)
    copies[0].wait()
    hots = one_hot_faces(order_o[...])
    copies[1].wait()
    copies[2].wait()
    pad = jnp.zeros((7, rho_s.shape[1]), F32)
    full = to_shared(jnp.concatenate([load_s[...], rho_s[...], pad], axis=0), hots)
    shared_o[...] = full
    put_sends((s0, s1, s2, s3), full, at)
    finish(ahead)


def k_neumann(order, neumann_s, lists, couple, neumann_o, avg_o, couple_o, lists_s, sem):
    listed = pltpu.make_async_copy(lists, lists_s, sem.at[4])
    listed.start()
    ahead = begin(couple, couple_o, sem, 4)
    hots = one_hot_faces(order[...])
    points = order.shape[1]
    listed.wait()
    named = lists_s[...]
    position = lax.broadcasted_iota(jnp.int32, (8, points), 1)
    total = jnp.zeros((8, points), F32)
    length = named.shape[1]
    for item in range(length):
        total = total + jnp.where(named[:, item : item + 1] == position, 1.0, 0.0)
    avg_o[...] = to_shared(total * (1.0 / length), hots)
    tall = jnp.concatenate(cut(neumann_s[...], PIECES), axis=0)
    half = jnp.concatenate(
        [narrow(part, hot, True).astype(BF16) for part, hot in zip(faces_of(tall), hots)], axis=1
    )
    for n in range(PIECES):
        for f in range(4):
            first = n * points + f * LANES
            neumann_o[n, f * LANES : (f + 1) * LANES, :] = narrow(
                hots[f], half[first : first + LANES]
            ).astype(BF16)
    finish(ahead)


def k_couple(
    order, after, couple_s, diag, blocks, row_coarse, lower, upper,
    diag_o, couple_o, blocks_o, coefs_o,
    diag_s, blocks_s, rows_s, lower_s, upper_s, sem,
):
    copies = [None] * 4
    copies.append(pltpu.make_async_copy(blocks, blocks_s, sem.at[4]))
    copies.append(pltpu.make_async_copy(diag, diag_s, sem.at[5]))
    copies.append(pltpu.make_async_copy(row_coarse, rows_s, sem.at[6]))
    copies.append(pltpu.make_async_copy(lower, lower_s, sem.at[7]))
    copies.append(pltpu.make_async_copy(upper, upper_s, sem.at[8]))
    for copy in copies[4:]:
        copy.start()
    hots = one_hot_faces(order[...])
    copies[5].wait()
    diag_o[...] = to_shared(jnp.broadcast_to(diag_s[...], (8, diag_s.shape[1])), hots)[:1]
    for f in range(4):
        rows = slice(f * LANES, (f + 1) * LANES)
        for n, piece in enumerate(cut(couple_s[rows, :], PIECES)):
            couple_o[n, rows, :] = narrow(hots[f], piece).astype(BF16)
    copies[4].wait()
    for f in range(4):
        for n, piece in enumerate(cut(blocks_s[f], PIECES)):
            blocks_o[n, f] = piece
    for n in (6, 7, 8):
        copies[n].wait()
    count = lower_s.shape[1]
    lane = lax.broadcasted_iota(jnp.int32, (count, LANES), 1)
    eye = lax.broadcasted_iota(jnp.int32, (count, count), 0) == lax.broadcasted_iota(
        jnp.int32, (count, count), 1
    )
    tile = jnp.zeros((count, LANES), F32)
    for n in range(count):
        tile = tile + jnp.where(lane == 112 + n, rows_s[:, n : n + 1], 0.0)
    for n, ref in ((120, lower_s), (121, upper_s)):
        column = jnp.sum(
            jnp.where(eye, jnp.broadcast_to(ref[...], (count, count)), 0.0), axis=1, keepdims=True
        )
        tile = tile + jnp.where(lane == n, column, 0.0)
    coefs_o[0:24, :] = jnp.zeros((24, LANES), F32)
    coefs_o[24:32, :] = tile


def k_first(place, shared, g0, g1, g2, g3, neumann, avg, r_o, share_o, prim_o, t_o, *sends):
    at = Place(place)
    rhs = r_o.shape[0]
    full = assembled(shared[...], (g0, g1, g2, g3), at, shared.shape[0], keep=False)
    share = shared[rhs : rhs + 1, :] / full[rhs : rhs + 1]
    south, north, west, east = faces_of(full[:rhs])
    r = jnp.concatenate([south * at.keep_south, north * at.keep_north, west, east], axis=1)
    r_o[...] = r
    share_o[...] = share
    weighted = share * r
    prim_o[...] = averages(avg[...], weighted)
    t = jnp.concatenate([share * product(weighted, held(neumann)), share * avg[...]], axis=0)
    t_o[...] = t
    put_sends(sends, t, at)


def k_schur(
    place, t, g0, g1, g2, g3, diag, couple, blocks, z_o, q_o, s0, s1, s2, s3, z_s, sem, *, rhs
):
    at = Place(place)
    z = assembled(t[...], (g0, g1, g2, g3), at, rhs)
    z_s[...] = z
    copy = pltpu.make_async_copy(z_s, z_o, sem.at[0])
    copy.start()
    q = schur(z, diag[...], held(couple), held(blocks))
    q_o[...] = q
    put_sends((s0, s1, s2, s3), q, at)
    copy.wait()


def k_second(place, q, g2, g3, g0, g1, r, share, neumann, avg, v_o, t_o, pr_o, *sends):
    at = Place(place)
    rhs = r.shape[0]
    w = assembled(q[...], (g0, g1, g2, g3), at, rhs)
    v = jnp.concatenate([w[:rhs] - SHIFT * r[...], w[rhs:]], axis=0)
    v_o[...] = v
    weighted = share[...] * v
    pr_o[...] = jnp.concatenate(
        [averages(avg[...], weighted[:rhs]), averages(avg[...], weighted[rhs:])], axis=1
    )
    t = share[...] * product(weighted, held(neumann))
    t_o[...] = t
    put_sends(sends, t, at)


def k_third(place, q, g0, g1, g2, g3, v, share, avg, prim0, prim1, v2_o, pay_o, v2_s, sem):
    at = Place(place)
    rhs = prim0.shape[1]
    w = assembled(q[...], (g0, g1, g2, g3), at, rhs)
    fields = w[:rhs] - SHIFT * v[:rhs, :]
    v2_s[0:rhs, :] = fields
    copies = begin(v2_s.at[0:rhs], v2_o.at[0:rhs], sem.at[0], 2)
    prim2 = averages(avg[...], share[...] * fields)
    zero = jnp.zeros((16, w.shape[1]), F32)
    basis = w[rhs:] - SHIFT * jnp.concatenate([zero, v[rhs:, :], zero], axis=0)
    v2_s[rhs:, :] = basis
    copies += begin(v2_s.at[rhs:], v2_o.at[rhs:], sem.at[1], 2)
    reach2 = averages(avg[...], share[...] * basis)
    reach1 = prim1[...][:, rhs:]
    spare = jnp.zeros((8, LANES - reach1.shape[1] - reach2.shape[1]), F32)
    tail = jnp.concatenate([reach1, reach2, spare], axis=1)
    pay = jnp.concatenate([prim0[...], prim1[...][:, :rhs], prim2, tail], axis=0)
    for item in range(pay_o.shape[0]):
        pay_o[item] = pay
    finish(copies)


def summed(got):
    total = got[0]
    for item in range(1, got.shape[0]):
        total = total + got[item]
    return total


def k_sum_spread(got, coefs, out):
    total = summed(got) + coefs[...]
    for item in range(out.shape[0]):
        out[item] = total


def banded_product(pieces, value):
    first, second = cut(value, 2)
    return (narrow(pieces[1], first) + narrow(pieces[0], second)) + narrow(pieces[0], first)


def coarse_rows(totals, lowers, uppers):
    carry = jnp.zeros_like(totals[0])
    smooth = []
    for low, value in zip(lowers, [(1.0 - low) * value for low, value in zip(lowers, totals)]):
        carry = low * carry + value
        smooth.append(carry)
    carry = jnp.zeros_like(totals[0])
    tops = []
    smooth = [(1.0 - up) * value for up, value in zip(uppers, smooth)]
    for up, value in zip(uppers[::-1], smooth[::-1]):
        carry = up * carry + value
        tops.append(carry)
    return tops[::-1]


def k_fourth(place, v2, share, neumann, t_o, s0, s1, s2, s3, v2_s, t_s, sem):
    at = Place(place)
    half = v2_s.shape[0] // 16 * 8
    bands = (slice(0, half), slice(half, v2_s.shape[0]))
    loads = [begin(v2.at[band], v2_s.at[band], sem.at[n], 2) for n, band in enumerate(bands)]
    copies, done = [], []
    for n, band in enumerate(bands):
        finish(loads[n])
        part = share[...] * product(share[...] * v2_s[band, :], held(neumann))
        t_s[band, :] = part
        copies += begin(t_s.at[band], t_o.at[band], sem.at[2 + n], 2)
        done.append(part)
    put_sends((s0, s1, s2, s3), jnp.concatenate(done, axis=0), at)
    finish(copies)


def lift(coefs, basis):
    spare = -coefs.shape[0] % 16
    if spare:
        coefs = jnp.concatenate([coefs, jnp.zeros((spare, coefs.shape[1]), F32)], axis=0)
        basis = jnp.concatenate([basis, jnp.zeros((spare, basis.shape[1]), F32)], axis=0)
    c, b = cut(coefs, 2), cut(basis, 2)

    def times(x, y):
        return lax.dot_general(x, y, (((0,), (0,)), ((), ())), preferred_element_type=F32)

    return (times(c[1], b[0]) + times(c[0], b[1])) + times(c[0], b[0])


def k_core(
    place, mine, other, t, g0, g1, g2, g3, z0, v1, z1, v2, r, diag, couple, blocks,
    z0_o, z1_o, z2_o, w0_o, w1_o, q_o, pay_o, s0, s1, s2, s3,
    band0, band1, band2, c0_s, c1_s, c2_s, full_s, t_s, z1_s, v2_s, sem, in_sem,
):
    at = Place(place)
    loads = []
    for n, (source, target) in enumerate(((z1, z1_s), (v2, v2_s), (t, t_s))):
        loads += begin(source, target, in_sem.at[n], 2)
    t, z1, v2 = t_s, z1_s, v2_s
    rhs = r.shape[0]
    rows = 2 * mine.shape[0]
    width = band0.shape[1]
    lane = lax.broadcasted_iota(jnp.int32, (8, width), 1)
    lowers, uppers = [], []
    for ref in (band0, band1, band2):
        if ref.shape[0] > rows * 8:
            ref[rows * 8 :, :] = jnp.zeros((ref.shape[0] - rows * 8, width), F32)
    pays = []
    for k in range(rows // 2):
        pays.append(jnp.where(at.even_row, mine[k], other[k]))
        pays.append(jnp.where(at.even_row, other[k], mine[k]))
    for k in range(rows):
        tail = pays[k][24:32]
        lowers.append(jnp.broadcast_to(tail[:, 120:121], (8, rhs)))
        uppers.append(jnp.broadcast_to(tail[:, 121:122], (8, rhs)))
        wide = tail
        if width > LANES:
            wide = jnp.concatenate([tail, jnp.zeros((8, width - LANES), F32)], axis=1)
        for ref, first, last, to in (
            (band1, 0, 40, 8 * (k - 2)),
            (band2, 40, 112, 8 * (k - 4)),
            (band0, 112, 120, 8 * k),
        ):
            picked = jnp.where((lane >= first) & (lane < last), wide, 0.0)
            ref[8 * k : 8 * k + 8, :] = pltpu.roll(picked, (to - first) % width, 1)

    def stacked(tiles):
        if width > rows * 8:
            tiles = tiles + [jnp.zeros((width - rows * 8, rhs), F32)]
        return jnp.concatenate(tiles, axis=0)

    own, near, wide = [cut(ref[...], 2) for ref in (band0, band1, band2)]

    def solve(total):
        tiles = [total[8 * k : 8 * k + 8] for k in range(rows)]
        return stacked(coarse_rows(tiles, lowers, uppers)) + banded_product(own, total)

    edge = jnp.zeros((40, rhs), F32)
    c0 = solve(stacked([part[0:8] for part in pays]))
    c1 = solve(stacked([part[8:16] for part in pays]) + banded_product(near, c0))
    c2 = solve(
        stacked([part[16:24] for part in pays])
        + banded_product(wide, c0)
        + banded_product(near, c1)
    )
    for ref, value in ((c0_s, c0), (c1_s, c1), (c2_s, c2)):
        ref[0:40, :] = edge
        ref[40 : 40 + width, :] = value
        ref[40 + width :, :] = edge
    start = at.row * 8
    c0 = c0_s[pl.ds(pl.multiple_of(start, 8), 88), :]
    c1 = c1_s[pl.ds(pl.multiple_of(start + 16, 8), 56), :]
    c2 = c2_s[pl.ds(pl.multiple_of(start + 32, 8), 24), :]
    r0 = r[...]
    z0f = z0[:rhs, :] + lift(c0[32:56], z0[rhs:, :])
    v1f = v1[:rhs, :] + lift(c0[24:64], v1[rhs:, :])
    finish(loads[0:2])
    z1f = z1[:rhs, :] + lift(
        jnp.concatenate([c0[16:72], c1[16:40]], axis=0),
        jnp.concatenate([z1[rhs:, :], z0[rhs:, :]], axis=0),
    )
    finish(loads[2:4])
    v2f = v2[:rhs, :] + lift(
        jnp.concatenate([c0[8:80], c1[8:48]], axis=0),
        jnp.concatenate([v2[rhs:, :], v1[rhs:, :]], axis=0),
    )
    copies = []

    def keep(n, value, out):
        full_s[n] = value
        copies.extend(begin(full_s.at[n], out, sem.at[n], 2))

    keep(0, z0f, z0_o)
    keep(1, z1f, z1_o)
    keep(2, v1f + SHIFT * r0, w0_o)
    keep(3, v2f + SHIFT * v1f, w1_o)
    finish(loads[4:6])
    z2 = assembled(t[...], (g0, g1, g2, g3), at, rhs)
    z2f = z2[:rhs] + lift(
        jnp.concatenate([c0, c1, c2], axis=0),
        jnp.concatenate([z2[rhs:], z1[rhs:, :], z0[rhs:, :]], axis=0),
    )
    keep(4, z2f, z2_o)
    q = schur(z2f, diag[...], held(couple), held(blocks))
    q_o[...] = q
    put_sends((s0, s1, s2, s3), q, at)
    table = dot_rows(
        [(r0, z0f), (r0, z1f), (v1f, z0f), (v1f, z1f), (v2f, z1f)]
        + [(r0, z2f), (v1f, z2f), (v2f, z2f), (z2f, q + q)]
    )
    line = jnp.concatenate([table[i : i + 1] for i in range(9)], axis=1)
    for item in range(pay_o.shape[0]):
        pay_o[item] = line
    finish(copies)


def dot_rows(pairs):
    parts = []
    for a, b in pairs:
        faces = faces_of(a * b)
        parts.append((faces[0] + faces[1]) + (faces[2] + faces[3]))
    wide = jnp.concatenate(parts, axis=1)
    shape = (16, wide.shape[1])
    pick = jnp.where(
        lax.broadcasted_iota(jnp.int32, shape, 0) == lax.broadcasted_iota(jnp.int32, shape, 1) // LANES,
        1.0,
        0.0,
    ).astype(BF16)
    high, middle, low = [narrow(pick, piece, True) for piece in cut(wide, 3)]
    return (low + middle) + high


def k_final(
    place, got, q, g0, g1, g2, g3, order, r0, z0, z1, z2, w0, w1, x_o, r_o, full_s, both_s, sem, out_sem
):
    loads = []
    for n, source in enumerate((z2, w0, w1)):
        loads += begin(source, full_s.at[n], sem.at[n], 2)
    w2 = assembled(q[...], (g0, g1, g2, g3), Place(place), q.shape[0])
    total = summed(got)
    v0z0, v0z1, v1z0, v1z1, v2z1, v0z2, v1z2, v2z2, z2w2 = [
        total[:, i * LANES : (i + 1) * LANES] for i in range(9)
    ]
    z1w0 = v1z1 + SHIFT * v0z1
    z2w0 = v1z2 + SHIFT * v0z2
    z2w1 = v2z2 + SHIFT * v1z2
    zw = [
        [v1z0 + SHIFT * v0z0, z1w0, z2w0],
        [z1w0, v2z1 + SHIFT * v1z1, z2w1],
        [z2w0, z2w1, z2w2],
    ]
    vz = [[v0z0, v0z1, v0z2], [v1z0, v1z1, v1z2], [z1w0 - SHIFT * v1z0, v2z1, v2z2]]

    def form(left, table, right):
        value = None
        for i, a in enumerate(left):
            for j, b in enumerate(right):
                if a is None or b is None:
                    continue
                term = a * table[i][j] * b
                value = term if value is None else value + term
        return value

    one = jnp.ones_like(vz[0][0])
    zero = jnp.zeros_like(one)
    toward = [one, None, None]
    steps = [zero, zero, zero]
    drops = [zero, zero, zero]
    rz = vz[0][0]
    for iteration in range(3):
        alpha = rz / form(toward, zw, toward)
        for j in range(3):
            if toward[j] is not None:
                steps[j] = steps[j] + alpha * toward[j]
                drops[j] = drops[j] - alpha * toward[j]
        if iteration < 2:
            mix = [one + SHIFT * drops[0], drops[0] + SHIFT * drops[1], None]
            if iteration == 1:
                mix[2] = drops[1]
            new = form(mix, vz, mix)
            beta = new / rz
            toward = [
                m if d is None else (beta * d if m is None else m + beta * d)
                for m, d in zip(mix, toward)
            ]
            rz = new
    table = jnp.concatenate(steps + drops + [zero, zero], axis=0)
    eye = jnp.where(
        lax.broadcasted_iota(jnp.int32, (LANES, LANES), 0)
        == lax.broadcasted_iota(jnp.int32, (LANES, LANES), 1),
        1.0,
        0.0,
    ).astype(F32)
    columns = mm_t(eye, table)
    col = [columns[:, i : i + 1] for i in range(6)]
    hots = one_hot_faces(order[...])
    finish(loads)
    x = col[0] * z0[...] + col[1] * z1[...] + col[2] * full_s[0]
    both_s[0] = to_points(x, hots)
    copies = begin(both_s.at[0], x_o, out_sem.at[0], 2)
    r = r0[...] + col[3] * full_s[1] + col[4] * full_s[2] + col[5] * w2
    both_s[1] = to_points(r, hots)
    copies += begin(both_s.at[1], r_o, out_sem.at[1], 2)
    finish(copies)


def call(body, outs, place, *args, scratch=(), raw=(), raw_outs=(), flops=1_000_000):
    args = tuple(
        pltpu.with_memory_space_constraint(arg, pltpu.HBM) if n in raw else arg
        for n, arg in enumerate(args)
    )
    space = [pltpu.HBM if n in raw else pltpu.VMEM for n in range(len(args))]
    specs = [pl.BlockSpec(memory_space=kind) for kind in space]
    if place is not None:
        specs = [pl.BlockSpec(memory_space=pltpu.SMEM)] + specs
        args = (place,) + args
    return pl.pallas_call(
        body,
        out_shape=[
            out
            if isinstance(out, jax.ShapeDtypeStruct)
            else (pltpu.HBM(out, F32) if n in raw_outs else jax.ShapeDtypeStruct(out, F32))
            for n, out in enumerate(outs)
        ],
        in_specs=specs,
        out_specs=[
            pl.BlockSpec(memory_space=pltpu.HBM if n in raw_outs else pltpu.VMEM)
            for n in range(len(outs))
        ],
        scratch_shapes=list(scratch),
        compiler_params=pltpu.CompilerParams(vmem_limit_bytes=16 * 1024 * 1024),
        cost_estimate=pl.CostEstimate(flops=flops, bytes_accessed=1_000_000, transcendentals=0),
    )(*args)


def exchange_far(sends, columns):
    far = [(i, (i + 1 if i % 2 else i - 1) % columns) for i in range(columns)]
    return [lax.ppermute(sends[0], "circ", far)]


def exchange_near(sends, columns):
    return [lax.ppermute(sends[1], "circ", [(i, i ^ 1) for i in range(columns)])]


def exchange_rows(sends, rows):
    core = [(i, i ^ 1) for i in range(rows)]
    link = [(i, i + 1 if i % 2 else i - 1) for i in range(1, rows - 1)]
    return [lax.ppermute(sends[2], "axial", link), lax.ppermute(sends[3], "axial", core)]


def exchange(sends, rows, columns):
    return exchange_far(sends, columns) + exchange_near(sends, columns) + exchange_rows(sends, rows)


def spread(value, axis, groups=None):
    return lax.all_to_all(
        value, axis, split_axis=0, concat_axis=0, tiled=True, axis_index_groups=groups
    )


def local(
    load_terms, diffusivity, interface_diag, coupling, interior_inverse, neumann_solve,
    row_coarse, lower_coef, upper_coef, face_order, primal_lists,
):
    rows, columns = lax.axis_size("axial"), lax.axis_size("circ")
    rhs, points = load_terms.shape[2], load_terms.shape[3]
    place = jnp.stack(
        [lax.axis_index("axial"), jnp.int32(rows), lax.axis_index("circ")]
    ).astype(jnp.int32)
    swap = functools.partial(exchange, rows=rows, columns=columns)
    dma = pltpu.SemaphoreType.DMA

    def face(n):
        return [(n, LANES)] * 4

    def bf16(*shape):
        return jax.ShapeDtypeStruct((PIECES,) + shape, BF16)

    shared, order, *sends, neumann = call(
        k_prepare,
        [(rhs + 8, points), jax.ShapeDtypeStruct((1, points), jnp.int32)]
        + face(rhs + 8)
        + [(points, points)],
        place, load_terms[0, 0], diffusivity[0], face_order[0], neumann_solve[0, 0],
        raw=(0, 1, 2, 3),
        scratch=[
            pltpu.VMEM((rhs, points), F32),
            pltpu.VMEM((1, points), F32),
            dma((3,)),
            dma((4,)),
        ],
    )
    got = swap(sends)
    neumann, avg, couple = call(
        k_neumann,
        [bf16(points, points), (8, points), (points, points)],
        None, order, neumann, primal_lists[0, 0], coupling[0, 0],
        raw=(2, 3),
        scratch=[
            pltpu.VMEM(primal_lists.shape[2:], jnp.int32),
            dma((5,)),
        ],
        flops=2_000_000_000,
    )
    r0, share, prim0, t0, *sends = call(
        k_first,
        [(rhs, points), (1, points), (8, rhs), (rhs + 8, points)] + face(rhs + 8),
        place, shared, *got, neumann, avg,
    )
    got = swap(sends)
    inner = interior_inverse.shape[2:]
    diag, couple, blocks, coefs = call(
        k_couple,
        [(1, points), bf16(points, points), bf16(*inner), (32, LANES)],
        None, order, share, couple, interface_diag[0], interior_inverse[0, 0],
        row_coarse[0], lower_coef, upper_coef,
        raw=(3, 4, 5, 6, 7),
        scratch=[
            pltpu.VMEM((1, points), F32),
            pltpu.VMEM(inner, F32),
            pltpu.VMEM(row_coarse.shape[1:], F32),
            pltpu.VMEM(lower_coef.shape, F32),
            pltpu.VMEM(upper_coef.shape, F32),
            dma((9,)),
        ],
        flops=2_000_000_000,
    )
    n = rhs + 24
    z0, q0, *sends = call(
        functools.partial(k_schur, rhs=rhs), [(n, points)] * 2 + face(n),
        place, t0, *got, diag, couple, blocks,
        raw_outs=(0,), scratch=[pltpu.VMEM((n, points), F32), dma((1,))],
    )
    got = swap(sends)
    n = rhs + 40
    v1, t1, prim1, *sends = call(
        k_second, [(n, points)] * 2 + [(8, n)] + face(n), place, q0, *got[2:], *got[:2], r0, share, neumann, avg
    )
    got = swap(sends)
    n = rhs + 56
    z1, q1, *sends = call(
        functools.partial(k_schur, rhs=rhs), [(n, points)] * 2 + face(n),
        place, t1, *got, diag, couple, blocks,
        raw_outs=(0,), scratch=[pltpu.VMEM((n, points), F32), dma((1,))],
    )
    got = swap(sends)
    n = rhs + 72
    v2, pay = call(
        k_third, [(n, points), (columns, 32, LANES)], place, q1, *got, v1, share, avg, prim0, prim1,
        raw_outs=(0,), scratch=[pltpu.VMEM((n, points), F32), dma((2, 2))],
    )
    got = spread(pay, "circ")
    t2, *sends = call(
        k_fourth, [(n, points)] + face(n), place, v2, share, neumann,
        raw=(0,), raw_outs=(0,),
        scratch=[pltpu.VMEM((n, points), F32)] * 2 + [dma((4, 2))],
        flops=500_000_000,
    )
    got, t2 = lax.optimization_barrier((got, t2))
    (pay,) = call(k_sum_spread, [(rows // 2, 32, LANES)], None, got, coefs)
    pay, *sends = lax.optimization_barrier((pay, *sends))
    along = [list(range(core, rows, 2)) for core in range(2)]
    mine = spread(pay, "axial", along)
    mine, *got = lax.optimization_barrier((mine, *swap(sends)))
    other = lax.ppermute(mine, "axial", [(i, i ^ 1) for i in range(rows)])
    width = max(LANES, 8 * rows)
    z0f, z1f, z2f, w0f, w1f, q2, pay, *sends = call(
        k_core,
        [(rhs, points)] * 6 + [(2 * columns, 1, 9 * LANES)] + face(rhs),
        place, mine, other, t2, *got, z0, v1, z1, v2, r0, diag, couple, blocks,
        raw=(2, 9, 10),
        raw_outs=(0, 1, 2, 3, 4),
        scratch=[pltpu.VMEM((width, width), F32)] * 3
        + [pltpu.VMEM((width + 80, rhs), F32)] * 3
        + [pltpu.VMEM((5, rhs, points), F32)]
        + [pltpu.VMEM((rhs + m, points), F32) for m in (72, 56, 72)]
        + [dma((5, 2)), dma((3, 2))],
    )
    chips = [
        [row * columns + column for row in (pair, pair + 1) for column in range(columns)]
        for pair in range(0, rows, 2)
    ]
    dots = spread(pay, ("axial", "circ"), chips)
    got = exchange_far(sends, columns)
    dots, *got = lax.optimization_barrier((dots, *got))
    blank = jnp.zeros((1, 9 * LANES), F32)
    (pay,) = call(k_sum_spread, [(rows // 2, 1, 9 * LANES)], None, dots, blank)
    pay, *sends = lax.optimization_barrier((pay, *sends))
    dots = spread(pay, "axial", along)
    got = got + exchange_near(sends, columns) + exchange_rows(sends, rows)
    x, r = call(
        k_final, [(rhs, points)] * 2,
        place, dots, q2, *got, order, r0, z0f, z1f, z2f, w0f, w1f,
        raw=(10, 11, 12),
        raw_outs=(0, 1),
        scratch=[
            pltpu.VMEM((3, rhs, points), F32),
            pltpu.VMEM((2, rhs, points), F32),
            dma((3, 2)),
            dma((2, 2)),
        ],
    )
    return (x[None, None], r[None, None])


def solution(mesh):
    in_specs = (
        P("axial", "circ", None, None),
        P("axial", "circ", None),
        P("axial", "circ", None),
        P("axial", "circ", None, None),
        P("axial", "circ", None, None, None),
        P("axial", "circ", None, None),
        P("axial", None, None),
        P("axial", None),
        P("axial", None),
        P("axial", "circ", None),
        P("axial", "circ", None, None),
    )
    out_specs = (P("axial", "circ", None, None), P("axial", "circ", None, None))
    return jax.shard_map(local, mesh=mesh, in_specs=in_specs, out_specs=out_specs, check_vma=False)
```
